32 devices in a mesh: ctx: 8 (over y, x, core), wa: 4 (over z).
Axes of the slice: x: 2, y: 2, z: 4, core: 2. Of those that a mesh axis runs over, the one named last changes fastest.
Arguments:
- tokens: bfloat16 [4, 1024, 2048], P('wa', 'ctx'), may hold values from -6 to 6
- lengths: int32 [4, 2], P('wa'), may hold values from 384 to 640, as said below
- dealing: int32 [4, 8], P('wa'), may hold values from 0 to 7, each once within a row
- norm1_gain: float32 [2048], replicated, may hold values from 0.1 to 1.9
- w_qkv: bfloat16 [2048, 6144], P('wa'), may hold values from -0.125 to 0.125
- w_out: bfloat16 [2048, 2048], P('wa'), may hold values from -2 to 2
- norm2_gain: float32 [2048], replicated, may hold values from 0.1 to 1.9
- w_gate_up: bfloat16 [2048, 11008], P('wa'), may hold values from -0.125 to 0.125
- w_down: bfloat16 [5504, 2048], P('wa'), may hold values from -0.078125 to 0.078125
- grad_out: bfloat16 [4, 1024, 2048], P('wa', 'ctx'), may hold values from -6 to 6
Outputs:
- out: bfloat16 [4, 1024, 2048], P('wa', 'ctx')
- d_tokens: bfloat16 [4, 1024, 2048], P('wa', 'ctx')
- d_norm1_gain: float32 [2048], replicated
- d_w_qkv: float32 [2048, 6144], P('wa')
- d_w_out: float32 [2048, 2048], P('wa')
- d_norm2_gain: float32 [2048], replicated
- d_w_gate_up: float32 [2048, 11008], P('wa')
- d_w_down: float32 [5504, 2048], P('wa')
The draws below stay inside these ranges and needn't reach their ends.
Inputs may be any that keep to these rules, and one draw needn't show every extreme that they name: Each row holds the lengths of the two sequences of that group, first sequence first; they sum to 1024; some row holds a sequence of exactly 384 tokens. `dealing`: each row is a permutation of the block numbers of the group.
All inputs are finite; a program needn't handle non-finite values.
Results may differ from the reference program's by a relative error of at most 0.019.
Values may be sent and summed in bfloat16 or wider, within the bound.
A program may use at most 576 MiB of HBM per device.

```python
import math
import jax
import jax.numpy as jnp
from jax import lax

D = 2048
HEADS = 16
HEAD = 128
FF = 5504
WINDOW = 2048
BLOCK = 128
LEN_MIN = 384
GROUP = 1024
GROUPS = 4
NBLK = 8


def draw_lengths(key, part):
    half_group = GROUP // 2
    spread = half_group - LEN_MIN
    offsets = jax.random.randint(jax.random.fold_in(key, 11), (GROUPS,), spread // 4, spread + 1)
    offsets = offsets.at[0].set(spread)
    sides = jax.random.randint(jax.random.fold_in(key, 12), (GROUPS,), 0, 2)
    first_length = jnp.where(sides == 1, half_group - offsets, half_group + offsets)
    return jnp.stack([first_length, GROUP - first_length], axis=1).astype(jnp.int32)


def block_levels(stream_key, shape, cuts, least, top_value):
    def one(position, parts):
        steps = jax.random.uniform(jax.random.fold_in(jax.random.fold_in(stream_key, 6), position), (parts,), jnp.float32, least / len(cuts), top_value / len(cuts))
        return jnp.repeat(jnp.exp(steps), shape[position] // parts).reshape((-1,) + (1,) * (len(shape) - position - 1))

    factor_of = one(*cuts[0])
    for cut in cuts[1:]:
        factor_of = factor_of * one(*cut)
    return factor_of


def bell_draw(key, dims, scale, bound, split=(), kind=jnp.bfloat16):
    values = scale * jax.random.normal(key, dims, jnp.float32)
    if split:
        values = values * block_levels(key, dims, split, -0.22, 0.18)
    return jnp.clip(values, -bound, bound).astype(kind)


def setup_inputs(seed: int = 0) -> dict:
    arg_keys = jax.random.split(jax.random.key(seed), 11)
    return {
        "tokens": bell_draw(arg_keys[0], (GROUPS, GROUP, D), 1.0, 6.0, ((0, 4), (1, 8))),
        "lengths": draw_lengths(jax.random.fold_in(arg_keys[10], 71), 0),
        "dealing": jax.vmap(lambda own: jax.random.permutation(own, NBLK))(jax.random.split(arg_keys[2], GROUPS)).reshape((GROUPS, NBLK)).astype(jnp.int32),
        "norm1_gain": jnp.clip(1.0 + 0.18 * jax.random.normal(arg_keys[3], (D,), jnp.float32), 0.1, 1.9),
        "w_qkv": bell_draw(arg_keys[4], (D, 3 * D), D ** -0.5, 0.125, ((0, 4),)),
        "w_out": bell_draw(arg_keys[5], (D, D), 8 ** -0.5, 2.0, ((0, 4),)),
        "norm2_gain": jnp.clip(1.0 + 0.18 * jax.random.normal(arg_keys[6], (D,), jnp.float32), 0.1, 1.9),
        "w_gate_up": bell_draw(arg_keys[7], (D, 2 * FF), D ** -0.5, 0.125, ((0, 4),)),
        "w_down": bell_draw(arg_keys[8], (FF, D), FF ** -0.5, 0.078125, ((0, 4),)),
        "grad_out": bell_draw(arg_keys[9], (GROUPS, GROUP, D), 1.0, 6.0, ((0, 4), (1, 8))),
    }


@jax.custom_vjp
def low(v):
    return lax.optimization_barrier(v.astype(jnp.bfloat16)).astype(jnp.float32)

@jax.custom_vjp
def low_back(v):
    return v

def low_keep(v):
    return (low(v), None)

def low_pass(kept, grad):
    return (grad,)

def back_keep(v):
    return (v, None)

def back_low(kept, grad):
    return (low(grad),)
low.defvjp(low_keep, low_pass)
low_back.defvjp(back_keep, back_low)
EPSILON = 1e-06

def matmul(left, right):
    return jnp.dot(left, right, precision=lax.Precision.HIGHEST, preferred_element_type=jnp.float32)

def rms_scale(values):
    return lax.rsqrt(lax.optimization_barrier(jnp.mean(values * values, axis=-1, keepdims=True)) + EPSILON)

def rotary_tables(seq_pos):
    half_width = HEAD // 2
    inverse_freq = jnp.power(10000.0, -2.0 * jnp.arange(half_width, dtype=jnp.float32) / HEAD)
    angles = seq_pos.astype(jnp.float32)[:, None] * inverse_freq[None, :]
    return (jnp.cos(angles)[:, None, :], jnp.sin(angles)[:, None, :])

def rotate(values, cosine, sine):
    half_width = HEAD // 2
    first_half = values[..., :half_width]
    second_half = values[..., half_width:]
    return jnp.concatenate([first_half * cosine - second_half * sine, first_half * sine + second_half * cosine], axis=-1)

def attend(queries, keys_all, values_all, seg_ids, given_pos):
    row_total = queries.shape[0]
    block_rows = min(512, row_total)
    block_count = row_total // block_rows
    query_blocks = queries.reshape(block_count, block_rows, HEADS, HEAD)
    seg_blocks = seg_ids.reshape(block_count, block_rows)
    pos_blocks = given_pos.reshape(block_count, block_rows)

    def one_block(inputs):
        query_block, seg_block, pos_block = inputs
        scores = jnp.einsum('qhe,khe->hqk', query_block, keys_all, precision=lax.Precision.HIGHEST) / math.sqrt(HEAD)
        scores = low_back(scores)
        distance = pos_block[:, None] - given_pos[None, :]
        allowed = (seg_block[:, None] == seg_ids[None, :]) & (distance >= 0) & (distance < WINDOW)
        weights = low(jax.nn.softmax(jnp.where(allowed[None], scores, -jnp.inf), axis=-1))
        mixed = jnp.einsum('hqk,khe->qhe', weights, values_all, precision=lax.Precision.HIGHEST)
        return mixed.reshape(block_rows, HEADS * HEAD)
    return lax.map(jax.checkpoint(one_block), (query_blocks, seg_blocks, pos_blocks)).reshape(row_total, HEADS * HEAD)

def layer(given, gain_one, weight_qkv, weight_out, gain_two, weight_gate_up, weight_down, seg_ids, given_pos, cosine, sine):
    row_total = given.shape[0]
    normed_one = low(given * rms_scale(given) * gain_one)
    projected = low_back(matmul(normed_one, weight_qkv))
    queries = low(rotate(projected[:, :D].reshape(row_total, HEADS, HEAD), cosine, sine))
    keys_all = low(rotate(projected[:, D:2 * D].reshape(row_total, HEADS, HEAD), cosine, sine))
    values_all = low(projected[:, 2 * D:].reshape(row_total, HEADS, HEAD))
    attended = low(low_back(attend(queries, keys_all, values_all, seg_ids, given_pos)))
    hidden = given + low_back(matmul(attended, weight_out))
    normed_two = low(hidden * rms_scale(hidden) * gain_two)
    gate_up = low_back(matmul(normed_two, weight_gate_up))
    inner = low(jax.nn.silu(gate_up[:, :FF]) * gate_up[:, FF:])
    return hidden + low_back(matmul(inner, weight_down))

def reference(tokens, lengths, dealing, norm1_gain, w_qkv, w_out, norm2_gain, w_gate_up, w_down, grad_out):
    params = (norm1_gain.astype(jnp.float32), w_qkv.astype(jnp.float32), w_out.astype(jnp.float32), norm2_gain.astype(jnp.float32), w_gate_up.astype(jnp.float32), w_down.astype(jnp.float32))
    given_pos = jnp.arange(GROUP, dtype=jnp.int32)

    def per_group(carried, inputs):
        dealt_tokens, length_pair, block_order, cotangent = inputs
        inverse = jnp.argsort(block_order, stable=True).astype(jnp.int32)
        given = dealt_tokens.reshape(NBLK, BLOCK, D)[inverse].reshape(GROUP, D).astype(jnp.float32)
        seg_ids = (given_pos >= length_pair[0]).astype(jnp.int32)
        seq_pos = given_pos - seg_ids * length_pair[0]
        cosine, sine = rotary_tables(seq_pos)

        def forward(given_in, gain_one, weight_qkv, weight_out, gain_two, weight_gate_up, weight_down):
            return layer(given_in, gain_one, weight_qkv, weight_out, gain_two, weight_gate_up, weight_down, seg_ids, given_pos, cosine, sine)
        result, pullback = jax.vjp(forward, given, *params)
        grads = pullback(cotangent.astype(jnp.float32))
        d_dealt = grads[0].reshape(NBLK, BLOCK, D)[block_order].reshape(GROUP, D)
        carried = tuple((total + part for total, part in zip(carried, grads[1:])))
        return (carried, (result.astype(jnp.bfloat16), d_dealt.astype(jnp.bfloat16)))
    zeros = tuple((jnp.zeros_like(param) for param in params))
    sums, (outputs, d_dealt_all) = lax.scan(per_group, zeros, (tokens, lengths, dealing, grad_out))
    return (outputs, d_dealt_all, sums[0], sums[1], sums[2], sums[3], sums[4], sums[5])
```

```python
import math

import jax
import jax.numpy as jnp
from jax import lax
from jax.sharding import PartitionSpec as P

HEADS = 16
HEAD = 128
WINDOW = 2048
BLOCK = 128

EPSILON = 1e-06
BF = jnp.bfloat16
F32 = jnp.float32


def dot_plain(left, right):
    return jnp.dot(left, right, preferred_element_type=F32)


def dot_right_t(left, right):
    return lax.dot_general(left, right, (((1,), (1,)), ((), ())), preferred_element_type=F32)


def dot_left_t(left, right):
    return lax.dot_general(left, right, (((0,), (0,)), ((), ())), preferred_element_type=F32)


def rms_scale(values):
    return lax.rsqrt(jnp.mean(values * values, axis=-1, keepdims=True) + EPSILON)


def rotary_tables(seq_pos):
    half_width = HEAD // 2
    inverse_freq = jnp.power(10000.0, -2.0 * jnp.arange(half_width, dtype=F32) / HEAD)
    angles = seq_pos.astype(F32)[:, None] * inverse_freq[None, :]
    return (jnp.cos(angles)[:, None, :], jnp.sin(angles)[:, None, :])


def rotate(values, cosine, sine):
    half_width = HEAD // 2
    first = values[..., :half_width]
    second = values[..., half_width:]
    return jnp.concatenate(
        [first * cosine - second * sine, first * sine + second * cosine], axis=-1
    )


def gather_rows(values, axis):
    return lax.all_gather(values, axis, axis=0, tiled=True)


def scatter_rows(values, axis):
    return lax.psum_scatter(values, axis, scatter_dimension=0, tiled=True)


def per_device(
    tokens, lengths, dealing, norm1_gain, w_qkv, w_out, norm2_gain, w_gate_up, w_down, grad_out
):
    tok_rows, width = tokens.shape[1], tokens.shape[2]
    ctx_size = lax.axis_size("ctx")
    wa_size = lax.axis_size("wa")
    ctx_index = lax.axis_index("ctx")
    block_order = dealing[0]
    block_total = block_order.shape[0]
    group_rows = block_total * BLOCK
    own_blocks = tok_rows // BLOCK
    first_length = lengths[0, 0]
    heads_own = HEADS // ctx_size
    head_cols = heads_own * HEAD
    wa_rows = width // wa_size
    ff_total = w_gate_up.shape[1] // 2
    ff_own = w_down.shape[0]
    piece_rows = wa_rows // ctx_size

    block_ids = jnp.arange(block_total, dtype=jnp.int32)
    inverse = jnp.sum(
        jnp.where(block_order[None, :] == block_ids[:, None], block_ids[None, :], 0), axis=1
    )

    def pick_blocks(values, order):
        parts = [
            lax.dynamic_slice_in_dim(values, order[i] * BLOCK, BLOCK) for i in range(block_total)
        ]
        return jnp.concatenate(parts, axis=0)

    qkv_slice = jnp.concatenate(
        [
            lax.dynamic_slice_in_dim(w_qkv, part * width + ctx_index * head_cols, head_cols, 1)
            for part in range(3)
        ],
        axis=1,
    )
    qkv_cols = gather_rows(qkv_slice, "wa")
    out_cols = gather_rows(
        lax.dynamic_slice_in_dim(w_out, ctx_index * head_cols, head_cols, 1), "wa"
    )
    out_rows = lax.all_to_all(out_cols, "ctx", 0, 1, tiled=True)
    gu_piece = lax.dynamic_slice_in_dim(w_gate_up, ctx_index * piece_rows, piece_rows, 0)
    gu_send = jnp.stack(
        [
            jnp.concatenate(
                [
                    gu_piece[:, to * ff_own : (to + 1) * ff_own],
                    gu_piece[:, ff_total + to * ff_own : ff_total + (to + 1) * ff_own],
                ],
                axis=1,
            )
            for to in range(wa_size)
        ]
    )
    gu_mine = lax.all_to_all(gu_send, "wa", 0, 0, tiled=True)
    gu_all = lax.all_gather(gu_mine, "ctx", axis=0)
    gu_weight = jnp.transpose(gu_all, (1, 0, 2, 3)).reshape(width, 2 * ff_own)

    dealt = gather_rows(tokens[0], "ctx")
    given_b = pick_blocks(dealt, inverse)
    given = given_b.astype(F32)
    positions = jnp.arange(group_rows, dtype=jnp.int32)
    segments = (positions >= first_length).astype(jnp.int32)
    cosine, sine = rotary_tables(positions - segments * first_length)
    normed_one = given * rms_scale(given)
    act_one = (normed_one * norm1_gain).astype(BF)

    projected = dot_plain(act_one, qkv_cols)
    parts = [
        projected[:, i * head_cols : (i + 1) * head_cols].reshape(group_rows, heads_own, HEAD)
        for i in range(3)
    ]
    query_b = rotate(parts[0], cosine, sine).astype(BF)
    key_b = rotate(parts[1], cosine, sine).astype(BF)
    value_b = parts[2].astype(BF)
    score_scale = math.sqrt(HEAD)
    distance = positions[:, None] - positions[None, :]
    allowed = (segments[:, None] == segments[None, :]) & (distance >= 0) & (distance < WINDOW)
    scores = jnp.einsum("qhe,khe->hqk", query_b, key_b, preferred_element_type=F32) / score_scale
    scores = jnp.where(allowed[None], scores, -jnp.inf)
    largest = jnp.max(scores, axis=2, keepdims=True)
    weights = jnp.exp(scores - largest)
    probs = weights / jnp.sum(weights, axis=2, keepdims=True)
    probs_b = probs.astype(BF)
    mixed = jnp.einsum("hqk,khe->qhe", probs_b, value_b, preferred_element_type=F32)
    mixed_b = mixed.reshape(group_rows, head_cols).astype(BF)

    branch = scatter_rows(dot_plain(mixed_b, out_rows).astype(BF), "ctx")
    own_given = lax.dynamic_slice_in_dim(given_b, ctx_index * tok_rows, tok_rows)
    hidden = own_given.astype(F32) + branch.astype(F32)
    scale_two = rms_scale(hidden)
    normed_two = hidden * scale_two
    act_two = gather_rows((normed_two * norm2_gain).astype(BF), "wa")
    cotangent = gather_rows(grad_out[0], "wa")

    gate_up = dot_plain(act_two, gu_weight)
    gate_part = gate_up[:, :ff_own]
    up_part = gate_up[:, ff_own:]
    sigmoid_gate = jax.nn.sigmoid(gate_part)
    silu_gate = gate_part * sigmoid_gate
    inner_b = (silu_gate * up_part).astype(BF)
    result = scatter_rows(dot_plain(inner_b, w_down).astype(BF), "wa")
    out_given = (hidden + result.astype(F32)).astype(BF)

    d_inner = dot_right_t(cotangent, w_down)
    d_gate = d_inner * up_part * sigmoid_gate * (1.0 + gate_part * (1.0 - sigmoid_gate))
    d_gu_b = jnp.concatenate([d_gate, d_inner * silu_gate], axis=1).astype(BF)
    d_normed_two = scatter_rows(dot_right_t(d_gu_b, gu_weight).astype(BF), "wa").astype(F32)
    d_down = lax.psum(dot_left_t(inner_b, cotangent).astype(BF), "ctx").astype(F32)

    d_gu_share = dot_left_t(act_two, d_gu_b).astype(BF)
    d_gu_share = jnp.transpose(
        d_gu_share.reshape(wa_size, ctx_size, piece_rows, 2 * ff_own), (1, 0, 2, 3)
    ).reshape(ctx_size * wa_size, piece_rows, 2 * ff_own)
    d_gu_piece = scatter_rows(d_gu_share, "ctx")
    d_gu_back = lax.all_to_all(d_gu_piece, "wa", 0, 0, tiled=True)
    d_gu_rows = jnp.concatenate(
        [d_gu_back[i, :, :ff_own] for i in range(wa_size)]
        + [d_gu_back[i, :, ff_own:] for i in range(wa_size)],
        axis=1,
    )
    d_gate_up = gather_rows(d_gu_rows, "ctx").astype(F32)

    gain_two_part = jnp.sum(d_normed_two * normed_two, axis=0)
    scaled_two = d_normed_two * norm2_gain
    d_hidden = grad_out[0].astype(F32) + scale_two * (
        scaled_two - normed_two * jnp.mean(scaled_two * normed_two, axis=1, keepdims=True)
    )
    d_branch_b = gather_rows(d_hidden.astype(BF), "ctx")
    grad_mixed_b = dot_right_t(d_branch_b, out_rows).astype(BF)
    d_out_part = dot_left_t(mixed_b, d_branch_b).astype(BF)
    d_out_cols = lax.all_to_all(d_out_part, "ctx", 1, 0, tiled=True)
    d_out = lax.all_gather(scatter_rows(d_out_cols, "wa"), "ctx", axis=1, tiled=True).astype(F32)

    grad_heads = grad_mixed_b.reshape(group_rows, heads_own, HEAD)
    d_probs = jnp.einsum("qhe,khe->hqk", grad_heads, value_b, preferred_element_type=F32)
    row_dot = jnp.sum(probs * d_probs, axis=2, keepdims=True)
    d_scores = (probs * (d_probs - row_dot)).astype(BF)
    d_query = jnp.einsum("hqk,khe->qhe", d_scores, key_b, preferred_element_type=F32) / score_scale
    d_key = jnp.einsum("hqk,qhe->khe", d_scores, query_b, preferred_element_type=F32) / score_scale
    d_value = jnp.einsum("hqk,qhe->khe", probs_b, grad_heads, preferred_element_type=F32)
    d_qkv_b = jnp.concatenate(
        [
            rotate(d_query, cosine, -sine).reshape(group_rows, head_cols),
            rotate(d_key, cosine, -sine).reshape(group_rows, head_cols),
            d_value.reshape(group_rows, head_cols),
        ],
        axis=1,
    ).astype(BF)
    d_qkv_share = scatter_rows(dot_left_t(act_one, d_qkv_b).astype(BF), "wa")
    d_qkv_all = lax.all_gather(d_qkv_share, "ctx", axis=0)
    d_qkv = jnp.transpose(
        d_qkv_all.reshape(ctx_size, wa_rows, 3, head_cols), (1, 2, 0, 3)
    ).reshape(wa_rows, 3 * width).astype(F32)

    d_one_part = dot_right_t(d_qkv_b, qkv_cols)
    gain_one_part = jnp.sum(d_one_part * normed_one, axis=0)
    d_normed_one = scatter_rows(pick_blocks(d_one_part.astype(BF), block_order), "ctx").astype(F32)
    own = tokens[0].astype(F32)
    own_scale = rms_scale(own)
    own_normed = own * own_scale
    scaled_one = d_normed_one * norm1_gain
    own_order = lax.dynamic_slice_in_dim(block_order, ctx_index * own_blocks, own_blocks)
    d_hidden_dealt = jnp.concatenate(
        [
            lax.dynamic_slice_in_dim(d_branch_b, own_order[i] * BLOCK, BLOCK)
            for i in range(own_blocks)
        ],
        axis=0,
    ).astype(F32)
    d_tokens = d_hidden_dealt + own_scale * (
        scaled_one - own_normed * jnp.mean(scaled_one * own_normed, axis=1, keepdims=True)
    )
    gain_parts = jnp.stack([gain_one_part, gain_two_part])
    gain_sums = jnp.sum(lax.all_gather(gain_parts, ("ctx", "wa"), axis=0), axis=0)
    return (
        out_given[None],
        d_tokens.astype(BF)[None],
        gain_sums[0],
        d_qkv,
        d_out,
        gain_sums[1],
        d_gate_up,
        d_down,
    )


def solution(mesh):
    in_specs = (
        P("wa", "ctx", None),
        P("wa", None),
        P("wa", None),
        P(),
        P("wa", None),
        P("wa", None),
        P(),
        P("wa", None),
        P("wa", None),
        P("wa", "ctx", None),
    )
    out_specs = (
        P("wa", "ctx", None),
        P("wa", "ctx", None),
        P(),
        P("wa", None),
        P("wa", None),
        P(),
        P("wa", None),
        P("wa", None),
    )
    return jax.shard_map(
        per_device, mesh=mesh, in_specs=in_specs, out_specs=out_specs, check_vma=False
    )
```

```python
import functools
import math

import jax
import jax.numpy as jnp
from jax import lax
from jax.experimental import pallas as pl
from jax.experimental.pallas import tpu as pltpu
from jax.sharding import PartitionSpec as P

HEADS = 16
HEAD = 128
WINDOW = 2048
BLOCK = 128

EPSILON = 1e-06
BF = jnp.bfloat16
F32 = jnp.float32
VMEM_LIMIT = 56 * 1024 * 1024


def dot_plain(left, right):
    return jnp.dot(left, right, preferred_element_type=F32)


def dot_right_t(left, right):
    return lax.dot_general(left, right, (((1,), (1,)), ((), ())), preferred_element_type=F32)


def dot_left_t(left, right):
    return lax.dot_general(left, right, (((0,), (0,)), ((), ())), preferred_element_type=F32)


def rms_scale(values):
    return lax.rsqrt(jnp.mean(values * values, axis=-1, keepdims=True) + EPSILON)


def rotary_tables(seq_pos):
    half_width = HEAD // 2
    inverse_freq = jnp.power(10000.0, -2.0 * jnp.arange(half_width, dtype=F32) / HEAD)
    angles = seq_pos.astype(F32)[:, None] * inverse_freq[None, :]
    return (jnp.cos(angles)[:, None, :], jnp.sin(angles)[:, None, :])


def rotate(values, cosine, sine):
    half_width = HEAD // 2
    first = values[..., :half_width]
    second = values[..., half_width:]
    return jnp.concatenate(
        [first * cosine - second * sine, first * sine + second * cosine], axis=-1
    )


def gather_rows(values, axis):
    return lax.all_gather(values, axis, axis=0, tiled=True)


def shifted(values, axis, step):
    size = lax.axis_size(axis)
    return lax.ppermute(values, axis, [(i, (i + step) % size) for i in range(size)])


def crossed(values, axis, mask):
    size = lax.axis_size(axis)
    return lax.ppermute(values, axis, [(i, i ^ mask) for i in range(size)])


def direct_scatter(parts, axis):
    total = parts[0].astype(F32)
    for step in range(1, len(parts)):
        total = total + shifted(parts[step].astype(BF), axis, -step).astype(F32)
    return total


def sum_everywhere(values):
    for axis in ("ctx", "wa"):
        mask = 1
        while mask < lax.axis_size(axis):
            values = values + crossed(values, axis, mask)
            mask *= 2
    return values


def take(values, index):
    return lax.dynamic_index_in_dim(values, index, 0, keepdims=False)


def split(values, count):
    rows = values.shape[0] // count
    return [values[i * rows : (i + 1) * rows] for i in range(count)]


MESH = pl.DeviceIdType.MESH


def greet(ctx_peers, wa_peers):
    barrier = pltpu.get_barrier_semaphore()
    for peer in ctx_peers:
        pl.semaphore_signal(barrier, inc=1, device_id={"ctx": peer}, device_id_type=MESH)
    for peer in wa_peers:
        pl.semaphore_signal(barrier, inc=1, device_id={"wa": peer}, device_id_type=MESH)
    pl.semaphore_wait(barrier, len(ctx_peers) + len(wa_peers))


def send(source, target, send_sem, recv_sem, **peer):
    copy = pltpu.make_async_remote_copy(
        src_ref=source,
        dst_ref=target,
        send_sem=send_sem,
        recv_sem=recv_sem,
        device_id=peer,
        device_id_type=MESH,
    )
    copy.start()
    return copy


def places(ctx_size, wa_size):
    chips = ctx_size // 2
    ctx, wa = lax.axis_index("ctx"), lax.axis_index("wa")
    core, chip = lax.rem(ctx, 2), lax.div(ctx, 2)
    beside = chip * 2 + 1 - core
    ahead = [lax.rem(chip + m, chips) * 2 + core for m in range(chips)]
    behind = [lax.rem(chip + chips - m, chips) * 2 + core for m in range(chips)]
    up = [lax.rem(wa + s, wa_size) for s in range(wa_size)]
    down = [lax.rem(wa + wa_size - s, wa_size) for s in range(wa_size)]
    return ctx, wa, core, chip, beside, ahead, behind, up, down


def plane_gather_start(own, found, ctx, beside, ahead, sems):
    send_sem, recv_sem, side_send, side_recv = sems
    copies = [
        send(own, found.at[ctx], send_sem.at[m], recv_sem.at[m], ctx=ahead[m])
        for m in range(1, len(ahead))
    ]
    side = [send(own, found.at[ctx], side_send.at[0], side_recv.at[0], ctx=beside)]
    return copies, side


def plane_gather_finish(found, beside, behind, copies, side, sems):
    send_sem, recv_sem, side_send, side_recv = sems
    for m in range(1, len(behind)):
        copies[m - 1].wait_recv()
        block = found.at[behind[m]]
        side.append(send(block, block, side_send.at[m], side_recv.at[m], ctx=beside))
    for copy in copies:
        copy.wait_send()
    for copy in side:
        copy.wait()


def gather_kernel(ctx_size, wa_size, cuts, x_ref, w_ref, xs_ref, ws_ref, *sems):
    plane_sems, (ring_send, ring_recv, local) = sems[:4], sems[4:]
    ctx, wa, _, _, beside, ahead, behind, up, down = places(ctx_size, wa_size)
    greet([beside] + ahead[1:], [up[1], down[1]])
    rows = w_ref.shape[0] // cuts
    ring = []
    for i in range(cuts):
        part = pl.ds(i * rows, rows)
        ring.append(
            send(
                w_ref.at[part],
                ws_ref.at[wa, part],
                ring_send.at[0, i],
                ring_recv.at[0, i],
                wa=up[1],
            )
        )
    copies, side = plane_gather_start(x_ref, xs_ref, ctx, beside, ahead, plane_sems)
    own_x = pltpu.make_async_copy(x_ref, xs_ref.at[ctx], local.at[0])
    own_w = pltpu.make_async_copy(w_ref, ws_ref.at[wa], local.at[1])
    own_x.start()
    own_w.start()
    late = []
    for step in range(1, wa_size):
        for i in range(cuts):
            ring[i].wait_recv()
            late.append(ring[i])
            if step < wa_size - 1:
                block = ws_ref.at[down[step], pl.ds(i * rows, rows)]
                ring[i] = send(
                    block, block, ring_send.at[step, i], ring_recv.at[step, i], wa=up[1]
                )
        if step == 1:
            plane_gather_finish(xs_ref, beside, behind, copies, side, plane_sems)
    for copy in late:
        copy.wait_send()
    own_x.wait()
    own_w.wait()


def gather_both(x, w, ctx_size, wa_size, cuts=4):
    chips = ctx_size // 2
    anywhere = pl.BlockSpec(memory_space=pl.ANY)
    return pl.pallas_call(
        functools.partial(gather_kernel, ctx_size, wa_size, cuts),
        out_shape=(
            jax.ShapeDtypeStruct((ctx_size,) + x.shape, x.dtype),
            jax.ShapeDtypeStruct((wa_size,) + w.shape, w.dtype),
        ),
        in_specs=[anywhere] * 2,
        out_specs=[anywhere] * 2,
        scratch_shapes=[pltpu.SemaphoreType.DMA((chips,))] * 4
        + [pltpu.SemaphoreType.DMA((wa_size - 1, cuts))] * 2
        + [pltpu.SemaphoreType.DMA((2,))],
        compiler_params=pltpu.CompilerParams(collective_id=0, has_side_effects=True),
        cost_estimate=pl.CostEstimate(flops=0, bytes_accessed=200_000_000, transcendentals=0),
        name="gather_both",
    )(x, w)


def plane_scatter(part_of, ctx_size, core, chip, beside, ahead, refs):
    chips = ctx_size // 2
    side_out, side_in, chip_out, chip_in, side_send, side_recv, chip_send, chip_recv = refs
    side, out = [], []
    order = list(range(1, chips)) + [0]
    for m in order:
        there = lax.rem(chip + m, chips) * 2
        side_out[m] = part_of(there + 1 - core).astype(BF)
        side.append(
            send(side_out.at[m], side_in.at[m], side_send.at[m], side_recv.at[m], ctx=beside)
        )
    total = None
    for i, m in enumerate(order):
        there = lax.rem(chip + m, chips) * 2
        mine = part_of(there + core)
        side[i].wait_recv()
        total = mine + side_in[m].astype(F32)
        if m > 0:
            chip_out[m - 1] = total.astype(BF)
            out.append(
                send(
                    chip_out.at[m - 1],
                    chip_in.at[m - 1],
                    chip_send.at[m - 1],
                    chip_recv.at[m - 1],
                    ctx=ahead[m],
                )
            )
    for m in range(1, chips):
        out[m - 1].wait_recv()
        total = total + chip_in[m - 1].astype(F32)
    return total, side + out


def scatter_scratch(ctx_size, rows, width):
    chips = ctx_size // 2
    return [
        pltpu.VMEM((chips, rows, width), BF),
        pltpu.VMEM((chips, rows, width), BF),
        pltpu.VMEM((chips - 1, rows, width), BF),
        pltpu.VMEM((chips - 1, rows, width), BF),
    ] + [pltpu.SemaphoreType.DMA((chips,))] * 4


def out_kernel(
    ctx_size, wa_size, mixed_ref, w_ref, x_ref, gain_ref, hidden_ref, acts_ref, *scratch
):
    refs, (act_send, act_recv) = scratch[:8], scratch[8:]
    ctx, wa, core, chip, beside, ahead, behind, up, down = places(ctx_size, wa_size)
    greet([beside] + ahead[1:], up[1:])
    rows = x_ref.shape[0]

    def part_of(device):
        block = mixed_ref[pl.ds(pl.multiple_of(device * rows, rows), rows), :]
        return jnp.dot(block, w_ref[...], preferred_element_type=F32)

    total, pending = plane_scatter(part_of, ctx_size, core, chip, beside, ahead, refs)
    hidden = x_ref[...].astype(F32) + total
    hidden_ref[...] = hidden
    scale = lax.rsqrt(jnp.mean(hidden * hidden, axis=-1, keepdims=True) + EPSILON)
    acts_ref[0] = (hidden * scale * gain_ref[...]).astype(BF)
    copies = [
        send(acts_ref.at[0], acts_ref.at[s], act_send.at[s], act_recv.at[s], wa=up[s])
        for s in range(1, wa_size)
    ]
    for copy in pending:
        copy.wait_send()
    for copy in copies:
        copy.wait()


def out_project(mixed, w_rows, x_own, gain, ctx_size, wa_size):
    rows, width = x_own.shape
    vmem = pl.BlockSpec(memory_space=pltpu.VMEM)
    return pl.pallas_call(
        functools.partial(out_kernel, ctx_size, wa_size),
        out_shape=(
            jax.ShapeDtypeStruct((rows, width), F32),
            jax.ShapeDtypeStruct((wa_size, rows, width), BF),
        ),
        in_specs=[vmem] * 4,
        out_specs=[vmem] * 2,
        scratch_shapes=scatter_scratch(ctx_size, rows, width)
        + [pltpu.SemaphoreType.DMA((wa_size,))] * 2,
        compiler_params=pltpu.CompilerParams(
            collective_id=1, has_side_effects=True, vmem_limit_bytes=VMEM_LIMIT
        ),
        cost_estimate=pl.CostEstimate(
            flops=2 * mixed.size * width, bytes_accessed=200_000_000, transcendentals=0
        ),
        name="out_project",
    )(mixed, w_rows, x_own, gain)


def turn_kernel(
    ctx_size, wa_size, parts_ref, hidden_ref, gain_ref, dz_ref, all_ref, gain_out_ref, *scratch
):
    got_ref, wa_send, wa_recv = scratch[:3]
    plane_sems = scratch[3:]
    ctx, wa, core, chip, beside, ahead, behind, up, down = places(ctx_size, wa_size)
    greet([beside] + ahead[1:], down[1:])
    copies = [
        send(parts_ref.at[s], got_ref.at[s], wa_send.at[s], wa_recv.at[s], wa=down[s])
        for s in range(1, wa_size)
    ]
    hidden = hidden_ref[...]
    scale = lax.rsqrt(jnp.mean(hidden * hidden, axis=-1, keepdims=True) + EPSILON)
    normed = hidden * scale
    d_normed = parts_ref[0].astype(F32)
    for s in range(1, wa_size):
        copies[s - 1].wait_recv()
        d_normed = d_normed + got_ref[s].astype(F32)
    gain_out_ref[...] = jnp.sum(d_normed * normed, axis=0, keepdims=True)
    scaled = d_normed * gain_ref[...]
    d_hidden = dz_ref[...].astype(F32) + scale * (
        scaled - normed * jnp.mean(scaled * normed, axis=-1, keepdims=True)
    )
    all_ref[ctx] = d_hidden.astype(BF)
    own = all_ref.at[ctx]
    plane, side = plane_gather_start(own, all_ref, ctx, beside, ahead, plane_sems)
    for copy in copies:
        copy.wait_send()
    plane_gather_finish(all_ref, beside, behind, plane, side, plane_sems)


def turn(parts, hidden, gain, dz, ctx_size, wa_size):
    rows, width = hidden.shape
    chips = ctx_size // 2
    vmem = pl.BlockSpec(memory_space=pltpu.VMEM)
    return pl.pallas_call(
        functools.partial(turn_kernel, ctx_size, wa_size),
        out_shape=(
            jax.ShapeDtypeStruct((ctx_size, rows, width), BF),
            jax.ShapeDtypeStruct((1, width), F32),
        ),
        in_specs=[vmem] * 4,
        out_specs=[vmem] * 2,
        scratch_shapes=[pltpu.VMEM((wa_size, rows, width), BF)]
        + [pltpu.SemaphoreType.DMA((wa_size,))] * 2
        + [pltpu.SemaphoreType.DMA((chips,))] * 4,
        compiler_params=pltpu.CompilerParams(
            collective_id=2, has_side_effects=True, vmem_limit_bytes=VMEM_LIMIT
        ),
        cost_estimate=pl.CostEstimate(flops=0, bytes_accessed=200_000_000, transcendentals=0),
        name="turn",
    )(parts, hidden, gain, dz)


def last_kernel(
    ctx_size,
    wa_size,
    grads_ref,
    w_ref,
    dw_ref,
    dealt_ref,
    x_ref,
    gain_ref,
    dh_ref,
    out_ref,
    dw_out_ref,
    gain_out_ref,
    *scratch,
):
    refs, (dw_in, dw_send, dw_recv) = scratch[:8], scratch[8:]
    ctx, wa, core, chip, beside, ahead, behind, up, down = places(ctx_size, wa_size)
    greet([beside] + ahead[1:], up[1:])
    copies = [
        send(dw_ref.at[up[s]], dw_in.at[s], dw_send.at[s], dw_recv.at[s], wa=up[s])
        for s in range(1, wa_size)
    ]
    rows = x_ref.shape[0]
    gain_out_ref[...] = jnp.zeros_like(gain_out_ref)

    def part_of(device):
        place = pl.ds(pl.multiple_of(device * rows, rows), rows)
        part = lax.dot_general(
            grads_ref[place, :],
            w_ref[...],
            (((1,), (1,)), ((), ())),
            preferred_element_type=F32,
        )
        x = dealt_ref[place, :].astype(F32)
        scale = lax.rsqrt(jnp.mean(x * x, axis=-1, keepdims=True) + EPSILON)
        gain_out_ref[...] += jnp.sum(part * (x * scale), axis=0, keepdims=True)
        return part

    d_normed, pending = plane_scatter(part_of, ctx_size, core, chip, beside, ahead, refs)
    x = x_ref[...].astype(F32)
    scale = lax.rsqrt(jnp.mean(x * x, axis=-1, keepdims=True) + EPSILON)
    normed = x * scale
    scaled = d_normed * gain_ref[...]
    d_x = dh_ref[...].astype(F32) + scale * (
        scaled - normed * jnp.mean(scaled * normed, axis=-1, keepdims=True)
    )
    out_ref[...] = d_x.astype(BF)
    for copy in pending:
        copy.wait_send()
    total = dw_ref[wa].astype(F32)
    for s in range(1, wa_size):
        copies[s - 1].wait_recv()
        total = total + dw_in[s].astype(F32)
    dw_out_ref[...] = total.astype(BF)
    for copy in copies:
        copy.wait_send()


def last_exchange(grads, w, dw, dealt, x_own, gain, dh, ctx_size, wa_size):
    rows, width = x_own.shape
    vmem = pl.BlockSpec(memory_space=pltpu.VMEM)
    return pl.pallas_call(
        functools.partial(last_kernel, ctx_size, wa_size),
        out_shape=(
            jax.ShapeDtypeStruct((rows, width), BF),
            jax.ShapeDtypeStruct(dw.shape[1:], BF),
            jax.ShapeDtypeStruct((1, width), F32),
        ),
        in_specs=[vmem] * 7,
        out_specs=[vmem] * 3,
        scratch_shapes=scatter_scratch(ctx_size, rows, width)
        + [pltpu.VMEM(dw.shape, BF)]
        + [pltpu.SemaphoreType.DMA((wa_size,))] * 2,
        compiler_params=pltpu.CompilerParams(
            collective_id=3, has_side_effects=True, vmem_limit_bytes=VMEM_LIMIT
        ),
        cost_estimate=pl.CostEstimate(
            flops=2 * grads.size * width, bytes_accessed=250_000_000, transcendentals=0
        ),
        name="last_exchange",
    )(grads, w, dw, dealt, x_own, gain, dh)


def per_device(
    tokens, lengths, dealing, norm1_gain, w_qkv, w_out, norm2_gain, w_gate_up, w_down, grad_out
):
    tok_rows, width = tokens.shape[1], tokens.shape[2]
    ctx_size = lax.axis_size("ctx")
    wa_size = lax.axis_size("wa")
    ctx_index = lax.axis_index("ctx")
    wa_index = lax.axis_index("wa")
    block_order = dealing[0]
    block_total = block_order.shape[0]
    group_rows = block_total * BLOCK
    own_blocks = tok_rows // BLOCK
    first_length = lengths[0, 0]
    heads_own = HEADS // ctx_size
    head_cols = heads_own * HEAD
    wa_rows = width // wa_size
    ff_total = w_gate_up.shape[1] // 2
    ff_own = w_down.shape[0]
    piece_rows = wa_rows // ctx_size

    block_ids = jnp.arange(block_total, dtype=jnp.int32)
    inverse = jnp.sum(
        jnp.where(block_order[None, :] == block_ids[:, None], block_ids[None, :], 0), axis=1
    )

    def pick_blocks(values, order):
        parts = [
            lax.dynamic_slice_in_dim(values, order[i] * BLOCK, BLOCK) for i in range(block_total)
        ]
        return jnp.concatenate(parts, axis=0)

    qkv_slice = jnp.concatenate(
        [
            lax.dynamic_slice_in_dim(w_qkv, part * width + ctx_index * head_cols, head_cols, 1)
            for part in range(3)
        ],
        axis=1,
    )
    dealt, qkv_cols = gather_both(tokens[0], qkv_slice, ctx_size, wa_size)
    dealt = dealt.reshape(group_rows, width)
    qkv_cols = qkv_cols.reshape(width, 3 * head_cols)
    out_slice = lax.dynamic_slice_in_dim(w_out, ctx_index * head_cols, head_cols, 1)
    out_cols = gather_rows(out_slice, "wa")
    out_rows = lax.all_to_all(out_cols, "ctx", 0, 1, tiled=True)
    gu_piece = lax.dynamic_slice_in_dim(w_gate_up, ctx_index * piece_rows, piece_rows, 0)
    gu_piece, qkv_cols = lax.optimization_barrier((gu_piece, qkv_cols))
    gu_send = jnp.stack(
        [
            jnp.concatenate(
                [
                    gu_piece[:, to * ff_own : (to + 1) * ff_own],
                    gu_piece[:, ff_total + to * ff_own : ff_total + (to + 1) * ff_own],
                ],
                axis=1,
            )
            for to in range(wa_size)
        ]
    )
    gu_parts = [take(gu_send, (wa_index - s) % wa_size) for s in range(wa_size)]
    gu_got = [gu_parts[0]] + [shifted(gu_parts[s], "wa", -s) for s in range(1, wa_size)]
    gu_mine = jnp.stack([gu_got[(wa_size - s) % wa_size] for s in range(wa_size)])
    gu_mine = jnp.stack([take(gu_mine, (wa_index - i) % wa_size) for i in range(wa_size)])
    gu_all = lax.all_gather(gu_mine, "ctx", axis=0)
    gu_weight = jnp.transpose(gu_all, (1, 0, 2, 3)).reshape(width, 2 * ff_own)

    given_b = pick_blocks(dealt, inverse)
    given = given_b.astype(F32)
    positions = jnp.arange(group_rows, dtype=jnp.int32)
    segments = (positions >= first_length).astype(jnp.int32)
    cosine, sine = rotary_tables(positions - segments * first_length)
    normed_one = given * rms_scale(given)
    act_one = (normed_one * norm1_gain).astype(BF)

    projected = dot_plain(act_one, qkv_cols)
    parts = [
        projected[:, i * head_cols : (i + 1) * head_cols].reshape(group_rows, heads_own, HEAD)
        for i in range(3)
    ]
    query_b = rotate(parts[0], cosine, sine).astype(BF)
    key_b = rotate(parts[1], cosine, sine).astype(BF)
    value_b = parts[2].astype(BF)
    score_scale = math.sqrt(HEAD)
    distance = positions[:, None] - positions[None, :]
    allowed = (segments[:, None] == segments[None, :]) & (distance >= 0) & (distance < WINDOW)
    scores = jnp.einsum("qhe,khe->hqk", query_b, key_b, preferred_element_type=F32) / score_scale
    scores = jnp.where(allowed[None], scores, -jnp.inf)
    largest = jnp.max(scores, axis=2, keepdims=True)
    weights = jnp.exp(scores - largest)
    probs = weights / jnp.sum(weights, axis=2, keepdims=True)
    probs_b = probs.astype(BF)
    mixed = jnp.einsum("hqk,khe->qhe", probs_b, value_b, preferred_element_type=F32)
    mixed_b = mixed.reshape(group_rows, head_cols).astype(BF)

    own_given = lax.dynamic_slice_in_dim(given_b, ctx_index * tok_rows, tok_rows)
    gain_two = norm2_gain[None, :]
    hidden, acts = out_project(mixed_b, out_rows, own_given, gain_two, ctx_size, wa_size)
    act_two = acts.reshape(wa_size * tok_rows, width)
    early = lax.optimization_barrier((grad_out[0], qkv_cols))[0]
    grads_all = lax.all_gather(early, "wa", axis=0)
    cotangent = jnp.concatenate(
        [take(grads_all, (wa_index - s) % wa_size) for s in range(wa_size)], axis=0
    )

    gate_up = dot_plain(act_two, gu_weight)
    gate_part = gate_up[:, :ff_own]
    up_part = gate_up[:, ff_own:]
    sigmoid_gate = jax.nn.sigmoid(gate_part)
    silu_gate = gate_part * sigmoid_gate
    inner_b = (silu_gate * up_part).astype(BF)

    d_inner = dot_right_t(cotangent, w_down)
    d_gate = d_inner * up_part * sigmoid_gate * (1.0 + gate_part * (1.0 - sigmoid_gate))
    d_gu_b = jnp.concatenate([d_gate, d_inner * silu_gate], axis=1).astype(BF)
    d_act = dot_right_t(d_gu_b, gu_weight).astype(BF).reshape(wa_size, tok_rows, width)
    d_branches, gain_two_part = turn(d_act, hidden, gain_two, grad_out[0], ctx_size, wa_size)
    d_branch_b = d_branches.reshape(group_rows, width)
    mlp_parts, d_branch_b = lax.optimization_barrier((dot_plain(inner_b, w_down).astype(BF), d_branch_b))
    result = direct_scatter(split(mlp_parts, wa_size), "wa")
    out_given = (hidden + result).astype(BF)

    core = ctx_index % 2
    chip = ctx_index // 2
    chips = ctx_size // 2
    down_part = dot_left_t(inner_b, cotangent).astype(BF)
    down_half = width // 2
    down_send = lax.dynamic_slice_in_dim(down_part, (1 - core) * down_half, down_half, 1)
    down_keep = lax.dynamic_slice_in_dim(down_part, core * down_half, down_half, 1)
    down_sum = (down_keep.astype(F32) + crossed(down_send, "ctx", 1).astype(F32)).astype(BF)
    down_cols = down_half // chips
    down_mine = lax.dynamic_slice_in_dim(down_sum, chip * down_cols, down_cols, 1).astype(F32)
    for i in range(1, chips):
        down_piece = lax.dynamic_slice_in_dim(down_sum, (chip ^ i) * down_cols, down_cols, 1)
        down_mine = down_mine + crossed(down_piece, "ctx", 2 * i).astype(F32)
    down_all = lax.all_gather(down_mine.astype(BF), "ctx", axis=0)
    d_down = jnp.concatenate(
        [down_all[(i % chips) * 2 + i // chips] for i in range(ctx_size)], axis=1
    ).astype(F32)

    gu_share = dot_left_t(act_two, d_gu_b).astype(BF)
    gu_share = gu_share.reshape(wa_size, chips, 2, piece_rows, 2 * ff_own)
    gu_send_back = lax.dynamic_slice_in_dim(gu_share, 1 - core, 1, 2)[:, :, 0]
    gu_keep = lax.dynamic_slice_in_dim(gu_share, core, 1, 2)[:, :, 0]
    gu_sum = (gu_keep.astype(F32) + crossed(gu_send_back, "ctx", 1).astype(F32)).astype(BF)
    d_gu_piece = lax.dynamic_slice_in_dim(gu_sum, chip, 1, 1)[:, 0].astype(F32)
    for i in range(1, chips):
        gu_one = lax.dynamic_slice_in_dim(gu_sum, chip ^ i, 1, 1)[:, 0]
        d_gu_piece = d_gu_piece + crossed(gu_one, "ctx", 2 * i).astype(F32)
    d_gu_piece = d_gu_piece.astype(BF)
    back = [take(d_gu_piece, (wa_index - s) % wa_size) for s in range(wa_size)]
    back = [back[0]] + [shifted(back[s], "wa", -s) for s in range(1, wa_size)]
    d_gu_back = jnp.stack([back[(wa_size - s) % wa_size] for s in range(wa_size)])
    d_gu_back = jnp.stack([take(d_gu_back, (wa_index - i) % wa_size) for i in range(wa_size)])
    d_gu_rows = jnp.concatenate(
        [d_gu_back[i, :, :ff_own] for i in range(wa_size)]
        + [d_gu_back[i, :, ff_own:] for i in range(wa_size)],
        axis=1,
    )
    d_gate_up = gather_rows(d_gu_rows, "ctx").astype(F32)

    grad_mixed_b = dot_right_t(d_branch_b, out_rows).astype(BF)
    d_out_part = dot_left_t(mixed_b, d_branch_b).astype(BF)
    d_out_cols = lax.all_to_all(d_out_part, "ctx", 1, 0, tiled=True)
    out_parts = d_out_cols.reshape(wa_size, wa_rows, head_cols)
    d_out_mine = direct_scatter(
        [take(out_parts, (wa_index - s) % wa_size) for s in range(wa_size)], "wa"
    ).astype(BF)
    d_out = lax.all_gather(d_out_mine, "ctx", axis=1, tiled=True).astype(F32)

    grad_heads = grad_mixed_b.reshape(group_rows, heads_own, HEAD)
    d_probs = jnp.einsum("qhe,khe->hqk", grad_heads, value_b, preferred_element_type=F32)
    row_dot = jnp.sum(probs * d_probs, axis=2, keepdims=True)
    d_scores = (probs * (d_probs - row_dot)).astype(BF)
    d_query = jnp.einsum("hqk,khe->qhe", d_scores, key_b, preferred_element_type=F32) / score_scale
    d_key = jnp.einsum("hqk,qhe->khe", d_scores, query_b, preferred_element_type=F32) / score_scale
    d_value = jnp.einsum("hqk,qhe->khe", probs_b, grad_heads, preferred_element_type=F32)
    d_qkv_b = jnp.concatenate(
        [
            rotate(d_query, cosine, -sine).reshape(group_rows, head_cols),
            rotate(d_key, cosine, -sine).reshape(group_rows, head_cols),
            d_value.reshape(group_rows, head_cols),
        ],
        axis=1,
    ).astype(BF)
    qkv_parts = dot_left_t(act_one, d_qkv_b).astype(BF).reshape(wa_size, wa_rows, 3 * head_cols)
    own_order = lax.dynamic_slice_in_dim(block_order, ctx_index * own_blocks, own_blocks)
    d_hidden_dealt = jnp.concatenate(
        [
            lax.dynamic_slice_in_dim(d_branch_b, own_order[i] * BLOCK, BLOCK)
            for i in range(own_blocks)
        ],
        axis=0,
    )
    d_tokens, d_qkv_share, gain_one_part = last_exchange(
        pick_blocks(d_qkv_b, block_order),
        qkv_cols,
        qkv_parts,
        dealt,
        tokens[0],
        norm1_gain[None, :],
        d_hidden_dealt,
        ctx_size,
        wa_size,
    )
    d_qkv_all = lax.all_gather(d_qkv_share, "ctx", axis=0)
    d_qkv = jnp.transpose(
        d_qkv_all.reshape(ctx_size, wa_rows, 3, head_cols), (1, 2, 0, 3)
    ).reshape(wa_rows, 3 * width).astype(F32)

    gain_parts = jnp.concatenate([gain_one_part, gain_two_part], axis=0)
    gain_sums = sum_everywhere(gain_parts)
    return (
        out_given[None],
        d_tokens[None],
        gain_sums[0],
        d_qkv,
        d_out,
        gain_sums[1],
        d_gate_up,
        d_down,
    )


def solution(mesh):
    in_specs = (
        P("wa", "ctx", None),
        P("wa", None),
        P("wa", None),
        P(),
        P("wa", None),
        P("wa", None),
        P(),
        P("wa", None),
        P("wa", None),
        P("wa", "ctx", None),
    )
    out_specs = (
        P("wa", "ctx", None),
        P("wa", "ctx", None),
        P(),
        P("wa", None),
        P("wa", None),
        P(),
        P("wa", None),
        P("wa", None),
    )
    return jax.shard_map(
        per_device, mesh=mesh, in_specs=in_specs, out_specs=out_specs, check_vma=False
    )
```

```python
import functools
import math
import types

import jax
import jax.numpy as jnp
from jax import lax
from jax.experimental import pallas as pl
from jax.experimental.pallas import tpu as pltpu
from jax.sharding import PartitionSpec as P

HEADS = 16
HEAD = 128
WINDOW = 2048
BLOCK = 128

EPSILON = 1e-06
BF = jnp.bfloat16
F32 = jnp.float32
VMEM_LIMIT = 56 * 1024 * 1024


def dot_plain(left, right):
    return jnp.dot(left, right, preferred_element_type=F32)


def dot_right_t(left, right):
    return lax.dot_general(left, right, (((1,), (1,)), ((), ())), preferred_element_type=F32)


def dot_left_t(left, right):
    return lax.dot_general(left, right, (((0,), (0,)), ((), ())), preferred_element_type=F32)


def rms_scale(values):
    return lax.rsqrt(jnp.mean(values * values, axis=-1, keepdims=True) + EPSILON)


def rotary_tables(seq_pos):
    half_width = HEAD // 2
    inverse_freq = jnp.power(10000.0, -2.0 * jnp.arange(half_width, dtype=F32) / HEAD)
    angles = seq_pos.astype(F32)[:, None] * inverse_freq[None, :]
    return (jnp.cos(angles)[:, None, :], jnp.sin(angles)[:, None, :])


def rotate(values, cosine, sine):
    half_width = HEAD // 2
    first = values[..., :half_width]
    second = values[..., half_width:]
    return jnp.concatenate(
        [first * cosine - second * sine, first * sine + second * cosine], axis=-1
    )


def gather_rows(values, axis):
    return lax.all_gather(values, axis, axis=0, tiled=True)


def take(values, index):
    return lax.dynamic_index_in_dim(values, index, 0, keepdims=False)


def split(values, count):
    rows = values.shape[0] // count
    return [values[i * rows : (i + 1) * rows] for i in range(count)]


MESH = pl.DeviceIdType.MESH


def greet(ctx_peers, wa_peers):
    barrier = pltpu.get_barrier_semaphore()
    for peer in ctx_peers:
        pl.semaphore_signal(barrier, inc=1, device_id={"ctx": peer}, device_id_type=MESH)
    for peer in wa_peers:
        pl.semaphore_signal(barrier, inc=1, device_id={"wa": peer}, device_id_type=MESH)
    pl.semaphore_wait(barrier, len(ctx_peers) + len(wa_peers))


def send(source, target, send_sem, recv_sem, **peer):
    copy = pltpu.make_async_remote_copy(
        src_ref=source,
        dst_ref=target,
        send_sem=send_sem,
        recv_sem=recv_sem,
        device_id=peer,
        device_id_type=MESH,
    )
    copy.start()
    return copy


def place_of(ctx_size, wa_size):
    chips = ctx_size // 2
    p = types.SimpleNamespace(ctx_size=ctx_size, wa_size=wa_size, chips=chips)
    p.ctx, p.wa = lax.axis_index("ctx"), lax.axis_index("wa")
    p.core, p.chip = lax.rem(p.ctx, 2), lax.div(p.ctx, 2)
    p.beside = p.chip * 2 + 1 - p.core
    p.ahead = [lax.rem(p.chip + m, chips) * 2 + p.core for m in range(chips)]
    p.behind = [lax.rem(p.chip + chips - m, chips) * 2 + p.core for m in range(chips)]
    p.up = [lax.rem(p.wa + s, wa_size) for s in range(wa_size)]
    p.down = [lax.rem(p.wa + wa_size - s, wa_size) for s in range(wa_size)]
    p.square = chips == 4
    if p.square:
        p.near = [p.chip + 1 - 2 * lax.rem(p.chip, 2), lax.rem(p.chip + 2, 4)]
        p.far = 3 - p.chip
    return p


def on_core(p, chip):
    return chip * 2 + p.core


def off_core(p, chip):
    return chip * 2 + 1 - p.core


def plane_sems(ctx_size):
    count = max(ctx_size // 2, 5)
    return [pltpu.SemaphoreType.DMA((count,))] * 4


class Spread:
    def __init__(self, p, own, slot, half, sems):
        self.p, self.own, self.slot, self.half = p, own, slot, half
        self.chip_send, self.chip_recv, self.side_send, self.side_recv = sems
        self.chip, self.side = [], []

    def across(self, source, target, chip):
        i = len(self.chip)
        self.chip.append(
            send(source, target, self.chip_send.at[i], self.chip_recv.at[i], ctx=on_core(self.p, chip))
        )

    def aside(self, source, target):
        i = len(self.side)
        self.side.append(
            send(source, target, self.side_send.at[i], self.side_recv.at[i], ctx=self.p.beside)
        )

    def start(self):
        p = self.p
        target = self.slot(p.ctx)
        if p.square:
            for chip in p.near:
                self.across(self.own, target, chip)
        else:
            for m in range(1, p.chips):
                self.across(self.own, target, lax.rem(p.chip + m, p.chips))
        self.aside(self.own, target)

    def arrivals(self):
        p = self.p
        if not p.square:
            for m in range(1, p.chips):
                self.chip[m - 1].wait_recv()
                block = self.slot(p.behind[m])
                self.aside(block, block)
                yield p.behind[m]
            self.side[0].wait_recv()
            yield p.beside
            for m in range(1, p.chips):
                self.side[m].wait_recv()
                yield off_core(p, lax.rem(p.chip + p.chips - m, p.chips))
            return
        for i in range(2):
            self.chip[i].wait_recv()
            device = on_core(p, p.near[i])
            part = self.half(device, i)
            self.across(part, part, p.near[1 - i])
            self.aside(self.slot(device), self.slot(device))
            yield device
        self.side[0].wait_recv()
        yield p.beside
        for i in range(2):
            self.side[1 + i].wait_recv()
            yield off_core(p, p.near[i])
        device = on_core(p, p.far)
        for i in range(2):
            self.chip[2 + i].wait_recv()
            part = self.half(device, i)
            self.aside(part, part)
        yield device
        for i in range(2):
            self.side[3 + i].wait_recv()
        yield off_core(p, p.far)

    def finish(self):
        for copy in self.chip + self.side:
            copy.wait_send()


class Fold:
    def __init__(self, p, source, kept, got, near, sent, piece, half, add, sems):
        self.p, self.source, self.kept, self.got, self.near, self.sent = p, source, kept, got, near, sent
        self.piece, self.half, self.add = piece, half, add
        self.chip_send, self.chip_recv, self.side_send, self.side_recv = sems
        self.chip = []

    def across(self, source, target, chip):
        i = len(self.chip)
        self.chip.append(
            send(source, target, self.chip_send.at[i], self.chip_recv.at[i], ctx=on_core(self.p, chip))
        )

    def start(self):
        p = self.p
        self.side = send(
            self.source(1 - p.core), self.got, self.side_send.at[0], self.side_recv.at[0], ctx=p.beside
        )
        self.load = pltpu.make_async_copy(self.source(p.core), self.kept, self.side_send.at[1])
        self.load.start()

    def between(self):
        p = self.p
        self.load.wait()
        self.side.wait_recv()
        self.add(self.kept, self.got)
        if not p.square:
            for m in range(1, p.chips):
                chip = lax.rem(p.chip + m, p.chips)
                self.across(self.piece(self.kept, chip), self.sent.at[m - 1], chip)
            return
        for i in range(2):
            self.across(self.half(self.kept, p.far, i), self.near.at[i], p.near[i])
        for i in range(2):
            self.across(
                self.half(self.kept, p.near[i], i), self.half(self.sent.at[i], None, i), p.near[i]
            )

    def onward(self):
        p = self.p
        if not p.square:
            return
        for i in range(2):
            self.chip[i].wait_recv()
            part = self.half(self.kept, p.near[1 - i], i)
            self.add(part, self.near.at[i])
            self.across(part, self.half(self.sent.at[1 - i], None, i), p.near[1 - i])

    def total(self):
        p = self.p
        for copy in self.chip[2:] if p.square else self.chip:
            copy.wait_recv()
        mine = self.piece(self.kept, p.chip)
        for i in range(2 if p.square else p.chips - 1):
            self.add(mine, self.sent.at[i])
        return mine

    def finish(self):
        self.side.wait_send()
        for copy in self.chip:
            copy.wait_send()


def add_rows(into, other, step):
    def one(i, carried):
        place = pl.ds(pl.multiple_of(i * step, step), step)
        into[place, :] = (into[place, :].astype(F32) + other[place, :].astype(F32)).astype(BF)
        return carried

    lax.fori_loop(0, into.shape[0] // step, one, 0)


def add_blocks(into, other):
    lead = into.shape[:-2]

    def one(i, carried):
        at = (i,) if len(lead) == 1 else (i // lead[1], i % lead[1])
        into[at] = (into[at].astype(F32) + other[at].astype(F32)).astype(BF)
        return carried

    lax.fori_loop(0, math.prod(lead), one, 0)


class Stager:
    def __init__(self, stage, sems, widen):
        self.stage, self.sems, self.widen = stage, sems, widen
        self.flying = [[], []]
        self.count = 0

    def put(self, block, targets):
        slot = self.count % 2
        self.count += 1
        for copy in self.flying[slot]:
            copy.wait()
        stage = self.stage.at[slot]
        self.widen(stage, block)
        self.flying[slot] = []
        for i, (target, columns) in enumerate(targets):
            part = stage if columns is None else stage.at[:, columns]
            copy = pltpu.make_async_copy(part, target, self.sems.at[slot, i])
            copy.start()
            self.flying[slot].append(copy)

    def finish(self):
        for copies in self.flying:
            for copy in copies:
                copy.wait()


def widen_rows(step):
    def widen(stage, block):
        def one(i, carried):
            place = pl.ds(pl.multiple_of(i * step, step), step)
            stage[place, :] = block[place, :].astype(F32)
            return carried

        lax.fori_loop(0, stage.shape[0] // step, one, 0)

    return widen


class Scatter:
    def __init__(self, p, part_of, refs):
        self.p, self.part_of, self.refs = p, part_of, refs

    def start(self):
        p = self.p
        side_out, side_in, chip_out, chip_in, side_send, side_recv, chip_send, chip_recv = self.refs
        self.side, self.out = [], []
        order = list(range(1, p.chips)) + [0]
        for m in order:
            side_out[m] = self.part_of(lax.div(p.ahead[m], 2) * 2 + 1 - p.core).astype(BF)
            self.side.append(
                send(side_out.at[m], side_in.at[m], side_send.at[m], side_recv.at[m], ctx=p.beside)
            )
        for i, m in enumerate(order):
            mine = self.part_of(p.ahead[m])
            self.side[i].wait_recv()
            self.kept = mine + side_in[m].astype(F32)
            if m > 0:
                chip_out[m - 1] = self.kept.astype(BF)
                self.out.append(
                    send(
                        chip_out.at[m - 1],
                        chip_in.at[m - 1],
                        chip_send.at[m - 1],
                        chip_recv.at[m - 1],
                        ctx=p.ahead[m],
                    )
                )

    def total(self):
        chip_in = self.refs[3]
        total = self.kept
        for m in range(1, self.p.chips):
            self.out[m - 1].wait_recv()
            total = total + chip_in[m - 1].astype(F32)
        return total

    def finish(self):
        for copy in self.side + self.out:
            copy.wait_send()


def scatter_scratch(ctx_size, rows, width):
    chips = ctx_size // 2
    return [
        pltpu.VMEM((chips, rows, width), BF),
        pltpu.VMEM((chips, rows, width), BF),
        pltpu.VMEM((chips - 1, rows, width), BF),
        pltpu.VMEM((chips - 1, rows, width), BF),
    ] + [pltpu.SemaphoreType.DMA((chips,))] * 4


def norm_back(x, scale, gain, d_scaled, d_other):
    normed = x * scale
    scaled = d_scaled * gain
    return d_other + scale * (
        scaled - normed * jnp.mean(scaled * normed, axis=-1, keepdims=True)
    )


def gather_kernel(ctx_size, wa_size, cuts, x_ref, w_ref, xs_ref, ws_ref, *sems):
    p = place_of(ctx_size, wa_size)
    ring_send, ring_recv, local = sems[4:]
    greet([p.beside] + p.ahead[1:], [p.up[1], p.down[1]])
    rows = w_ref.shape[0] // cuts
    half_rows = x_ref.shape[0] // 2
    ring = []
    for i in range(cuts):
        part = pl.ds(i * rows, rows)
        ring.append(
            send(
                w_ref.at[part],
                ws_ref.at[p.wa, part],
                ring_send.at[0, i],
                ring_recv.at[0, i],
                wa=p.up[1],
            )
        )
    spread = Spread(
        p,
        x_ref,
        lambda d: xs_ref.at[d],
        lambda d, h: xs_ref.at[d, pl.ds(h * half_rows, half_rows)],
        sems[:4],
    )
    spread.start()
    own_x = pltpu.make_async_copy(x_ref, xs_ref.at[p.ctx], local.at[0])
    own_w = pltpu.make_async_copy(w_ref, ws_ref.at[p.wa], local.at[1])
    own_x.start()
    own_w.start()
    late = []
    for step in range(1, wa_size):
        for i in range(cuts):
            ring[i].wait_recv()
            late.append(ring[i])
            if step < wa_size - 1:
                block = ws_ref.at[p.down[step], pl.ds(i * rows, rows)]
                ring[i] = send(
                    block, block, ring_send.at[step, i], ring_recv.at[step, i], wa=p.up[1]
                )
        if step == 1:
            for _ in spread.arrivals():
                pass
    for copy in late:
        copy.wait_send()
    spread.finish()
    own_x.wait()
    own_w.wait()


def gather_both(x, w, ctx_size, wa_size, cuts=4):
    anywhere = pl.BlockSpec(memory_space=pl.ANY)
    return pl.pallas_call(
        functools.partial(gather_kernel, ctx_size, wa_size, cuts),
        out_shape=(
            jax.ShapeDtypeStruct((ctx_size,) + x.shape, x.dtype),
            jax.ShapeDtypeStruct((wa_size,) + w.shape, w.dtype),
        ),
        in_specs=[anywhere] * 2,
        out_specs=[anywhere] * 2,
        scratch_shapes=plane_sems(ctx_size)
        + [pltpu.SemaphoreType.DMA((wa_size - 1, cuts))] * 2
        + [pltpu.SemaphoreType.DMA((2,))],
        compiler_params=pltpu.CompilerParams(collective_id=0, has_side_effects=True),
        cost_estimate=pl.CostEstimate(flops=0, bytes_accessed=200_000_000, transcendentals=0),
        name="gather_both",
    )(x, w)


def out_kernel(
    ctx_size,
    wa_size,
    mixed_ref,
    w_ref,
    x_ref,
    gain_ref,
    gu_ref,
    hidden_ref,
    acts_ref,
    gw_ref,
    *scratch,
):
    p = place_of(ctx_size, wa_size)
    act_send, act_recv, gu_send, gu_recv, local = scratch[12:]
    greet([p.beside] + p.ahead[1:], p.up[1:])
    deal = [
        send(
            gu_ref.at[p.up[s]], gw_ref.at[p.wa, p.ctx], gu_send.at[s], gu_recv.at[s], wa=p.up[s]
        )
        for s in range(1, wa_size)
    ]
    own = pltpu.make_async_copy(gu_ref.at[p.wa], gw_ref.at[p.wa, p.ctx], local.at[0])
    own.start()
    rows = x_ref.shape[0]

    def part_of(device):
        block = mixed_ref[pl.ds(pl.multiple_of(device * rows, rows), rows), :]
        return jnp.dot(block, w_ref[...], preferred_element_type=F32)

    scatter = Scatter(p, part_of, scratch[:8])
    scatter.start()
    hidden = x_ref[...].astype(F32) + scatter.total()
    hidden_ref[...] = hidden
    scale = lax.rsqrt(jnp.mean(hidden * hidden, axis=-1, keepdims=True) + EPSILON)
    acts_ref[0] = (hidden * scale * gain_ref[...]).astype(BF)
    copies = [
        send(acts_ref.at[0], acts_ref.at[s], act_send.at[s], act_recv.at[s], wa=p.up[s])
        for s in range(1, wa_size)
    ]
    own.wait()
    for copy in deal:
        copy.wait_recv()
    half = wa_size // 2
    spread = Spread(
        p,
        gw_ref.at[:, p.ctx],
        lambda d: gw_ref.at[:, d],
        lambda d, h: gw_ref.at[pl.ds(h * half, half), d],
        scratch[8:12],
    )
    spread.start()
    for _ in spread.arrivals():
        pass
    scatter.finish()
    spread.finish()
    for copy in deal:
        copy.wait_send()
    for copy in copies:
        copy.wait()


def out_project(mixed, w_rows, x_own, gain, gu, ctx_size, wa_size):
    rows, width = x_own.shape
    vmem = pl.BlockSpec(memory_space=pltpu.VMEM)
    anywhere = pl.BlockSpec(memory_space=pl.ANY)
    return pl.pallas_call(
        functools.partial(out_kernel, ctx_size, wa_size),
        out_shape=(
            jax.ShapeDtypeStruct((rows, width), F32),
            jax.ShapeDtypeStruct((wa_size, rows, width), BF),
            jax.ShapeDtypeStruct((wa_size, ctx_size) + gu.shape[1:], BF),
        ),
        in_specs=[vmem] * 4 + [anywhere],
        out_specs=[vmem] * 2 + [anywhere],
        scratch_shapes=scatter_scratch(ctx_size, rows, width)
        + plane_sems(ctx_size)
        + [pltpu.SemaphoreType.DMA((wa_size,))] * 5,
        compiler_params=pltpu.CompilerParams(
            collective_id=1, has_side_effects=True, vmem_limit_bytes=VMEM_LIMIT
        ),
        cost_estimate=pl.CostEstimate(
            flops=2 * mixed.size * width, bytes_accessed=200_000_000, transcendentals=0
        ),
        name="out_project",
    )(mixed, w_rows, x_own, gain, gu)


def turn_kernel(
    ctx_size,
    wa_size,
    parts_ref,
    mlp_ref,
    hidden_ref,
    gain_ref,
    dz_ref,
    gu_ref,
    down_ref,
    all_ref,
    gain_out_ref,
    out_ref,
    gu_out_ref,
    down_out_ref,
    *scratch,
):
    p = place_of(ctx_size, wa_size)
    got_ref, more_ref, wa_send, wa_recv, more_send, more_recv = scratch[:6]
    gu_kept, gu_got, gu_near, gu_sent, down_kept, down_got, down_near, down_sent = scratch[6:14]
    gu_sems, down_sems, spread_sems = scratch[14:18], scratch[18:22], scratch[22:26]
    greet([p.beside] + p.ahead[1:], p.down[1:])
    copies = [
        send(parts_ref.at[s], got_ref.at[s], wa_send.at[s], wa_recv.at[s], wa=p.down[s])
        for s in range(1, wa_size)
    ]
    columns = down_ref.shape[1] // ctx_size
    core_columns = columns * p.chips
    down_rows = down_ref.shape[0] // 2
    half = wa_size // 2

    def down_piece(ref, chip):
        return ref.at[:, pl.ds(pl.multiple_of(chip * columns, columns), columns)]

    def down_half(ref, chip, h):
        place = pl.ds(h * down_rows, down_rows)
        if chip is None:
            return ref.at[place]
        return ref.at[place, pl.ds(pl.multiple_of(chip * columns, columns), columns)]

    down = Fold(
        p,
        lambda core: down_ref.at[
            :, pl.ds(pl.multiple_of(core * core_columns, core_columns), core_columns)
        ],
        down_kept,
        down_got,
        down_near,
        down_sent,
        down_piece,
        down_half,
        lambda into, other: add_rows(into, other, 16),
        down_sems,
    )

    def gu_half(ref, chip, h):
        place = pl.ds(h * half, half)
        return ref.at[place] if chip is None else ref.at[place, chip]

    gu = Fold(
        p,
        lambda core: gu_ref.at[:, :, core],
        gu_kept,
        gu_got,
        gu_near,
        gu_sent,
        lambda ref, chip: ref.at[:, chip],
        gu_half,
        add_blocks,
        gu_sems,
    )
    down.start()
    gu.start()
    down.between()
    gu.between()
    hidden = hidden_ref[...]
    scale = lax.rsqrt(jnp.mean(hidden * hidden, axis=-1, keepdims=True) + EPSILON)
    down.onward()
    d_normed = parts_ref[0].astype(F32)
    for s in range(1, wa_size):
        copies[s - 1].wait_recv()
        d_normed = d_normed + got_ref[s].astype(F32)
    more = [
        send(mlp_ref.at[s], more_ref.at[s], more_send.at[s], more_recv.at[s], wa=p.down[s])
        for s in range(1, wa_size)
    ]
    gain_out_ref[...] = jnp.sum(d_normed * (hidden * scale), axis=0, keepdims=True)
    d_hidden = norm_back(hidden, scale, gain_ref[...], d_normed, dz_ref[...].astype(F32))
    all_ref[p.ctx] = d_hidden.astype(BF)
    half_rows = all_ref.shape[1] // 2
    spread = Spread(
        p,
        all_ref.at[p.ctx],
        lambda d: all_ref.at[d],
        lambda d, h: all_ref.at[d, pl.ds(h * half_rows, half_rows)],
        spread_sems,
    )
    spread.start()
    gu.onward()
    down_out_ref[...] = down.total()[...]
    for _ in spread.arrivals():
        pass
    gu_out_ref[...] = gu.total()[...]
    result = hidden + mlp_ref[0].astype(F32)
    for s in range(1, wa_size):
        more[s - 1].wait_recv()
        result = result + more_ref[s].astype(F32)
    out_ref[...] = result.astype(BF)
    for copy in copies + more:
        copy.wait_send()
    down.finish()
    gu.finish()
    spread.finish()


def turn(parts, mlp, hidden, gain, dz, gu, down, ctx_size, wa_size):
    rows, width = hidden.shape
    chips = ctx_size // 2
    columns = down.shape[1] // ctx_size
    gu_rows, gu_columns = gu.shape[3:]
    vmem = pl.BlockSpec(memory_space=pltpu.VMEM)
    anywhere = pl.BlockSpec(memory_space=pl.ANY)
    many = 2 if chips == 4 else chips - 1
    return pl.pallas_call(
        functools.partial(turn_kernel, ctx_size, wa_size),
        out_shape=(
            jax.ShapeDtypeStruct((ctx_size, rows, width), BF),
            jax.ShapeDtypeStruct((1, width), F32),
            jax.ShapeDtypeStruct((rows, width), BF),
            jax.ShapeDtypeStruct((wa_size, gu_rows, gu_columns), BF),
            jax.ShapeDtypeStruct((down.shape[0], columns), BF),
        ),
        in_specs=[vmem] * 5 + [anywhere] * 2,
        out_specs=[vmem] * 5,
        scratch_shapes=[pltpu.VMEM((wa_size, rows, width), BF)] * 2
        + [pltpu.SemaphoreType.DMA((wa_size,))] * 4
        + [
            pltpu.VMEM((wa_size, chips, gu_rows, gu_columns), BF),
            pltpu.VMEM((wa_size, chips, gu_rows, gu_columns), BF),
            pltpu.VMEM((2, wa_size // 2, gu_rows, gu_columns), BF),
            pltpu.VMEM((many, wa_size, gu_rows, gu_columns), BF),
            pltpu.VMEM((down.shape[0], columns * chips), BF),
            pltpu.VMEM((down.shape[0], columns * chips), BF),
            pltpu.VMEM((2, down.shape[0] // 2, columns), BF),
            pltpu.VMEM((many, down.shape[0], columns), BF),
        ]
        + [pltpu.SemaphoreType.DMA((max(chips, 6),))] * 8
        + plane_sems(ctx_size),
        compiler_params=pltpu.CompilerParams(
            collective_id=2, has_side_effects=True, vmem_limit_bytes=VMEM_LIMIT
        ),
        cost_estimate=pl.CostEstimate(flops=0, bytes_accessed=200_000_000, transcendentals=0),
        name="turn",
    )(parts, mlp, hidden, gain, dz, gu, down)


def last_kernel(
    ctx_size,
    wa_size,
    grads_ref,
    w_ref,
    dealt_ref,
    x_ref,
    gain_ref,
    dh_ref,
    gu_ref,
    dw_ref,
    down_ref,
    out_ref,
    gain_out_ref,
    rows_ref,
    dw_out_ref,
    down_out_ref,
    *scratch,
):
    p = place_of(ctx_size, wa_size)
    gu_in, dw_in, gu_send, gu_recv, dw_send, dw_recv = scratch[8:14]
    downs, stage, stage_sems = scratch[14:17]
    greet([p.beside] + p.ahead[1:], p.up[1:])
    deal = [
        send(gu_ref.at[p.up[s]], gu_in.at[p.wa], gu_send.at[s], gu_recv.at[s], wa=p.up[s])
        for s in range(1, wa_size)
    ]
    copies = [
        send(dw_ref.at[p.up[s]], dw_in.at[s], dw_send.at[s], dw_recv.at[s], wa=p.up[s])
        for s in range(1, wa_size)
    ]
    rows = x_ref.shape[0]
    gain_out_ref[...] = jnp.zeros_like(gain_out_ref)

    def part_of(device):
        place = pl.ds(pl.multiple_of(device * rows, rows), rows)
        part = lax.dot_general(
            grads_ref[place, :],
            w_ref[...],
            (((1,), (1,)), ((), ())),
            preferred_element_type=F32,
        )
        x = dealt_ref[place, :].astype(F32)
        scale = lax.rsqrt(jnp.mean(x * x, axis=-1, keepdims=True) + EPSILON)
        gain_out_ref[...] += jnp.sum(part * (x * scale), axis=0, keepdims=True)
        return part

    scatter = Scatter(p, part_of, scratch[:8])
    scatter.start()
    columns = down_ref.shape[1]
    down_rows = down_ref.shape[0] // 2
    spread = Spread(
        p,
        down_ref,
        lambda d: downs.at[d],
        lambda d, h: downs.at[d, pl.ds(h * down_rows, down_rows)],
        scratch[17:21],
    )
    spread.start()
    stager = Stager(stage, stage_sems, widen_rows(16))

    def put(block, device):
        first = (lax.rem(device, 2) * p.chips + lax.div(device, 2)) * columns
        place = pl.ds(pl.multiple_of(first, columns), columns)
        stager.put(block, [(down_out_ref.at[:, place], None)])

    put(down_ref, p.ctx)
    gu_in[p.wa] = gu_ref[p.wa]
    x = x_ref[...].astype(F32)
    scale = lax.rsqrt(jnp.mean(x * x, axis=-1, keepdims=True) + EPSILON)
    d_normed = scatter.total()
    out_ref[...] = norm_back(
        x, scale, gain_ref[...], d_normed, dh_ref[...].astype(F32)
    ).astype(BF)
    for copy in deal:
        copy.wait_recv()
    own_columns = gu_in.shape[2] // 2
    total_columns = rows_ref.shape[1] // 2
    for i in range(wa_size):
        for part in range(2):
            first = part * total_columns + i * own_columns
            rows_ref[:, first : first + own_columns] = gu_in[
                i, :, part * own_columns : (part + 1) * own_columns
            ]
    for device in spread.arrivals():
        put(downs.at[device], device)
    total = dw_ref[p.wa].astype(F32)
    for s in range(1, wa_size):
        copies[s - 1].wait_recv()
        total = total + dw_in[s].astype(F32)
    dw_out_ref[...] = total.astype(BF)
    stager.finish()
    scatter.finish()
    spread.finish()
    for copy in copies + deal:
        copy.wait_send()


def last_exchange(grads, w, dealt, x_own, gain, dh, gu, dw, down, ctx_size, wa_size):
    rows, width = x_own.shape
    vmem = pl.BlockSpec(memory_space=pltpu.VMEM)
    anywhere = pl.BlockSpec(memory_space=pl.ANY)
    return pl.pallas_call(
        functools.partial(last_kernel, ctx_size, wa_size),
        out_shape=(
            jax.ShapeDtypeStruct((rows, width), BF),
            jax.ShapeDtypeStruct((1, width), F32),
            jax.ShapeDtypeStruct((gu.shape[1], wa_size * gu.shape[2]), BF),
            jax.ShapeDtypeStruct(dw.shape[1:], BF),
            jax.ShapeDtypeStruct((down.shape[0], ctx_size * down.shape[1]), F32),
        ),
        in_specs=[vmem] * 9,
        out_specs=[vmem] * 4 + [anywhere],
        scratch_shapes=scatter_scratch(ctx_size, rows, width)
        + [pltpu.VMEM(gu.shape, BF), pltpu.VMEM(dw.shape, BF)]
        + [pltpu.SemaphoreType.DMA((wa_size,))] * 4
        + [
            pltpu.VMEM((ctx_size,) + down.shape, BF),
            pltpu.VMEM((2,) + down.shape, F32),
            pltpu.SemaphoreType.DMA((2, 1)),
        ]
        + plane_sems(ctx_size),
        compiler_params=pltpu.CompilerParams(
            collective_id=3, has_side_effects=True, vmem_limit_bytes=VMEM_LIMIT
        ),
        cost_estimate=pl.CostEstimate(
            flops=2 * grads.size * width, bytes_accessed=250_000_000, transcendentals=0
        ),
        name="last_exchange",
    )(grads, w, dealt, x_own, gain, dh, gu, dw, down)


def final_kernel(
    ctx_size,
    wa_size,
    dw_ref,
    rows_ref,
    out_ref,
    gains_ref,
    d_gu_ref,
    d_qkv_ref,
    d_out_ref,
    sums_ref,
    *scratch,
):
    p = place_of(ctx_size, wa_size)
    dw_in, dw_send, dw_recv, share = scratch[:4]
    gus, gu_stage, gu_sems = scratch[4:7]
    qkvs, qkv_stage, qkv_sems = scratch[7:10]
    outs, out_stage, out_sems = scratch[10:13]
    wa_gains, ctx_gains, wa_send, wa_recv, ctx_send, ctx_recv = scratch[13:19]
    gu_plane, qkv_plane, out_plane = scratch[19:23], scratch[23:27], scratch[27:31]
    peers = [lax.rem(p.ctx + i, ctx_size) for i in range(1, ctx_size)]
    greet(peers, p.up[1:])
    small = [
        send(gains_ref, wa_gains.at[p.wa], wa_send.at[s], wa_recv.at[s], wa=p.up[s])
        for s in range(1, wa_size)
    ]
    copies = [
        send(dw_ref.at[p.up[s]], dw_in.at[s], dw_send.at[s], dw_recv.at[s], wa=p.up[s])
        for s in range(1, wa_size)
    ]

    def spread_of(own, slots, sems):
        half = slots.shape[1] // 2
        return Spread(
            p,
            own,
            lambda d: slots.at[d],
            lambda d, h: slots.at[d, pl.ds(h * half, half)],
            sems,
        )

    out_spread = spread_of(out_ref, outs, out_plane)
    gu_spread = spread_of(rows_ref, gus, gu_plane)
    out_spread.start()
    gu_spread.start()
    gu_stager = Stager(gu_stage, gu_sems, widen_rows(16))
    qkv_stager = Stager(qkv_stage, qkv_sems, widen_rows(16))
    out_stager = Stager(out_stage, out_sems, widen_rows(16))
    gu_rows = rows_ref.shape[0]
    head_columns = out_ref.shape[1]
    width = d_out_ref.shape[1]

    def put_gu(block, device):
        place = pl.ds(pl.multiple_of(device * gu_rows, gu_rows), gu_rows)
        gu_stager.put(block, [(d_gu_ref.at[place], None)])

    def put_columns(stager, block, target, device, count):
        places = []
        for part in range(count):
            first = pl.multiple_of(part * width + device * head_columns, head_columns)
            columns = pl.ds(part * head_columns, head_columns)
            places.append((target.at[:, pl.ds(first, head_columns)], columns))
        stager.put(block, places)

    put_gu(rows_ref, p.ctx)
    put_columns(out_stager, out_ref, d_out_ref, p.ctx, 1)
    for device in out_spread.arrivals():
        put_columns(out_stager, outs.at[device], d_out_ref, device, 1)
    wa_gains[p.wa] = gains_ref[...]
    for copy in small:
        copy.wait()
    plane_gain = wa_gains[0]
    for i in range(1, wa_size):
        plane_gain = plane_gain + wa_gains[i]
    ctx_gains[p.ctx] = plane_gain
    own_gain = ctx_gains.at[p.ctx]
    small = [
        send(own_gain, own_gain, ctx_send.at[i], ctx_recv.at[i], ctx=peer)
        for i, peer in enumerate(peers)
    ]
    for device in gu_spread.arrivals():
        put_gu(gus.at[device], device)
    share[...] = dw_ref[p.wa]
    for s in range(1, wa_size):
        copies[s - 1].wait_recv()
    step = 16

    def add_up(i, carried):
        place = pl.ds(pl.multiple_of(i * step, step), step)
        total = share[place, :].astype(F32)
        for s in range(1, wa_size):
            total = total + dw_in[s, place, :].astype(F32)
        share[place, :] = total.astype(BF)
        return carried

    lax.fori_loop(0, share.shape[0] // step, add_up, 0)
    qkv_spread = spread_of(share, qkvs, qkv_plane)
    qkv_spread.start()
    put_columns(qkv_stager, share, d_qkv_ref, p.ctx, 3)
    for device in qkv_spread.arrivals():
        put_columns(qkv_stager, qkvs.at[device], d_qkv_ref, device, 3)
    for copy in small:
        copy.wait()
    total_gain = ctx_gains[0]
    for i in range(1, ctx_size):
        total_gain = total_gain + ctx_gains[i]
    sums_ref[...] = total_gain
    for stager in (gu_stager, qkv_stager, out_stager):
        stager.finish()
    for spread in (out_spread, gu_spread, qkv_spread):
        spread.finish()
    for copy in copies:
        copy.wait_send()


def final_gather(dw, gu_rows, out_share, gains, ctx_size, wa_size):
    vmem = pl.BlockSpec(memory_space=pltpu.VMEM)
    anywhere = pl.BlockSpec(memory_space=pl.ANY)
    qkv_rows, qkv_columns = dw.shape[1:]
    out_rows, out_columns = out_share.shape
    rows, columns = gu_rows.shape

    def staged(shape, count):
        return [
            pltpu.VMEM((ctx_size,) + shape, BF),
            pltpu.VMEM((2,) + shape, F32),
            pltpu.SemaphoreType.DMA((2, count)),
        ]

    return pl.pallas_call(
        functools.partial(final_kernel, ctx_size, wa_size),
        out_shape=(
            jax.ShapeDtypeStruct((ctx_size * rows, columns), F32),
            jax.ShapeDtypeStruct((qkv_rows, ctx_size * qkv_columns), F32),
            jax.ShapeDtypeStruct((out_rows, ctx_size * out_columns), F32),
            jax.ShapeDtypeStruct(gains.shape, F32),
        ),
        in_specs=[vmem] * 4,
        out_specs=[anywhere] * 3 + [vmem],
        scratch_shapes=[pltpu.VMEM(dw.shape, BF)]
        + [pltpu.SemaphoreType.DMA((wa_size,))] * 2
        + [pltpu.VMEM((qkv_rows, qkv_columns), BF)]
        + staged((rows, columns), 1)
        + staged((qkv_rows, qkv_columns), 3)
        + staged((out_rows, out_columns), 1)
        + [
            pltpu.VMEM((wa_size,) + gains.shape, F32),
            pltpu.VMEM((ctx_size,) + gains.shape, F32),
        ]
        + [pltpu.SemaphoreType.DMA((wa_size,))] * 2
        + [pltpu.SemaphoreType.DMA((ctx_size,))] * 2
        + plane_sems(ctx_size) * 3,
        compiler_params=pltpu.CompilerParams(
            collective_id=4, has_side_effects=True, vmem_limit_bytes=VMEM_LIMIT
        ),
        cost_estimate=pl.CostEstimate(flops=0, bytes_accessed=300_000_000, transcendentals=0),
        name="final_gather",
    )(dw, gu_rows, out_share, gains)


def per_device(
    tokens, lengths, dealing, norm1_gain, w_qkv, w_out, norm2_gain, w_gate_up, w_down, grad_out
):
    tok_rows, width = tokens.shape[1], tokens.shape[2]
    ctx_size = lax.axis_size("ctx")
    wa_size = lax.axis_size("wa")
    ctx_index = lax.axis_index("ctx")
    wa_index = lax.axis_index("wa")
    block_order = dealing[0]
    block_total = block_order.shape[0]
    group_rows = block_total * BLOCK
    own_blocks = tok_rows // BLOCK
    first_length = lengths[0, 0]
    heads_own = HEADS // ctx_size
    head_cols = heads_own * HEAD
    wa_rows = width // wa_size
    ff_total = w_gate_up.shape[1] // 2
    ff_own = w_down.shape[0]
    piece_rows = wa_rows // ctx_size

    block_ids = jnp.arange(block_total, dtype=jnp.int32)
    inverse = jnp.sum(
        jnp.where(block_order[None, :] == block_ids[:, None], block_ids[None, :], 0), axis=1
    )

    def pick_blocks(values, order):
        parts = [
            lax.dynamic_slice_in_dim(values, order[i] * BLOCK, BLOCK) for i in range(block_total)
        ]
        return jnp.concatenate(parts, axis=0)

    qkv_slice = jnp.concatenate(
        [
            lax.dynamic_slice_in_dim(w_qkv, part * width + ctx_index * head_cols, head_cols, 1)
            for part in range(3)
        ],
        axis=1,
    )
    dealt, qkv_cols = gather_both(tokens[0], qkv_slice, ctx_size, wa_size)
    dealt = dealt.reshape(group_rows, width)
    qkv_cols = qkv_cols.reshape(width, 3 * head_cols)
    out_slice = lax.dynamic_slice_in_dim(w_out, ctx_index * head_cols, head_cols, 1)
    out_cols = gather_rows(out_slice, "wa")
    out_rows = lax.all_to_all(out_cols, "ctx", 0, 1, tiled=True)
    gu_piece = lax.dynamic_slice_in_dim(w_gate_up, ctx_index * piece_rows, piece_rows, 0)
    gu_send = jnp.stack(
        [
            jnp.concatenate(
                [
                    gu_piece[:, to * ff_own : (to + 1) * ff_own],
                    gu_piece[:, ff_total + to * ff_own : ff_total + (to + 1) * ff_own],
                ],
                axis=1,
            )
            for to in range(wa_size)
        ]
    )

    given_b = pick_blocks(dealt, inverse)
    given = given_b.astype(F32)
    positions = jnp.arange(group_rows, dtype=jnp.int32)
    segments = (positions >= first_length).astype(jnp.int32)
    cosine, sine = rotary_tables(positions - segments * first_length)
    normed_one = given * rms_scale(given)
    act_one = (normed_one * norm1_gain).astype(BF)

    projected = dot_plain(act_one, qkv_cols)
    parts = [
        projected[:, i * head_cols : (i + 1) * head_cols].reshape(group_rows, heads_own, HEAD)
        for i in range(3)
    ]
    query_b = rotate(parts[0], cosine, sine).astype(BF)
    key_b = rotate(parts[1], cosine, sine).astype(BF)
    value_b = parts[2].astype(BF)
    score_scale = math.sqrt(HEAD)
    distance = positions[:, None] - positions[None, :]
    allowed = (segments[:, None] == segments[None, :]) & (distance >= 0) & (distance < WINDOW)
    scores = jnp.einsum("qhe,khe->hqk", query_b, key_b, preferred_element_type=F32) / score_scale
    scores = jnp.where(allowed[None], scores, -jnp.inf)
    largest = jnp.max(scores, axis=2, keepdims=True)
    weights = jnp.exp(scores - largest)
    probs = weights / jnp.sum(weights, axis=2, keepdims=True)
    probs_b = probs.astype(BF)
    mixed = jnp.einsum("hqk,khe->qhe", probs_b, value_b, preferred_element_type=F32)
    mixed_b = mixed.reshape(group_rows, head_cols).astype(BF)

    own_given = lax.dynamic_slice_in_dim(given_b, ctx_index * tok_rows, tok_rows)
    gain_two = norm2_gain[None, :]
    hidden, acts, gu_weight = out_project(
        mixed_b, out_rows, own_given, gain_two, gu_send, ctx_size, wa_size
    )
    gu_weight = gu_weight.reshape(width, 2 * ff_own)
    act_two = acts.reshape(wa_size * tok_rows, width)
    early = lax.optimization_barrier((grad_out[0], qkv_cols))[0]
    grads_all = lax.all_gather(early, "wa", axis=0)
    cotangent = jnp.concatenate(
        [take(grads_all, (wa_index - s) % wa_size) for s in range(wa_size)], axis=0
    )

    gate_up = dot_plain(act_two, gu_weight)
    gate_part = gate_up[:, :ff_own]
    up_part = gate_up[:, ff_own:]
    sigmoid_gate = jax.nn.sigmoid(gate_part)
    silu_gate = gate_part * sigmoid_gate
    inner_b = (silu_gate * up_part).astype(BF)

    d_inner = dot_right_t(cotangent, w_down)
    d_gate = d_inner * up_part * sigmoid_gate * (1.0 + gate_part * (1.0 - sigmoid_gate))
    d_gu_b = jnp.concatenate([d_gate, d_inner * silu_gate], axis=1).astype(BF)
    d_act = dot_right_t(d_gu_b, gu_weight).astype(BF).reshape(wa_size, tok_rows, width)
    mlp_parts = dot_plain(inner_b, w_down).astype(BF).reshape(wa_size, tok_rows, width)
    down_part = dot_left_t(inner_b, cotangent).astype(BF)
    gu_part = dot_left_t(act_two, d_gu_b).astype(BF)
    gu_part = gu_part.reshape(wa_size, ctx_size // 2, 2, piece_rows, 2 * ff_own)
    d_branches, gain_two_part, out_given, gu_piece_grad, down_piece_grad = turn(
        d_act, mlp_parts, hidden, gain_two, grad_out[0], gu_part, down_part, ctx_size, wa_size
    )
    d_branch_b = d_branches.reshape(group_rows, width)
    grad_mixed_b = dot_right_t(d_branch_b, out_rows).astype(BF)
    d_out_part = dot_left_t(mixed_b, d_branch_b).astype(BF)
    d_out_cols = lax.all_to_all(d_out_part, "ctx", 1, 0, tiled=True)
    out_parts = d_out_cols.reshape(wa_size, wa_rows, head_cols)

    grad_heads = grad_mixed_b.reshape(group_rows, heads_own, HEAD)
    d_probs = jnp.einsum("qhe,khe->hqk", grad_heads, value_b, preferred_element_type=F32)
    row_dot = jnp.sum(probs * d_probs, axis=2, keepdims=True)
    d_scores = (probs * (d_probs - row_dot)).astype(BF)
    d_query = jnp.einsum("hqk,khe->qhe", d_scores, key_b, preferred_element_type=F32) / score_scale
    d_key = jnp.einsum("hqk,qhe->khe", d_scores, query_b, preferred_element_type=F32) / score_scale
    d_value = jnp.einsum("hqk,qhe->khe", probs_b, grad_heads, preferred_element_type=F32)
    d_qkv_b = jnp.concatenate(
        [
            rotate(d_query, cosine, -sine).reshape(group_rows, head_cols),
            rotate(d_key, cosine, -sine).reshape(group_rows, head_cols),
            d_value.reshape(group_rows, head_cols),
        ],
        axis=1,
    ).astype(BF)
    qkv_parts = dot_left_t(act_one, d_qkv_b).astype(BF).reshape(wa_size, wa_rows, 3 * head_cols)
    own_order = lax.dynamic_slice_in_dim(block_order, ctx_index * own_blocks, own_blocks)
    d_hidden_dealt = jnp.concatenate(
        [
            lax.dynamic_slice_in_dim(d_branch_b, own_order[i] * BLOCK, BLOCK)
            for i in range(own_blocks)
        ],
        axis=0,
    )
    d_tokens, gain_one_part, d_gu_rows, d_out_share, d_down = last_exchange(
        pick_blocks(d_qkv_b, block_order),
        qkv_cols,
        dealt,
        tokens[0],
        norm1_gain[None, :],
        d_hidden_dealt,
        gu_piece_grad,
        out_parts,
        down_piece_grad,
        ctx_size,
        wa_size,
    )
    gain_parts = jnp.concatenate([gain_one_part, gain_two_part], axis=0)
    d_gate_up, d_qkv, d_out, gain_sums = final_gather(
        qkv_parts, d_gu_rows, d_out_share, gain_parts, ctx_size, wa_size
    )
    return (
        out_given[None],
        d_tokens[None],
        gain_sums[0],
        d_qkv,
        d_out,
        gain_sums[1],
        d_gate_up,
        d_down,
    )


def solution(mesh):
    in_specs = (
        P("wa", "ctx", None),
        P("wa", None),
        P("wa", None),
        P(),
        P("wa", None),
        P("wa", None),
        P(),
        P("wa", None),
        P("wa", None),
        P("wa", "ctx", None),
    )
    out_specs = (
        P("wa", "ctx", None),
        P("wa", "ctx", None),
        P(),
        P("wa", None),
        P("wa", None),
        P(),
        P("wa", None),
        P("wa", None),
    )
    return jax.shard_map(
        per_device, mesh=mesh, in_specs=in_specs, out_specs=out_specs, check_vma=False
    )
```

```python
import functools
import math
import types

import jax
import jax.numpy as jnp
from jax import lax
from jax.experimental import pallas as pl
from jax.experimental.pallas import tpu as pltpu
from jax.sharding import PartitionSpec as P

HEADS = 16
HEAD = 128
WINDOW = 2048
BLOCK = 128

EPSILON = 1e-06
BF = jnp.bfloat16
F32 = jnp.float32
VMEM_LIMIT = 60 * 1024 * 1024
ATTEND_ROWS = 256
CHUNK = 256


def dot_left_t(left, right):
    return lax.dot_general(left, right, (((0,), (0,)), ((), ())), preferred_element_type=F32)


def rotary_tables(seq_pos):
    half_width = HEAD // 2
    inverse_freq = jnp.power(10000.0, -2.0 * jnp.arange(half_width, dtype=F32) / HEAD)
    angles = seq_pos.astype(F32)[:, None] * inverse_freq[None, :]
    cosine, sine = jnp.cos(angles), jnp.sin(angles)
    return (
        jnp.concatenate([cosine, cosine], axis=-1),
        jnp.concatenate([-sine, sine], axis=-1),
    )


def gather_rows(values, axis):
    return lax.all_gather(values, axis, axis=0, tiled=True)


def take(values, index):
    return lax.dynamic_index_in_dim(values, index, 0, keepdims=False)


MESH = pl.DeviceIdType.MESH


def greet(ctx_peers, wa_peers):
    barrier = pltpu.get_barrier_semaphore()
    for peer in ctx_peers:
        pl.semaphore_signal(barrier, inc=1, device_id={"ctx": peer}, device_id_type=MESH)
    for peer in wa_peers:
        pl.semaphore_signal(barrier, inc=1, device_id={"wa": peer}, device_id_type=MESH)
    pl.semaphore_wait(barrier, len(ctx_peers) + len(wa_peers))


def send(source, target, send_sem, recv_sem, **peer):
    copy = pltpu.make_async_remote_copy(
        src_ref=source,
        dst_ref=target,
        send_sem=send_sem,
        recv_sem=recv_sem,
        device_id=peer,
        device_id_type=MESH,
    )
    copy.start()
    return copy


def place_of(ctx_size, wa_size):
    chips = ctx_size // 2
    p = types.SimpleNamespace(ctx_size=ctx_size, wa_size=wa_size, chips=chips)
    p.ctx, p.wa = lax.axis_index("ctx"), lax.axis_index("wa")
    p.core, p.chip = lax.rem(p.ctx, 2), lax.div(p.ctx, 2)
    p.beside = p.chip * 2 + 1 - p.core
    p.ahead = [lax.rem(p.chip + m, chips) * 2 + p.core for m in range(chips)]
    p.behind = [lax.rem(p.chip + chips - m, chips) * 2 + p.core for m in range(chips)]
    p.up = [lax.rem(p.wa + s, wa_size) for s in range(wa_size)]
    p.down = [lax.rem(p.wa + wa_size - s, wa_size) for s in range(wa_size)]
    p.square = chips == 4
    if p.square:
        p.near = [p.chip + 1 - 2 * lax.rem(p.chip, 2), lax.rem(p.chip + 2, 4)]
        p.far = 3 - p.chip
    return p


def on_core(p, chip):
    return chip * 2 + p.core


def off_core(p, chip):
    return chip * 2 + 1 - p.core


def plane_sems(ctx_size):
    count = max(ctx_size // 2, 5)
    return [pltpu.SemaphoreType.DMA((count,))] * 4


class Spread:
    def __init__(self, p, own, slot, half, sems):
        self.p, self.own, self.slot, self.half = p, own, slot, half
        self.chip_send, self.chip_recv, self.side_send, self.side_recv = sems
        self.chip, self.side = [], []

    def across(self, source, target, chip):
        i = len(self.chip)
        self.chip.append(
            send(source, target, self.chip_send.at[i], self.chip_recv.at[i], ctx=on_core(self.p, chip))
        )

    def aside(self, source, target):
        i = len(self.side)
        self.side.append(
            send(source, target, self.side_send.at[i], self.side_recv.at[i], ctx=self.p.beside)
        )

    def start(self):
        p = self.p
        target = self.slot(p.ctx)
        if p.square:
            for chip in p.near:
                self.across(self.own, target, chip)
        else:
            for m in range(1, p.chips):
                self.across(self.own, target, lax.rem(p.chip + m, p.chips))
        self.aside(self.own, target)

    def arrivals(self):
        p = self.p
        if not p.square:
            for m in range(1, p.chips):
                self.chip[m - 1].wait_recv()
                block = self.slot(p.behind[m])
                self.aside(block, block)
                yield p.behind[m]
            self.side[0].wait_recv()
            yield p.beside
            for m in range(1, p.chips):
                self.side[m].wait_recv()
                yield off_core(p, lax.rem(p.chip + p.chips - m, p.chips))
            return
        for i in range(2):
            self.chip[i].wait_recv()
            device = on_core(p, p.near[i])
            part = self.half(device, i)
            self.across(part, part, p.near[1 - i])
            self.aside(self.slot(device), self.slot(device))
            yield device
        self.side[0].wait_recv()
        yield p.beside
        for i in range(2):
            self.side[1 + i].wait_recv()
            yield off_core(p, p.near[i])
        device = on_core(p, p.far)
        for i in range(2):
            self.chip[2 + i].wait_recv()
            part = self.half(device, i)
            self.aside(part, part)
        yield device
        for i in range(2):
            self.side[3 + i].wait_recv()
        yield off_core(p, p.far)

    def finish(self):
        for copy in self.chip + self.side:
            copy.wait_send()


class Fold:
    def __init__(self, p, both, got, near, sent, piece, half, add, sems):
        self.p, self.both, self.got, self.near, self.sent = p, both, got, near, sent
        self.kept = both.at[p.core]
        self.piece, self.half, self.add = piece, half, add
        self.chip_send, self.chip_recv, self.side_send, self.side_recv = sems
        self.chip, self.side = [], []
        if p.square:
            self.order = [p.far] + p.near + [p.chip]
        else:
            self.order = [lax.rem(p.chip + m, p.chips) for m in range(1, p.chips)] + [p.chip]

    def across(self, source, target, chip):
        i = len(self.chip)
        self.chip.append(
            send(source, target, self.chip_send.at[i], self.chip_recv.at[i], ctx=on_core(self.p, chip))
        )

    def start(self, i):
        p = self.p
        chip = self.order[i]
        self.side.append(
            send(
                self.piece(self.both.at[1 - p.core], chip),
                self.piece(self.got, chip),
                self.side_send.at[i],
                self.side_recv.at[i],
                ctx=p.beside,
            )
        )

    def between(self, i):
        p = self.p
        chip = self.order[i]
        self.side[i].wait_recv()
        self.add(self.piece(self.kept, chip), self.piece(self.got, chip))
        if i == p.chips - 1:
            return
        if not p.square:
            self.across(self.piece(self.kept, chip), self.sent.at[i], chip)
        elif i == 0:
            for j in range(2):
                self.across(self.half(self.kept, chip, j), self.near.at[j], p.near[j])
        else:
            j = i - 1
            self.across(self.half(self.kept, chip, j), self.half(self.sent.at[j], None, j), chip)

    def onward(self):
        p = self.p
        if not p.square:
            return
        for i in range(2):
            self.chip[i].wait_recv()
            part = self.half(self.kept, p.near[1 - i], i)
            self.add(part, self.near.at[i])
            self.across(part, self.half(self.sent.at[1 - i], None, i), p.near[1 - i])

    def total(self):
        p = self.p
        for copy in self.chip[2:] if p.square else self.chip:
            copy.wait_recv()
        mine = self.piece(self.kept, p.chip)
        for i in range(2 if p.square else p.chips - 1):
            self.add(mine, self.sent.at[i])
        return mine

    def finish(self):
        for copy in self.side + self.chip:
            copy.wait_send()


def add_rows(into, other, step):
    def one(i, carried):
        place = pl.ds(pl.multiple_of(i * step, step), step)
        into[place, :] = (into[place, :].astype(F32) + other[place, :].astype(F32)).astype(BF)
        return carried

    lax.fori_loop(0, into.shape[0] // step, one, 0)


def add_blocks(into, other):
    lead = into.shape[:-2]

    def one(i, carried):
        at = (i,) if len(lead) == 1 else (i // lead[1], i % lead[1])
        into[at] = (into[at].astype(F32) + other[at].astype(F32)).astype(BF)
        return carried

    lax.fori_loop(0, math.prod(lead), one, 0)


class Scatter:
    def __init__(self, p, part_of, refs):
        self.p, self.part_of, self.refs = p, part_of, refs

    def start(self):
        p = self.p
        side_out, side_in, chip_out, chip_in, side_send, side_recv, chip_send, chip_recv = self.refs
        self.side, self.out = [], []
        order = list(range(1, p.chips)) + [0]
        for m in order:
            side_out[m] = self.part_of(lax.div(p.ahead[m], 2) * 2 + 1 - p.core).astype(BF)
            self.side.append(
                send(side_out.at[m], side_in.at[m], side_send.at[m], side_recv.at[m], ctx=p.beside)
            )
        for i, m in enumerate(order):
            mine = self.part_of(p.ahead[m])
            self.side[i].wait_recv()
            self.kept = mine + side_in[m].astype(F32)
            if m > 0:
                chip_out[m - 1] = self.kept.astype(BF)
                self.out.append(
                    send(
                        chip_out.at[m - 1],
                        chip_in.at[m - 1],
                        chip_send.at[m - 1],
                        chip_recv.at[m - 1],
                        ctx=p.ahead[m],
                    )
                )

    def total(self):
        chip_in = self.refs[3]
        total = self.kept
        for m in range(1, self.p.chips):
            self.out[m - 1].wait_recv()
            total = total + chip_in[m - 1].astype(F32)
        return total

    def finish(self):
        for copy in self.side + self.out:
            copy.wait_send()


def scatter_scratch(ctx_size, rows, width):
    chips = ctx_size // 2
    return [
        pltpu.VMEM((chips, rows, width), BF),
        pltpu.VMEM((chips, rows, width), BF),
        pltpu.VMEM((chips - 1, rows, width), BF),
        pltpu.VMEM((chips - 1, rows, width), BF),
    ] + [pltpu.SemaphoreType.DMA((chips,))] * 4


def norm_back(x, scale, gain, d_scaled, d_other):
    normed = x * scale
    scaled = d_scaled * gain
    return d_other + scale * (
        scaled - normed * jnp.mean(scaled * normed, axis=-1, keepdims=True)
    )


def gather_kernel(ctx_size, wa_size, cuts, x_ref, w_ref, xs_ref, ws_ref, *sems):
    p = place_of(ctx_size, wa_size)
    ring_send, ring_recv, local = sems[4:]
    greet([p.beside] + p.ahead[1:], [p.up[1], p.down[1]])
    rows = w_ref.shape[0] // cuts
    half_rows = x_ref.shape[0] // 2
    ring = []
    for i in range(cuts):
        part = pl.ds(i * rows, rows)
        ring.append(
            send(
                w_ref.at[part],
                ws_ref.at[p.wa, part],
                ring_send.at[0, i],
                ring_recv.at[0, i],
                wa=p.up[1],
            )
        )
    spread = Spread(
        p,
        x_ref,
        lambda d: xs_ref.at[d],
        lambda d, h: xs_ref.at[d, pl.ds(h * half_rows, half_rows)],
        sems[:4],
    )
    spread.start()
    own_x = pltpu.make_async_copy(x_ref, xs_ref.at[p.ctx], local.at[0])
    own_w = pltpu.make_async_copy(w_ref, ws_ref.at[p.wa], local.at[1])
    own_x.start()
    own_w.start()
    late = []
    for step in range(1, wa_size):
        for i in range(cuts):
            ring[i].wait_recv()
            late.append(ring[i])
            if step < wa_size - 1:
                block = ws_ref.at[p.down[step], pl.ds(i * rows, rows)]
                ring[i] = send(
                    block, block, ring_send.at[step, i], ring_recv.at[step, i], wa=p.up[1]
                )
        if step == 1:
            for _ in spread.arrivals():
                pass
    for copy in late:
        copy.wait_send()
    spread.finish()
    own_x.wait()
    own_w.wait()


def gather_both(x, w, ctx_size, wa_size, cuts=4):
    anywhere = pl.BlockSpec(memory_space=pl.ANY)
    return pl.pallas_call(
        functools.partial(gather_kernel, ctx_size, wa_size, cuts),
        out_shape=(
            jax.ShapeDtypeStruct((ctx_size,) + x.shape, x.dtype),
            jax.ShapeDtypeStruct((wa_size,) + w.shape, w.dtype),
        ),
        in_specs=[anywhere] * 2,
        out_specs=[anywhere] * 2,
        scratch_shapes=plane_sems(ctx_size)
        + [pltpu.SemaphoreType.DMA((wa_size - 1, cuts))] * 2
        + [pltpu.SemaphoreType.DMA((2,))],
        compiler_params=pltpu.CompilerParams(collective_id=0, has_side_effects=True),
        cost_estimate=pl.CostEstimate(flops=0, bytes_accessed=200_000_000, transcendentals=0),
        name="gather_both",
    )(x, w)


def exchange_plane(peers, source, target, send_sem, recv_sem):
    here = target(peers[0])
    return [
        send(source(peer), here, send_sem.at[i], recv_sem.at[i], ctx=peer)
        for i, peer in enumerate(peers)
        if i > 0
    ]


def arrange_kernel(own_blocks, order_ref, first_ref, x_ref, gain_ref, act_ref, own_ref):
    x = x_ref[...]
    wide = x.astype(F32)
    scale = lax.rsqrt(jnp.mean(wide * wide, axis=-1, keepdims=True) + EPSILON)
    act_ref[...] = (wide * scale * gain_ref[...]).astype(BF)
    at = pl.program_id(0) - first_ref[0]

    @pl.when((at >= 0) & (at < own_blocks))
    def _():
        own_ref[...] = x


def arrange(order, first, dealt, gain, own_blocks):
    rows, width = dealt.shape
    block = (BLOCK, width)

    def own_place(i, order_ref, first_ref):
        return (jnp.clip(i - first_ref[0], 0, own_blocks - 1), 0)

    return pl.pallas_call(
        functools.partial(arrange_kernel, own_blocks),
        out_shape=(
            jax.ShapeDtypeStruct((rows, width), BF),
            jax.ShapeDtypeStruct((own_blocks * BLOCK, width), BF),
        ),
        grid_spec=pltpu.PrefetchScalarGridSpec(
            num_scalar_prefetch=2,
            grid=(rows // BLOCK,),
            in_specs=[
                pl.BlockSpec(block, lambda i, order_ref, first_ref: (order_ref[i], 0)),
                pl.BlockSpec((1, width), lambda i, order_ref, first_ref: (0, 0)),
            ],
            out_specs=[
                pl.BlockSpec(block, lambda i, order_ref, first_ref: (i, 0)),
                pl.BlockSpec(block, own_place),
            ],
        ),
        name="arrange",
    )(order, first, dealt, gain)


def attend_kernel(
    ctx_size,
    wa_size,
    heads,
    row_seg_ref,
    column_seg_ref,
    act_ref,
    w_ref,
    cos_ref,
    sin_ref,
    gu_ref,
    cols_ref,
    q_ref,
    k_ref,
    v_ref,
    o_ref,
    prob_ref,
    gw_ref,
    rows_ref,
    gu_send,
    gu_recv,
    local,
    out_send,
    out_recv,
):
    wa, ctx = lax.axis_index("wa"), lax.axis_index("ctx")
    up = [lax.rem(wa + s, wa_size) for s in range(wa_size)]
    peers = [lax.rem(ctx + i, ctx_size) for i in range(ctx_size)]
    greet(peers[1:], up[1:])
    deal_out = exchange_plane(
        peers,
        lambda d: cols_ref.at[d],
        lambda d: rows_ref.at[:, pl.ds(pl.multiple_of(d * cols_ref.shape[2], 128), cols_ref.shape[2])],
        out_send,
        out_recv,
    )
    own_out = pltpu.make_async_copy(
        cols_ref.at[ctx],
        rows_ref.at[:, pl.ds(pl.multiple_of(ctx * cols_ref.shape[2], 128), cols_ref.shape[2])],
        local.at[1],
    )
    own_out.start()
    deal = [
        send(gu_ref.at[up[s]], gw_ref.at[:, wa], gu_send.at[s], gu_recv.at[s], wa=up[s])
        for s in range(1, wa_size)
    ]
    own = pltpu.make_async_copy(gu_ref.at[wa], gw_ref.at[:, wa], local.at[0])
    own.start()
    rows = act_ref.shape[0]
    step = ATTEND_ROWS
    head_cols = heads * HEAD

    def project(i, carried):
        place = pl.ds(pl.multiple_of(i * step, step), step)
        made = jnp.dot(act_ref[place, :], w_ref[...], preferred_element_type=F32)
        cosine, sine = cos_ref[place, :], sin_ref[place, :]
        for head in range(heads):
            columns = slice(head * HEAD, (head + 1) * HEAD)
            for part, target in ((0, q_ref), (1, k_ref)):
                first = part * head_cols + head * HEAD
                u = made[:, first : first + HEAD]
                turned = u * cosine + pltpu.roll(u, HEAD // 2, 1) * sine
                target[place, columns] = turned.astype(BF)
        v_ref[place, :] = made[:, 2 * head_cols :].astype(BF)
        return carried

    lax.fori_loop(0, rows // step, project, 0)
    for i in range(rows // step):
        here = slice(i * step, (i + 1) * step)
        keys = (i + 1) * step
        row = lax.broadcasted_iota(jnp.int32, (step, keys), 0) + i * step
        column = lax.broadcasted_iota(jnp.int32, (step, keys), 1)
        allowed = (column <= row) & (row_seg_ref[here, :] == column_seg_ref[:, :keys])
        if rows > WINDOW:
            allowed = allowed & (row - column < WINDOW)
        for head in range(heads):
            columns = slice(head * HEAD, (head + 1) * HEAD)
            scores = lax.dot_general(
                q_ref[here, columns],
                k_ref[:keys, columns],
                (((1,), (1,)), ((), ())),
                preferred_element_type=F32,
            )
            scores = jnp.where(allowed, scores * (1.0 / math.sqrt(HEAD)), -1e30)
            largest = jnp.max(scores, axis=-1, keepdims=True)
            weights = jnp.exp(scores - largest)
            total = jnp.sum(weights, axis=-1, keepdims=True)
            probs = (weights * (1.0 / total)).astype(BF)
            prob_ref[head, here, :keys] = probs
            o_ref[here, columns] = jnp.dot(
                probs, v_ref[:keys, columns], preferred_element_type=F32
            ).astype(BF)
    own.wait()
    own_out.wait()
    for copy in deal + deal_out:
        copy.wait()


def attend(segments, act, w, cosine, sine, gu, out_cols, ctx_size, wa_size):
    rows, width = act.shape
    head_cols = w.shape[1] // 3
    heads = head_cols // HEAD
    vmem = pl.BlockSpec(memory_space=pltpu.VMEM)
    anywhere = pl.BlockSpec(memory_space=pl.ANY)
    heads_shape = jax.ShapeDtypeStruct((rows, head_cols), BF)
    return pl.pallas_call(
        functools.partial(attend_kernel, ctx_size, wa_size, heads),
        out_shape=(
            heads_shape,
            heads_shape,
            heads_shape,
            heads_shape,
            jax.ShapeDtypeStruct((heads, rows, rows), BF),
            jax.ShapeDtypeStruct((2, wa_size) + gu.shape[2:], BF),
            jax.ShapeDtypeStruct((out_cols.shape[1], width), BF),
        ),
        in_specs=[vmem] * 6 + [anywhere] * 2,
        out_specs=[vmem] * 5 + [anywhere] * 2,
        scratch_shapes=[pltpu.SemaphoreType.DMA((wa_size,))] * 3
        + [pltpu.SemaphoreType.DMA((ctx_size,))] * 2,
        compiler_params=pltpu.CompilerParams(
            collective_id=4, has_side_effects=True, vmem_limit_bytes=VMEM_LIMIT
        ),
        cost_estimate=pl.CostEstimate(
            flops=2 * rows * width * 3 * head_cols, bytes_accessed=100_000_000, transcendentals=0
        ),
        name="attend",
    )(segments[:, None], segments[None, :], act, w, cosine, sine, gu, out_cols)


def attend_back_kernel(
    heads,
    place_ref,
    own_ref,
    dy_ref,
    w_ref,
    o_ref,
    q_ref,
    k_ref,
    v_ref,
    prob_ref,
    cos_ref,
    sin_ref,
    grads_ref,
    dealt_ref,
    d_out_ref,
    dh_ref,
    do_ref,
    dk_ref,
    dv_ref,
):
    rows = dy_ref.shape[0]
    step = ATTEND_ROWS
    head_cols = heads * HEAD
    back_scale = 1.0 / math.sqrt(HEAD)

    def project(i, carried):
        place = pl.ds(pl.multiple_of(i * step, step), step)
        do_ref[place, :] = lax.dot_general(
            dy_ref[place, :],
            w_ref[...],
            (((1,), (1,)), ((), ())),
            preferred_element_type=F32,
        ).astype(BF)
        return carried

    lax.fori_loop(0, rows // step, project, 0)
    dk_ref[...] = jnp.zeros_like(dk_ref)
    dv_ref[...] = jnp.zeros_like(dv_ref)

    def unrotate(u, place):
        return u * cos_ref[place, :] - pltpu.roll(u, HEAD // 2, 1) * sin_ref[place, :]

    for i in range(rows // step):
        here = slice(i * step, (i + 1) * step)
        keys = (i + 1) * step
        for head in range(heads):
            columns = slice(head * HEAD, (head + 1) * HEAD)
            d_o = do_ref[here, columns]
            q = q_ref[here, columns]
            probs = prob_ref[head, here, :keys]
            d_probs = lax.dot_general(
                d_o,
                v_ref[:keys, columns],
                (((1,), (1,)), ((), ())),
                preferred_element_type=F32,
            )
            wide = probs.astype(F32)
            row_dot = jnp.sum(wide * d_probs, axis=-1, keepdims=True)
            d_scores = (wide * (d_probs - row_dot)).astype(BF)
            d_query = jnp.dot(d_scores, k_ref[:keys, columns], preferred_element_type=F32)
            grads_ref[here, columns] = unrotate(d_query * back_scale, here).astype(BF)
            dk_ref[:keys, columns] += lax.dot_general(
                d_scores, q, (((0,), (0,)), ((), ())), preferred_element_type=F32
            )
            dv_ref[:keys, columns] += lax.dot_general(
                probs, d_o, (((0,), (0,)), ((), ())), preferred_element_type=F32
            )
    for i in range(rows // BLOCK):
        here = slice(i * BLOCK, (i + 1) * BLOCK)
        for head in range(heads):
            columns = slice(head * HEAD, (head + 1) * HEAD)
            d_key = unrotate(dk_ref[here, columns] * back_scale, here)
            grads_ref[here, head_cols + head * HEAD : head_cols + (head + 1) * HEAD] = d_key.astype(BF)
        grads_ref[here, 2 * head_cols :] = dv_ref[here, :].astype(BF)
        there = pl.ds(pl.multiple_of(place_ref[i] * BLOCK, BLOCK), BLOCK)
        dealt_ref[there, :] = grads_ref[here, :]
    for j in range(dh_ref.shape[0] // BLOCK):
        at = pl.ds(pl.multiple_of(own_ref[j] * BLOCK, BLOCK), BLOCK)
        dh_ref[j * BLOCK : (j + 1) * BLOCK, :] = dy_ref[at, :]
    d_out_ref[...] = lax.dot_general(
        o_ref[...], dy_ref[...], (((0,), (0,)), ((), ())), preferred_element_type=F32
    ).astype(BF)


def attend_back(place, own, dy, w_rows, o, q, k, v, probs, cosine, sine):
    rows, width = dy.shape
    head_cols = o.shape[1]
    heads = head_cols // HEAD
    vmem = pl.BlockSpec(memory_space=pltpu.VMEM)
    grads_shape = jax.ShapeDtypeStruct((rows, 3 * head_cols), BF)
    return pl.pallas_call(
        functools.partial(attend_back_kernel, heads),
        out_shape=(
            grads_shape,
            grads_shape,
            jax.ShapeDtypeStruct((head_cols, width), BF),
            jax.ShapeDtypeStruct((own.shape[0] * BLOCK, width), BF),
        ),
        in_specs=[pl.BlockSpec(memory_space=pltpu.SMEM)] * 2 + [vmem] * 9,
        out_specs=[vmem] * 4,
        scratch_shapes=[
            pltpu.VMEM((rows, head_cols), BF),
            pltpu.VMEM((rows, head_cols), F32),
            pltpu.VMEM((rows, head_cols), F32),
        ],
        compiler_params=pltpu.CompilerParams(vmem_limit_bytes=VMEM_LIMIT),
        cost_estimate=pl.CostEstimate(
            flops=4 * rows * width * head_cols, bytes_accessed=20_000_000, transcendentals=0
        ),
        name="attend_back",
    )(place, own, dy, w_rows, o, q, k, v, probs, cosine, sine)


def out_kernel(
    ctx_size,
    wa_size,
    mixed_ref,
    w_ref,
    x_ref,
    gain_ref,
    gu_ref,
    hidden_ref,
    acts_ref,
    gw_ref,
    *scratch,
):
    p = place_of(ctx_size, wa_size)
    act_send, act_recv, local = scratch[12:]
    greet([p.beside] + p.ahead[1:], [p.up[1], p.down[1]])
    own = pltpu.make_async_copy(gu_ref, gw_ref.at[:, :, p.ctx], local.at[0])
    own.start()
    spread = Spread(
        p,
        gu_ref,
        lambda d: gw_ref.at[:, :, d],
        lambda d, h: gw_ref.at[h, :, d],
        scratch[8:12],
    )
    rows = x_ref.shape[0]

    def part_of(device):
        block = mixed_ref[pl.ds(pl.multiple_of(device * rows, rows), rows), :]
        return jnp.dot(block, w_ref[...], preferred_element_type=F32)

    scatter = Scatter(p, part_of, scratch[:8])
    scatter.start()
    hidden = x_ref[...].astype(F32) + scatter.total()
    hidden_ref[...] = hidden
    scale = lax.rsqrt(jnp.mean(hidden * hidden, axis=-1, keepdims=True) + EPSILON)
    acts_ref[0] = (hidden * scale * gain_ref[...]).astype(BF)
    half_rows = rows // 2

    def pass_on(s, i):
        place = pl.ds(i * half_rows, half_rows)
        return send(
            acts_ref.at[s, place],
            acts_ref.at[s + 1, place],
            act_send.at[s, i],
            act_recv.at[s, i],
            wa=p.up[1],
        )

    ring = [pass_on(0, 0), pass_on(0, 1)]
    spread.start()
    arrivals = spread.arrivals()
    for s in range(1, wa_size):
        for i in range(2):
            ring[2 * (s - 1) + i].wait_recv()
            if s < wa_size - 1:
                ring.append(pass_on(s, i))
        if s == 2:
            next(arrivals)
            next(arrivals)
    for _ in arrivals:
        pass
    scatter.finish()
    spread.finish()
    own.wait()
    for copy in ring:
        copy.wait_send()


def out_project(mixed, w_rows, x_own, gain, gu, ctx_size, wa_size):
    rows, width = x_own.shape
    vmem = pl.BlockSpec(memory_space=pltpu.VMEM)
    anywhere = pl.BlockSpec(memory_space=pl.ANY)
    return pl.pallas_call(
        functools.partial(out_kernel, ctx_size, wa_size),
        out_shape=(
            jax.ShapeDtypeStruct((rows, width), F32),
            jax.ShapeDtypeStruct((wa_size, rows, width), BF),
            jax.ShapeDtypeStruct((2, wa_size, ctx_size) + gu.shape[2:], BF),
        ),
        in_specs=[vmem] * 4 + [anywhere],
        out_specs=[vmem] * 2 + [anywhere],
        scratch_shapes=scatter_scratch(ctx_size, rows, width)
        + plane_sems(ctx_size)
        + [pltpu.SemaphoreType.DMA((wa_size, 2))] * 2
        + [pltpu.SemaphoreType.DMA((1,))],
        compiler_params=pltpu.CompilerParams(
            collective_id=1, has_side_effects=True, vmem_limit_bytes=VMEM_LIMIT
        ),
        cost_estimate=pl.CostEstimate(
            flops=2 * mixed.size * width, bytes_accessed=200_000_000, transcendentals=0
        ),
        name="out_project",
    )(mixed, w_rows, x_own, gain, gu)


def mlp_kernel(
    act_ref,
    dz_ref,
    gw_any,
    wd_any,
    d_act_ref,
    mlp_ref,
    act_t_ref,
    d_gu_ref,
    inner_t_ref,
    gw_ref,
    wd_ref,
    inner_ref,
    sems,
):
    hidden_rows = wd_any.shape[0]
    hidden = inner_ref.shape[1]
    width = act_ref.shape[1]
    loads = [
        pltpu.make_async_copy(gw_any.at[0], gw_ref.at[0], sems.at[0]),
        pltpu.make_async_copy(gw_any.at[1], gw_ref.at[1], sems.at[1]),
        pltpu.make_async_copy(wd_any, wd_ref.at[pl.ds(0, hidden_rows)], sems.at[2]),
    ]
    for copy in loads:
        copy.start()
    if hidden > hidden_rows:
        wd_ref[hidden_rows:, :] = jnp.zeros((hidden - hidden_rows, width), BF)
    act_t_ref[...] = act_ref[...].T
    for copy in loads:
        copy.wait()
    act = act_ref[...]
    dz = dz_ref[...]

    def part(first, size):
        columns = pl.ds(first, size)
        gate = jnp.dot(act, gw_ref[0, :, columns], preferred_element_type=F32)
        up = jnp.dot(act, gw_ref[1, :, columns], preferred_element_type=F32)
        d_inner = lax.dot_general(
            dz, wd_ref[columns, :], (((1,), (1,)), ((), ())), preferred_element_type=F32
        )
        sigmoid = 1.0 / (1.0 + jnp.exp(-gate))
        silu = gate * sigmoid
        inner = (silu * up).astype(BF)
        inner_ref[:, columns] = inner
        d_gate = (d_inner * up * sigmoid * (1.0 + gate * (1.0 - sigmoid))).astype(BF)
        d_up = (d_inner * silu).astype(BF)
        d_gu_ref[0, :, columns] = d_gate
        d_gu_ref[1, :, columns] = d_up
        inner_t_ref[columns, :] = inner.T

    whole = hidden // CHUNK

    def one(i, carried):
        part(pl.multiple_of(i * CHUNK, CHUNK), CHUNK)
        return carried

    lax.fori_loop(0, whole, one, 0)
    if hidden > whole * CHUNK:
        part(whole * CHUNK, hidden - whole * CHUNK)

    def two(i, carried):
        place = pl.ds(pl.multiple_of(i * CHUNK, CHUNK), CHUNK)
        back = lax.dot_general(
            d_gu_ref[0], gw_ref[0, place, :], (((1,), (1,)), ((), ())), preferred_element_type=F32
        )
        back = back + lax.dot_general(
            d_gu_ref[1], gw_ref[1, place, :], (((1,), (1,)), ((), ())), preferred_element_type=F32
        )
        d_act_ref[:, place] = back.astype(BF)
        mlp_ref[:, place] = jnp.dot(
            inner_ref[...], wd_ref[:, place], preferred_element_type=F32
        ).astype(BF)
        return carried

    lax.fori_loop(0, width // CHUNK, two, 0)


def mlp(act, dz, gw, wd):
    tokens, width = act.shape
    hidden = gw.shape[2]
    vmem = pl.BlockSpec(memory_space=pltpu.VMEM)
    anywhere = pl.BlockSpec(memory_space=pl.ANY)
    return pl.pallas_call(
        mlp_kernel,
        out_shape=(
            jax.ShapeDtypeStruct((tokens, width), BF),
            jax.ShapeDtypeStruct((tokens, width), BF),
            jax.ShapeDtypeStruct((width, tokens), BF),
            jax.ShapeDtypeStruct((2, tokens, hidden), BF),
            jax.ShapeDtypeStruct((hidden, tokens), BF),
        ),
        in_specs=[vmem, vmem, anywhere, anywhere],
        out_specs=[vmem] * 5,
        scratch_shapes=[
            pltpu.VMEM(gw.shape, BF),
            pltpu.VMEM((hidden, width), BF),
            pltpu.VMEM((tokens, hidden), BF),
            pltpu.SemaphoreType.DMA((3,)),
        ],
        compiler_params=pltpu.CompilerParams(vmem_limit_bytes=60 * 1024 * 1024),
        cost_estimate=pl.CostEstimate(
            flops=12 * tokens * width * hidden, bytes_accessed=50_000_000, transcendentals=0
        ),
        name="mlp",
    )(act, dz, gw, wd)


def turn_kernel(
    ctx_size,
    wa_size,
    parts_ref,
    mlp_ref,
    hidden_ref,
    gain_ref,
    dz_ref,
    act_t_ref,
    d_gu_ref,
    inner_t_ref,
    dz_all_ref,
    all_ref,
    gain_out_ref,
    out_ref,
    gu_out_ref,
    down_out_ref,
    *scratch,
):
    p = place_of(ctx_size, wa_size)
    got_ref, more_ref, wa_send, wa_recv, more_send, more_recv = scratch[:6]
    gu_both, gu_got, gu_near, gu_sent, down_both, down_got, down_near, down_sent = scratch[6:14]
    gu_sems, down_sems, spread_sems = scratch[14:18], scratch[18:22], scratch[22:26]
    own_parts, own_mlp, local = scratch[26:29]
    greet([p.beside] + p.ahead[1:], p.down[1:])
    copies = [
        send(parts_ref.at[s], got_ref.at[s], wa_send.at[s], wa_recv.at[s], wa=p.down[s])
        for s in range(1, wa_size)
    ]
    loads = [
        pltpu.make_async_copy(parts_ref.at[0], own_parts, local.at[0]),
        pltpu.make_async_copy(mlp_ref.at[0], own_mlp, local.at[1]),
    ]
    for copy in loads:
        copy.start()
    down_total = down_both.shape[1]
    down_rows = down_total // 2
    columns = dz_all_ref.shape[1] // ctx_size
    half = gu_both.shape[1] // 2
    piece_rows = gu_both.shape[3]
    wa_rows = act_t_ref.shape[0] // wa_size

    def down_piece(ref, chip):
        return ref.at[:, pl.ds(pl.multiple_of(chip * columns, columns), columns)]

    def down_half(ref, chip, h):
        place = pl.ds(h * down_rows, down_rows)
        if chip is None:
            return ref.at[place]
        return ref.at[place, pl.ds(pl.multiple_of(chip * columns, columns), columns)]

    down = Fold(
        p,
        down_both,
        down_got,
        down_near,
        down_sent,
        down_piece,
        down_half,
        lambda into, other: add_rows(into, other, 16),
        down_sems,
    )

    def gu_half(ref, chip, h):
        place = pl.ds(h * half, half)
        return ref.at[place] if chip is None else ref.at[place, chip]

    gu = Fold(
        p,
        gu_both,
        gu_got,
        gu_near,
        gu_sent,
        lambda ref, chip: ref.at[:, chip],
        gu_half,
        add_blocks,
        gu_sems,
    )

    def make(chip):
        first = chip * (2 * piece_rows)
        left = jnp.concatenate(
            [
                act_t_ref[pl.ds(pl.multiple_of(i * wa_rows + first, 2 * piece_rows), 2 * piece_rows), :]
                for i in range(wa_size)
            ],
            axis=0,
        )

        def gu_part(part, carried):
            made = jnp.dot(left, d_gu_ref[part], preferred_element_type=F32).astype(BF)
            for i in range(wa_size):
                for core in range(2):
                    at = (2 * i + core) * piece_rows
                    gu_both[core, part * wa_size + i, chip] = made[at : at + piece_rows]
            return carried

        lax.fori_loop(0, 2, gu_part, 0)

        def down_part(core, carried):
            place = pl.multiple_of((core * p.chips + chip) * columns, columns)
            made = jnp.dot(
                inner_t_ref[...], dz_all_ref[:, pl.ds(place, columns)], preferred_element_type=F32
            ).astype(BF)
            target = pl.ds(pl.multiple_of(chip * columns, columns), columns)
            down_both[core, :, target] = made[:down_total]
            return carried

        lax.fori_loop(0, 2, down_part, 0)

    for i in range(p.chips):
        make(gu.order[i])
        gu.start(i)
        down.start(i)
        if i > 0:
            gu.between(i - 1)
            down.between(i - 1)
    gu.between(p.chips - 1)
    down.between(p.chips - 1)
    hidden = hidden_ref[...]
    scale = lax.rsqrt(jnp.mean(hidden * hidden, axis=-1, keepdims=True) + EPSILON)
    down.onward()
    for copy in loads:
        copy.wait()
    d_normed = own_parts[...].astype(F32)
    for s in range(1, wa_size):
        copies[s - 1].wait_recv()
        d_normed = d_normed + got_ref[s].astype(F32)
    more = [
        send(mlp_ref.at[s], more_ref.at[s], more_send.at[s], more_recv.at[s], wa=p.down[s])
        for s in range(1, wa_size)
    ]
    gain_out_ref[...] = jnp.sum(d_normed * (hidden * scale), axis=0, keepdims=True)
    d_hidden = norm_back(hidden, scale, gain_ref[...], d_normed, dz_ref[...].astype(F32))
    all_ref[p.ctx] = d_hidden.astype(BF)
    half_rows = all_ref.shape[1] // 2
    spread = Spread(
        p,
        all_ref.at[p.ctx],
        lambda d: all_ref.at[d],
        lambda d, h: all_ref.at[d, pl.ds(h * half_rows, half_rows)],
        spread_sems,
    )
    spread.start()
    gu.onward()
    down_out_ref[...] = down.total()[...]
    for _ in spread.arrivals():
        pass
    gu_out_ref[...] = gu.total()[...]
    result = hidden + own_mlp[...].astype(F32)
    for s in range(1, wa_size):
        more[s - 1].wait_recv()
        result = result + more_ref[s].astype(F32)
    out_ref[...] = result.astype(BF)
    for copy in copies + more:
        copy.wait_send()
    down.finish()
    gu.finish()
    spread.finish()


def turn(
    parts, mlp, hidden, gain, dz, act_t, d_gu, inner_t, dz_all, hidden_rows, ctx_size, wa_size
):
    rows, width = hidden.shape
    chips = ctx_size // 2
    columns = width // ctx_size
    lead = 2 * wa_size
    gu_rows, gu_columns = width // (ctx_size * wa_size), d_gu.shape[2]
    vmem = pl.BlockSpec(memory_space=pltpu.VMEM)
    anywhere = pl.BlockSpec(memory_space=pl.ANY)
    many = 2 if chips == 4 else chips - 1
    return pl.pallas_call(
        functools.partial(turn_kernel, ctx_size, wa_size),
        out_shape=(
            jax.ShapeDtypeStruct((ctx_size, rows, width), BF),
            jax.ShapeDtypeStruct((1, width), F32),
            jax.ShapeDtypeStruct((rows, width), BF),
            jax.ShapeDtypeStruct((lead, gu_rows, gu_columns), BF),
            jax.ShapeDtypeStruct((hidden_rows, columns), BF),
        ),
        in_specs=[anywhere] * 2 + [vmem] * 7,
        out_specs=[vmem] * 5,
        scratch_shapes=[pltpu.VMEM((wa_size, rows, width), BF)] * 2
        + [pltpu.SemaphoreType.DMA((wa_size,))] * 4
        + [
            pltpu.VMEM((2, lead, chips, gu_rows, gu_columns), BF),
            pltpu.VMEM((lead, chips, gu_rows, gu_columns), BF),
            pltpu.VMEM((2, lead // 2, gu_rows, gu_columns), BF),
            pltpu.VMEM((many, lead, gu_rows, gu_columns), BF),
            pltpu.VMEM((2, hidden_rows, columns * chips), BF),
            pltpu.VMEM((hidden_rows, columns * chips), BF),
            pltpu.VMEM((2, hidden_rows // 2, columns), BF),
            pltpu.VMEM((many, hidden_rows, columns), BF),
        ]
        + [pltpu.SemaphoreType.DMA((max(chips, 6),))] * 8
        + plane_sems(ctx_size)
        + [pltpu.VMEM((rows, width), BF)] * 2
        + [pltpu.SemaphoreType.DMA((2,))],
        compiler_params=pltpu.CompilerParams(
            collective_id=2, has_side_effects=True, vmem_limit_bytes=VMEM_LIMIT
        ),
        cost_estimate=pl.CostEstimate(flops=0, bytes_accessed=200_000_000, transcendentals=0),
        name="turn",
    )(parts, mlp, hidden, gain, dz, act_t, d_gu, inner_t, dz_all)


def close_kernel(
    ctx_size,
    wa_size,
    grads_ref,
    w_ref,
    x_ref,
    gain_ref,
    dh_ref,
    gu_ref,
    dw_ref,
    do_ref,
    down_ref,
    gains_ref,
    out_ref,
    gus_ref,
    downs_ref,
    qkvs_ref,
    outs_ref,
    sums_ref,
    *scratch,
):
    p = place_of(ctx_size, wa_size)
    gu_in, rows_ref, dw_in, share_ref, do_in, out_share_ref = scratch[8:14]
    do_parts, part_send, part_recv = scratch[43:46]
    wa_gains, ctx_gains, local = scratch[14:17]
    gu_sems, dw_sems, do_sems = scratch[17:19], scratch[19:21], scratch[21:23]
    wa_sems, ctx_sems = scratch[23:25], scratch[25:27]
    down_plane, gu_plane, qkv_plane, out_plane = (scratch[i : i + 4] for i in (27, 31, 35, 39))
    peers = [lax.rem(p.ctx + i, ctx_size) for i in range(1, ctx_size)]
    greet(peers, p.up[1:])
    locals_ = []

    def keep(source, target):
        copy = pltpu.make_async_copy(source, target, local.at[len(locals_)])
        copy.start()
        locals_.append(copy)

    def spread_of(own, slots, sems):
        half = slots.shape[1] // 2
        keep(own, slots.at[p.ctx])
        spread = Spread(
            p,
            own,
            lambda d: slots.at[d],
            lambda d, h: slots.at[d, pl.ds(h * half, half)],
            sems,
        )
        spread.start()
        return spread

    def over_wa(source, target, sems):
        return [
            send(
                source(p.up[s]),
                target.at[s],
                sems[0].at[s],
                sems[1].at[s],
                wa=p.up[s],
            )
            for s in range(1, wa_size)
        ]

    def add_up(source, found, into, step):
        def one(i, carried):
            place = pl.ds(pl.multiple_of(i * step, step), step)
            total = source(p.wa)[place, :].astype(F32)
            for s in range(1, wa_size):
                total = total + found[s, place, :].astype(F32)
            into[place, :] = total.astype(BF)
            return carried

        lax.fori_loop(0, into.shape[0] // step, one, 0)

    deal = [
        send(
            gu_ref.at[:, p.up[s]], gu_in.at[p.wa], gu_sems[0].at[s], gu_sems[1].at[s], wa=p.up[s]
        )
        for s in range(1, wa_size)
    ]
    rows = x_ref.shape[0]

    def part_of(device):
        place = pl.ds(pl.multiple_of(device * rows, rows), rows)
        return lax.dot_general(
            grads_ref[place, :],
            w_ref[...],
            (((1,), (1,)), ((), ())),
            preferred_element_type=F32,
        )

    scatter = Scatter(p, part_of, scratch[:8])
    scatter.start()
    head_cols = do_ref.shape[0]

    def do_part(device):
        columns = pl.ds(pl.multiple_of(device * head_cols, head_cols), head_cols)
        return do_ref.at[:, columns]

    part_copies = exchange_plane(
        [p.ctx] + peers, do_part, lambda d: do_parts.at[d], part_send, part_recv
    )
    keep(do_part(p.ctx), do_parts.at[p.ctx])
    down_spread = spread_of(down_ref, downs_ref, down_plane)
    wa_gains[p.wa] = gains_ref[...]
    small = [
        send(gains_ref, wa_gains.at[p.wa], wa_sems[0].at[s], wa_sems[1].at[s], wa=p.up[s])
        for s in range(1, wa_size)
    ]
    gu_in[p.wa] = gu_ref[:, p.wa]
    for copy in deal:
        copy.wait_recv()
    dw_copies = over_wa(lambda d: dw_ref.at[d], dw_in, dw_sems)
    total_columns = rows_ref.shape[1] // 2
    own_columns = total_columns // wa_size
    for i in range(wa_size):
        for part in range(2):
            first = part * total_columns + i * own_columns
            rows_ref[:, first : first + own_columns] = gu_in[i, part, :, :own_columns]
    gu_spread = spread_of(rows_ref, gus_ref, gu_plane)
    for copy in small:
        copy.wait()
    plane_gain = wa_gains[0]
    for i in range(1, wa_size):
        plane_gain = plane_gain + wa_gains[i]
    ctx_gains[p.ctx] = plane_gain
    own_gain = ctx_gains.at[p.ctx]
    small = [
        send(own_gain, own_gain, ctx_sems[0].at[i], ctx_sems[1].at[i], ctx=peer)
        for i, peer in enumerate(peers)
    ]
    x = x_ref[...].astype(F32)
    scale = lax.rsqrt(jnp.mean(x * x, axis=-1, keepdims=True) + EPSILON)
    d_normed = scatter.total()
    out_ref[...] = norm_back(
        x, scale, gain_ref[...], d_normed, dh_ref[...].astype(F32)
    ).astype(BF)
    for _ in down_spread.arrivals():
        pass
    for _ in gu_spread.arrivals():
        pass
    for copy in small:
        copy.wait()
    total_gain = ctx_gains[0]
    for i in range(1, ctx_size):
        total_gain = total_gain + ctx_gains[i]
    sums_ref[...] = total_gain
    for copy in dw_copies:
        copy.wait_recv()
    for copy in part_copies:
        copy.wait_recv()
    locals_[0].wait()
    per_wa = ctx_size // wa_size

    def do_block(device):
        return do_parts.at[pl.ds(device * per_wa, per_wa)]

    do_copies = over_wa(do_block, do_in, do_sems)
    add_up(lambda d: dw_ref.at[d], dw_in, share_ref, 16)
    qkv_spread = spread_of(share_ref, qkvs_ref, qkv_plane)
    for copy in do_copies:
        copy.wait_recv()
    for i in range(per_wa):
        place = pl.ds(i * head_cols, head_cols)
        total = do_parts[p.wa * per_wa + i].astype(F32)
        for s in range(1, wa_size):
            total = total + do_in[s, i].astype(F32)
        out_share_ref[place, :] = total.astype(BF)
    out_spread = spread_of(out_share_ref, outs_ref, out_plane)
    for _ in qkv_spread.arrivals():
        pass
    for _ in out_spread.arrivals():
        pass
    scatter.finish()
    for spread in (down_spread, gu_spread, qkv_spread, out_spread):
        spread.finish()
    for copy in deal + dw_copies + do_copies + part_copies:
        copy.wait_send()
    for copy in locals_[1:]:
        copy.wait()


def close(grads, w, x_own, gain, dh, gu, dw, do, down, gains_own, columns, ctx_size, wa_size):
    rows, width = x_own.shape
    vmem = pl.BlockSpec(memory_space=pltpu.VMEM)
    anywhere = pl.BlockSpec(memory_space=pl.ANY)
    gu_shape = (gu.shape[2], columns)
    out_shape = (width // wa_size, do.shape[0])
    shapes = [gu_shape, down.shape, dw.shape[1:], out_shape]
    gains = (2, width)
    return pl.pallas_call(
        functools.partial(close_kernel, ctx_size, wa_size),
        out_shape=(jax.ShapeDtypeStruct((rows, width), BF),)
        + tuple(jax.ShapeDtypeStruct((ctx_size,) + shape, BF) for shape in shapes)
        + (jax.ShapeDtypeStruct(gains, F32),),
        in_specs=[vmem] * 10,
        out_specs=[vmem] + [anywhere] * 4 + [vmem],
        scratch_shapes=scatter_scratch(ctx_size, rows, width)
        + [
            pltpu.VMEM((wa_size, 2) + gu.shape[2:], BF),
            pltpu.VMEM(gu_shape, BF),
            pltpu.VMEM(dw.shape, BF),
            pltpu.VMEM(dw.shape[1:], BF),
            pltpu.VMEM((wa_size, ctx_size // wa_size, do.shape[0], do.shape[0]), BF),
            pltpu.VMEM(out_shape, BF),
            pltpu.VMEM((wa_size,) + gains, F32),
            pltpu.VMEM((ctx_size,) + gains, F32),
            pltpu.SemaphoreType.DMA((5,)),
        ]
        + [pltpu.SemaphoreType.DMA((wa_size,))] * 8
        + [pltpu.SemaphoreType.DMA((ctx_size,))] * 2
        + plane_sems(ctx_size) * 4
        + [pltpu.VMEM((ctx_size, do.shape[0], do.shape[0]), BF)]
        + [pltpu.SemaphoreType.DMA((ctx_size,))] * 2,
        compiler_params=pltpu.CompilerParams(
            collective_id=3, has_side_effects=True, vmem_limit_bytes=VMEM_LIMIT
        ),
        cost_estimate=pl.CostEstimate(
            flops=2 * grads.size * width, bytes_accessed=400_000_000, transcendentals=0
        ),
        name="close",
    )(grads, w, x_own, gain, dh, gu, dw, do, down, gains_own)


def widen(blocks, columns, order, step):
    count, rows, own = blocks.shape
    parts = own // columns

    def body(block_ref, out_ref):
        for i in range(parts):
            for at, device in enumerate(order):
                first = (i * count + at) * columns
                out_ref[:, first : first + columns] = block_ref[
                    device, :, i * columns : (i + 1) * columns
                ].astype(F32)

    return pl.pallas_call(
        body,
        out_shape=jax.ShapeDtypeStruct((rows, count * own), F32),
        grid=(rows // step,),
        in_specs=[pl.BlockSpec((count, step, own), lambda r: (0, r, 0))],
        out_specs=pl.BlockSpec((step, count * own), lambda r: (r, 0)),
        compiler_params=pltpu.CompilerParams(vmem_limit_bytes=VMEM_LIMIT),
        name="widen",
    )(blocks)


def per_device(
    tokens, lengths, dealing, norm1_gain, w_qkv, w_out, norm2_gain, w_gate_up, w_down, grad_out
):
    tok_rows, width = tokens.shape[1], tokens.shape[2]
    ctx_size = lax.axis_size("ctx")
    wa_size = lax.axis_size("wa")
    ctx_index = lax.axis_index("ctx")
    wa_index = lax.axis_index("wa")
    block_order = dealing[0]
    block_total = block_order.shape[0]
    group_rows = block_total * BLOCK
    own_blocks = tok_rows // BLOCK
    first_length = lengths[0, 0]
    heads_own = HEADS // ctx_size
    head_cols = heads_own * HEAD
    wa_rows = width // wa_size
    ff_total = w_gate_up.shape[1] // 2
    ff_own = w_down.shape[0]
    piece_rows = wa_rows // ctx_size

    block_ids = jnp.arange(block_total, dtype=jnp.int32)
    inverse = jnp.sum(
        jnp.where(block_order[None, :] == block_ids[:, None], block_ids[None, :], 0), axis=1
    )

    qkv_slice = jnp.concatenate(
        [
            lax.dynamic_slice_in_dim(w_qkv, part * width + ctx_index * head_cols, head_cols, 1)
            for part in range(3)
        ],
        axis=1,
    )
    dealt, qkv_cols = gather_both(tokens[0], qkv_slice, ctx_size, wa_size)
    dealt = dealt.reshape(group_rows, width)
    qkv_cols = qkv_cols.reshape(width, 3 * head_cols)
    out_slice = lax.dynamic_slice_in_dim(w_out, ctx_index * head_cols, head_cols, 1)
    out_cols = gather_rows(out_slice, "wa")
    out_cols = out_cols.reshape(ctx_size, head_cols, head_cols)
    gu_piece = lax.dynamic_slice_in_dim(w_gate_up, ctx_index * piece_rows, piece_rows, 0)
    hidden_own = -(-ff_own // 128) * 128
    gu_send = jnp.pad(
        jnp.stack(
            [
                jnp.stack(
                    [
                        gu_piece[:, first + to * ff_own : first + (to + 1) * ff_own]
                        for first in (0, ff_total)
                    ]
                )
                for to in range(wa_size)
            ]
        ),
        ((0, 0), (0, 0), (0, 0), (0, hidden_own - ff_own)),
    )

    positions = jnp.arange(group_rows, dtype=jnp.int32)
    segments = (positions >= first_length).astype(jnp.int32)
    cosine, sine = rotary_tables(positions - segments * first_length)
    first_block = (ctx_index * own_blocks)[None].astype(jnp.int32)
    act_one, own_given = arrange(inverse, first_block, dealt, norm1_gain[None, :], own_blocks)
    query_b, key_b, value_b, mixed_b, probs_b, gu_mine, out_rows = attend(
        segments,
        act_one,
        qkv_cols,
        cosine,
        sine,
        gu_send,
        out_cols,
        ctx_size,
        wa_size,
    )
    gain_two = norm2_gain[None, :]
    hidden, acts, gu_weight = out_project(
        mixed_b, out_rows, own_given, gain_two, gu_mine, ctx_size, wa_size
    )
    gu_weight = gu_weight.reshape(2, width, hidden_own)
    act_two = acts.reshape(wa_size * tok_rows, width)
    early = lax.optimization_barrier((grad_out[0], mixed_b))[0]
    grads_all = lax.all_gather(early, "wa", axis=0)
    cotangent = jnp.concatenate(
        [take(grads_all, (wa_index - s) % wa_size) for s in range(wa_size)], axis=0
    )

    d_act, mlp_parts, act_t, d_gu, inner_t = mlp(act_two, cotangent, gu_weight, w_down)
    d_branches, gain_two_part, out_given, gu_piece_grad, down_piece_grad = turn(
        d_act.reshape(wa_size, tok_rows, width),
        mlp_parts.reshape(wa_size, tok_rows, width),
        hidden,
        gain_two,
        grad_out[0],
        act_t,
        d_gu,
        inner_t,
        cotangent,
        ff_own,
        ctx_size,
        wa_size,
    )
    d_branch_b = d_branches.reshape(group_rows, width)
    own_order = lax.dynamic_slice_in_dim(block_order, ctx_index * own_blocks, own_blocks)
    d_qkv_b, dealt_qkv, d_out_part, d_hidden_dealt = attend_back(
        inverse,
        own_order,
        d_branch_b,
        out_rows,
        mixed_b,
        query_b,
        key_b,
        value_b,
        probs_b,
        cosine,
        sine,
    )
    qkv_grad = dot_left_t(act_one, d_qkv_b)
    gain_one_part = jnp.sum(qkv_grad * qkv_cols.astype(F32), axis=1) / norm1_gain
    qkv_parts = qkv_grad.astype(BF).reshape(wa_size, wa_rows, 3 * head_cols)
    d_tokens, gus, downs, qkvs, outs, gain_sums = close(
        dealt_qkv,
        qkv_cols,
        tokens[0],
        norm1_gain[None, :],
        d_hidden_dealt,
        gu_piece_grad.reshape(2, wa_size, piece_rows, hidden_own),
        qkv_parts,
        d_out_part,
        down_piece_grad,
        jnp.concatenate([gain_one_part[None, :], gain_two_part], axis=0),
        2 * ff_total,
        ctx_size,
        wa_size,
    )
    d_gate_up = gus.reshape(wa_rows, 2 * ff_total).astype(F32)
    in_order = list(range(ctx_size))
    by_core = in_order[0::2] + in_order[1::2]
    d_down = widen(downs, downs.shape[2], by_core, ff_own // 2 if ff_own % 32 == 0 else ff_own)
    d_qkv = widen(qkvs, head_cols, in_order, 64)
    d_out = widen(outs, head_cols, in_order, 128)
    return (
        out_given[None],
        d_tokens[None],
        gain_sums[0],
        d_qkv,
        d_out,
        gain_sums[1],
        d_gate_up,
        d_down,
    )


def solution(mesh):
    in_specs = (
        P("wa", "ctx", None),
        P("wa", None),
        P("wa", None),
        P(),
        P("wa", None),
        P("wa", None),
        P(),
        P("wa", None),
        P("wa", None),
        P("wa", "ctx", None),
    )
    out_specs = (
        P("wa", "ctx", None),
        P("wa", "ctx", None),
        P(),
        P("wa", None),
        P("wa", None),
        P(),
        P("wa", None),
        P("wa", None),
    )
    return jax.shard_map(
        per_device, mesh=mesh, in_specs=in_specs, out_specs=out_specs, check_vma=False
    )
```

```python
import functools
import math
import types

import jax
import jax.numpy as jnp
from jax import lax
from jax.experimental import pallas as pl
from jax.experimental.pallas import tpu as pltpu
from jax.sharding import PartitionSpec as P

HEADS = 16
HEAD = 128
WINDOW = 2048
BLOCK = 128

EPSILON = 1e-06
BF = jnp.bfloat16
F32 = jnp.float32
VMEM_LIMIT = 60 * 1024 * 1024
ATTEND_ROWS = 256
CHUNK = 256


def rotary_tables(seq_pos):
    half_width = HEAD // 2
    inverse_freq = jnp.power(10000.0, -2.0 * jnp.arange(half_width, dtype=F32) / HEAD)
    angles = seq_pos.astype(F32)[:, None] * inverse_freq[None, :]
    cosine, sine = jnp.cos(angles), jnp.sin(angles)
    return (
        jnp.concatenate([cosine, cosine], axis=-1),
        jnp.concatenate([-sine, sine], axis=-1),
    )


MESH = pl.DeviceIdType.MESH


def greet(ctx_peers, wa_peers):
    barrier = pltpu.get_barrier_semaphore()
    for peer in ctx_peers:
        pl.semaphore_signal(barrier, inc=1, device_id={"ctx": peer}, device_id_type=MESH)
    for peer in wa_peers:
        pl.semaphore_signal(barrier, inc=1, device_id={"wa": peer}, device_id_type=MESH)
    pl.semaphore_wait(barrier, len(ctx_peers) + len(wa_peers))


def send(source, target, send_sem, recv_sem, **peer):
    copy = pltpu.make_async_remote_copy(
        src_ref=source,
        dst_ref=target,
        send_sem=send_sem,
        recv_sem=recv_sem,
        device_id=peer,
        device_id_type=MESH,
    )
    copy.start()
    return copy


def place_of(ctx_size, wa_size):
    chips = ctx_size // 2
    p = types.SimpleNamespace(ctx_size=ctx_size, wa_size=wa_size, chips=chips)
    p.ctx, p.wa = lax.axis_index("ctx"), lax.axis_index("wa")
    p.core, p.chip = lax.rem(p.ctx, 2), lax.div(p.ctx, 2)
    p.beside = p.chip * 2 + 1 - p.core
    p.ahead = [lax.rem(p.chip + m, chips) * 2 + p.core for m in range(chips)]
    p.behind = [lax.rem(p.chip + chips - m, chips) * 2 + p.core for m in range(chips)]
    p.up = [lax.rem(p.wa + s, wa_size) for s in range(wa_size)]
    p.down = [lax.rem(p.wa + wa_size - s, wa_size) for s in range(wa_size)]
    p.square = chips == 4
    if p.square:
        p.near = [p.chip + 1 - 2 * lax.rem(p.chip, 2), lax.rem(p.chip + 2, 4)]
        p.far = 3 - p.chip
    return p


def on_core(p, chip):
    return chip * 2 + p.core


def off_core(p, chip):
    return chip * 2 + 1 - p.core


def plane_sems(ctx_size):
    count = max(ctx_size // 2, 5)
    return [pltpu.SemaphoreType.DMA((count,))] * 4


class Spread:
    def __init__(self, p, own, slot, half, sems):
        self.p, self.own, self.slot, self.half = p, own, slot, half
        self.chip_send, self.chip_recv, self.side_send, self.side_recv = sems
        self.chip, self.side = [], []

    def across(self, source, target, chip):
        i = len(self.chip)
        self.chip.append(
            send(source, target, self.chip_send.at[i], self.chip_recv.at[i], ctx=on_core(self.p, chip))
        )

    def aside(self, source, target):
        i = len(self.side)
        self.side.append(
            send(source, target, self.side_send.at[i], self.side_recv.at[i], ctx=self.p.beside)
        )

    def start(self):
        p = self.p
        target = self.slot(p.ctx)
        if p.square:
            for chip in p.near:
                self.across(self.own, target, chip)
        else:
            for m in range(1, p.chips):
                self.across(self.own, target, lax.rem(p.chip + m, p.chips))
        self.aside(self.own, target)

    def arrivals(self):
        p = self.p
        if not p.square:
            for m in range(1, p.chips):
                self.chip[m - 1].wait_recv()
                block = self.slot(p.behind[m])
                self.aside(block, block)
                yield p.behind[m]
            self.side[0].wait_recv()
            yield p.beside
            for m in range(1, p.chips):
                self.side[m].wait_recv()
                yield off_core(p, lax.rem(p.chip + p.chips - m, p.chips))
            return
        for i in range(2):
            self.chip[i].wait_recv()
            device = on_core(p, p.near[i])
            part = self.half(device, i)
            self.across(part, part, p.near[1 - i])
            self.aside(self.slot(device), self.slot(device))
            yield device
        self.side[0].wait_recv()
        yield p.beside
        for i in range(2):
            self.side[1 + i].wait_recv()
            yield off_core(p, p.near[i])
        device = on_core(p, p.far)
        for i in range(2):
            self.chip[2 + i].wait_recv()
            part = self.half(device, i)
            self.aside(part, part)
        yield device
        for i in range(2):
            self.side[3 + i].wait_recv()
        yield off_core(p, p.far)

    def finish(self):
        for copy in self.chip + self.side:
            copy.wait_send()


class Fold:
    def __init__(self, p, both, got, near, sent, piece, half, add, sems):
        self.p, self.both, self.got, self.near, self.sent = p, both, got, near, sent
        self.kept = both.at[p.core]
        self.piece, self.half, self.add = piece, half, add
        self.chip_send, self.chip_recv, self.side_send, self.side_recv = sems
        self.chip, self.side = [], []
        if p.square:
            self.order = [p.far] + p.near + [p.chip]
        else:
            self.order = [lax.rem(p.chip + m, p.chips) for m in range(1, p.chips)] + [p.chip]

    def across(self, source, target, chip):
        i = len(self.chip)
        self.chip.append(
            send(source, target, self.chip_send.at[i], self.chip_recv.at[i], ctx=on_core(self.p, chip))
        )

    def start(self, i):
        p = self.p
        chip = self.order[i]
        self.side.append(
            send(
                self.piece(self.both.at[1 - p.core], chip),
                self.piece(self.got, chip),
                self.side_send.at[i],
                self.side_recv.at[i],
                ctx=p.beside,
            )
        )

    def between(self, i):
        p = self.p
        chip = self.order[i]
        self.side[i].wait_recv()
        self.add(self.piece(self.kept, chip), self.piece(self.got, chip))
        if i == p.chips - 1:
            return
        if not p.square:
            self.across(self.piece(self.kept, chip), self.sent.at[i], chip)
        elif i == 0:
            for j in range(2):
                self.across(self.half(self.kept, chip, j), self.near.at[j], p.near[j])
        else:
            j = i - 1
            self.across(self.half(self.kept, chip, j), self.half(self.sent.at[j], None, j), chip)

    def onward(self):
        p = self.p
        if not p.square:
            return
        for i in range(2):
            self.chip[i].wait_recv()
            part = self.half(self.kept, p.near[1 - i], i)
            self.add(part, self.near.at[i])
            self.across(part, self.half(self.sent.at[1 - i], None, i), p.near[1 - i])

    def total(self):
        p = self.p
        for copy in self.chip[2:] if p.square else self.chip:
            copy.wait_recv()
        mine = self.piece(self.kept, p.chip)
        for i in range(2 if p.square else p.chips - 1):
            self.add(mine, self.sent.at[i])
        return mine

    def finish(self):
        for copy in self.side + self.chip:
            copy.wait_send()


def add_rows(into, other, step):
    def one(i, carried):
        place = pl.ds(pl.multiple_of(i * step, step), step)
        into[place, :] = (into[place, :].astype(F32) + other[place, :].astype(F32)).astype(BF)
        return carried

    lax.fori_loop(0, into.shape[0] // step, one, 0)


def add_blocks(into, other):
    lead = into.shape[:-2]

    def one(i, carried):
        at = (i,) if len(lead) == 1 else (i // lead[1], i % lead[1])
        into[at] = (into[at].astype(F32) + other[at].astype(F32)).astype(BF)
        return carried

    lax.fori_loop(0, math.prod(lead), one, 0)


class Scatter:
    def __init__(self, p, part_of, refs):
        self.p, self.part_of, self.refs = p, part_of, refs

    def start(self):
        p = self.p
        side_out, side_in, chip_out, chip_in, side_send, side_recv, chip_send, chip_recv = self.refs
        self.side, self.out = [], []
        order = list(range(1, p.chips)) + [0]
        for m in order:
            side_out[m] = self.part_of(lax.div(p.ahead[m], 2) * 2 + 1 - p.core).astype(BF)
            self.side.append(
                send(side_out.at[m], side_in.at[m], side_send.at[m], side_recv.at[m], ctx=p.beside)
            )
        for i, m in enumerate(order):
            mine = self.part_of(p.ahead[m])
            self.side[i].wait_recv()
            self.kept = mine + side_in[m].astype(F32)
            if m > 0:
                chip_out[m - 1] = self.kept.astype(BF)
                self.out.append(
                    send(
                        chip_out.at[m - 1],
                        chip_in.at[m - 1],
                        chip_send.at[m - 1],
                        chip_recv.at[m - 1],
                        ctx=p.ahead[m],
                    )
                )

    def total(self):
        chip_in = self.refs[3]
        total = self.kept
        for m in range(1, self.p.chips):
            self.out[m - 1].wait_recv()
            total = total + chip_in[m - 1].astype(F32)
        return total

    def finish(self):
        for copy in self.side + self.out:
            copy.wait_send()


def scatter_scratch(ctx_size, rows, width):
    chips = ctx_size // 2
    return [
        pltpu.VMEM((chips, rows, width), BF),
        pltpu.VMEM((chips, rows, width), BF),
        pltpu.VMEM((chips - 1, rows, width), BF),
        pltpu.VMEM((chips - 1, rows, width), BF),
    ] + [pltpu.SemaphoreType.DMA((chips,))] * 4


def norm_back(x, scale, gain, d_scaled, d_other):
    normed = x * scale
    scaled = d_scaled * gain
    return d_other + scale * (
        scaled - normed * jnp.mean(scaled * normed, axis=-1, keepdims=True)
    )


def gather_kernel(
    ctx_size, wa_size, cuts, own_columns, x_ref, w_ref, gu_ref, xs_ref, ws_ref, cut_ref, *scratch
):
    p = place_of(ctx_size, wa_size)
    ring_send, ring_recv, local, piece_ref = scratch[4:]
    greet([p.beside] + p.ahead[1:], [p.up[1], p.down[1]])
    rows = w_ref.shape[0] // cuts
    half_rows = x_ref.shape[0] // 2
    ring = []
    for i in range(cuts):
        part = pl.ds(i * rows, rows)
        ring.append(
            send(
                w_ref.at[part],
                ws_ref.at[p.wa, part],
                ring_send.at[0, i],
                ring_recv.at[0, i],
                wa=p.up[1],
            )
        )
    spread = Spread(
        p,
        x_ref,
        lambda d: xs_ref.at[d],
        lambda d, h: xs_ref.at[d, pl.ds(h * half_rows, half_rows)],
        scratch[:4],
    )
    spread.start()
    piece_rows = piece_ref.shape[0]
    place = pl.ds(pl.multiple_of(p.ctx * piece_rows, piece_rows), piece_rows)
    loads = [
        pltpu.make_async_copy(x_ref, xs_ref.at[p.ctx], local.at[0]),
        pltpu.make_async_copy(w_ref, ws_ref.at[p.wa], local.at[1]),
        pltpu.make_async_copy(gu_ref.at[place], piece_ref, local.at[2]),
    ]
    for copy in loads:
        copy.start()
    loads[2].wait()
    total = piece_ref.shape[1] // 2
    hidden = cut_ref.shape[3]
    for to in range(wa_size):
        for part in range(2):
            first = part * total + to * own_columns
            cut_ref[to, part, :, :own_columns] = piece_ref[:, first : first + own_columns]
            if hidden > own_columns:
                cut_ref[to, part, :, own_columns:] = jnp.zeros(
                    (piece_rows, hidden - own_columns), BF
                )
    late = []
    for step in range(1, wa_size):
        for i in range(cuts):
            ring[i].wait_recv()
            late.append(ring[i])
            if step < wa_size - 1:
                block = ws_ref.at[p.down[step], pl.ds(i * rows, rows)]
                ring[i] = send(
                    block, block, ring_send.at[step, i], ring_recv.at[step, i], wa=p.up[1]
                )
        if step == 1:
            for _ in spread.arrivals():
                pass
    for copy in late:
        copy.wait_send()
    spread.finish()
    for copy in loads[:2]:
        copy.wait()


def gather_both(x, w, gu, own_columns, ctx_size, wa_size, cuts=4):
    anywhere = pl.BlockSpec(memory_space=pl.ANY)
    piece_rows = w.shape[0] // ctx_size
    hidden = -(-own_columns // 128) * 128
    return pl.pallas_call(
        functools.partial(gather_kernel, ctx_size, wa_size, cuts, own_columns),
        out_shape=(
            jax.ShapeDtypeStruct((ctx_size,) + x.shape, x.dtype),
            jax.ShapeDtypeStruct((wa_size,) + w.shape, w.dtype),
            jax.ShapeDtypeStruct((wa_size, 2, piece_rows, hidden), BF),
        ),
        in_specs=[anywhere] * 3,
        out_specs=[anywhere] * 2 + [pl.BlockSpec(memory_space=pltpu.VMEM)],
        scratch_shapes=plane_sems(ctx_size)
        + [pltpu.SemaphoreType.DMA((wa_size - 1, cuts))] * 2
        + [pltpu.SemaphoreType.DMA((3,)), pltpu.VMEM((piece_rows, gu.shape[1]), BF)],
        compiler_params=pltpu.CompilerParams(
            collective_id=0, has_side_effects=True, vmem_limit_bytes=VMEM_LIMIT
        ),
        cost_estimate=pl.CostEstimate(flops=0, bytes_accessed=200_000_000, transcendentals=0),
        name="gather_both",
    )(x, w, gu)


def exchange_plane(peers, source, target, send_sem, recv_sem):
    here = target(peers[0])
    return [
        send(source(peer), here, send_sem.at[i], recv_sem.at[i], ctx=peer)
        for i, peer in enumerate(peers)
        if i > 0
    ]


def attend_kernel(
    ctx_size,
    wa_size,
    heads,
    row_seg_ref,
    column_seg_ref,
    x_ref,
    w_ref,
    gain_ref,
    pick_ref,
    cos_ref,
    sin_ref,
    gu_ref,
    act_t_ref,
    own_ref,
    q_ref,
    k_ref,
    v_ref,
    o_ref,
    prob_ref,
    gw_ref,
    rows_ref,
    gu_send,
    gu_recv,
    local,
    out_send,
    out_recv,
    dealt_ref,
):
    wa, ctx = lax.axis_index("wa"), lax.axis_index("ctx")
    up = [lax.rem(wa + s, wa_size) for s in range(wa_size)]
    peers = [lax.rem(ctx + i, ctx_size) for i in range(ctx_size)]
    greet(peers[1:], up[1:])
    head_cols = heads * HEAD

    def columns_of(d):
        rows = pl.ds(pl.multiple_of(d * head_cols, head_cols), head_cols)
        return w_ref.at[rows, pl.ds(3 * head_cols, head_cols)]

    def rows_of(d):
        return rows_ref.at[:, pl.ds(pl.multiple_of(d * head_cols, head_cols), head_cols)]

    deal_out = exchange_plane(peers, columns_of, rows_of, out_send, out_recv)
    own_out = pltpu.make_async_copy(columns_of(ctx), rows_of(ctx), local.at[1])
    own_out.start()
    deal = [
        send(gu_ref.at[up[s]], gw_ref.at[:, wa], gu_send.at[s], gu_recv.at[s], wa=up[s])
        for s in range(1, wa_size)
    ]
    own = pltpu.make_async_copy(gu_ref.at[wa], gw_ref.at[:, wa], local.at[0])
    own.start()
    rows = x_ref.shape[0]
    step = ATTEND_ROWS

    def project(i, carried):
        place = pl.ds(pl.multiple_of(i * step, step), step)
        x = x_ref[place, :].astype(F32)
        scale = lax.rsqrt(jnp.mean(x * x, axis=-1, keepdims=True) + EPSILON)
        act = (x * scale * gain_ref[...]).astype(BF)
        act_t_ref[:, place] = act.T
        made = jnp.dot(act, w_ref[:, : 3 * head_cols], preferred_element_type=F32)
        cosine, sine = cos_ref[place, :], sin_ref[place, :]
        for head in range(2 * heads):
            columns = slice(head * HEAD, (head + 1) * HEAD)
            u = made[:, columns]
            dealt_ref[place, columns] = (
                u * cosine + pltpu.roll(u, HEAD // 2, 1) * sine
            ).astype(BF)
        dealt_ref[place, 2 * head_cols :] = made[:, 2 * head_cols :].astype(BF)
        return carried

    lax.fori_loop(0, rows // step, project, 0)

    def put_in_order(i, carried):
        place = pl.ds(pl.multiple_of(i * step, step), step)
        given = jnp.dot(pick_ref[place, :], dealt_ref[...], preferred_element_type=F32).astype(BF)
        q_ref[place, :] = given[:, :head_cols]
        k_ref[place, :] = given[:, head_cols : 2 * head_cols]
        v_ref[place, :] = given[:, 2 * head_cols :]
        return carried

    lax.fori_loop(0, rows // step, put_in_order, 0)
    own_rows = own_ref.shape[0]
    own_place = pl.ds(pl.multiple_of(ctx * own_rows, own_rows), own_rows)
    own_ref[...] = jnp.dot(
        pick_ref[own_place, :], x_ref[...], preferred_element_type=F32
    ).astype(BF)
    for i in range(rows // step):
        here = slice(i * step, (i + 1) * step)
        keys = (i + 1) * step
        row = lax.broadcasted_iota(jnp.int32, (step, keys), 0) + i * step
        column = lax.broadcasted_iota(jnp.int32, (step, keys), 1)
        allowed = (column <= row) & (row_seg_ref[here, :] == column_seg_ref[:, :keys])
        if rows > WINDOW:
            allowed = allowed & (row - column < WINDOW)
        for head in range(heads):
            columns = slice(head * HEAD, (head + 1) * HEAD)
            scores = lax.dot_general(
                q_ref[here, columns],
                k_ref[:keys, columns],
                (((1,), (1,)), ((), ())),
                preferred_element_type=F32,
            )
            scores = jnp.where(allowed, scores * (1.0 / math.sqrt(HEAD)), -1e30)
            largest = jnp.max(scores, axis=-1, keepdims=True)
            weights = jnp.exp(scores - largest)
            total = jnp.sum(weights, axis=-1, keepdims=True)
            probs = (weights * (1.0 / total)).astype(BF)
            prob_ref[head, here, :keys] = probs
            o_ref[here, columns] = jnp.dot(
                probs, v_ref[:keys, columns], preferred_element_type=F32
            ).astype(BF)
    own.wait()
    own_out.wait()
    for copy in deal + deal_out:
        copy.wait()


def attend(segments, x, w, gain, pick, cosine, sine, gu, ctx_size, wa_size):
    rows, width = x.shape
    head_cols = w.shape[1] // 4
    heads = head_cols // HEAD
    vmem = pl.BlockSpec(memory_space=pltpu.VMEM)
    anywhere = pl.BlockSpec(memory_space=pl.ANY)
    heads_shape = jax.ShapeDtypeStruct((rows, head_cols), BF)
    return pl.pallas_call(
        functools.partial(attend_kernel, ctx_size, wa_size, heads),
        out_shape=(
            jax.ShapeDtypeStruct((width, rows), BF),
            jax.ShapeDtypeStruct((rows // ctx_size, width), BF),
            heads_shape,
            heads_shape,
            heads_shape,
            heads_shape,
            jax.ShapeDtypeStruct((heads, rows, rows), BF),
            jax.ShapeDtypeStruct((2, wa_size) + gu.shape[2:], BF),
            jax.ShapeDtypeStruct((head_cols, width), BF),
        ),
        in_specs=[vmem] * 8 + [anywhere],
        out_specs=[vmem] * 7 + [anywhere] * 2,
        scratch_shapes=[pltpu.SemaphoreType.DMA((wa_size,))] * 3
        + [pltpu.SemaphoreType.DMA((ctx_size,))] * 2
        + [pltpu.VMEM((rows, 3 * head_cols), BF)],
        compiler_params=pltpu.CompilerParams(
            collective_id=4, has_side_effects=True, vmem_limit_bytes=VMEM_LIMIT
        ),
        cost_estimate=pl.CostEstimate(
            flops=2 * rows * width * 3 * head_cols, bytes_accessed=100_000_000, transcendentals=0
        ),
        name="attend",
    )(segments[:, None], segments[None, :], x, w, gain, pick, cosine, sine, gu)


def attend_back_kernel(
    ctx_size,
    wa_size,
    heads,
    dy_ref,
    w_ref,
    o_ref,
    q_ref,
    k_ref,
    v_ref,
    cos_ref,
    sin_ref,
    prob_any,
    act_t_any,
    w_all_any,
    unpick_any,
    gu_ref,
    down_ref,
    grads_ref,
    dh_ref,
    dw_ref,
    gain_ref,
    parts_ref,
    gu_in_ref,
    downs_ref,
    do_ref,
    dk_ref,
    dv_ref,
    d_out_ref,
    given_ref,
    prob_ref,
    act_t_ref,
    w_all_ref,
    unpick_ref,
    *sems,
):
    p = place_of(ctx_size, wa_size)
    gu_send, gu_recv, part_send, part_recv, local = sems[4:]
    peers = [lax.rem(p.ctx + i, ctx_size) for i in range(ctx_size)]
    greet(peers[1:], p.up[1:])
    deal = [
        send(gu_ref.at[:, p.up[s]], gu_in_ref.at[p.wa], gu_send.at[s], gu_recv.at[s], wa=p.up[s])
        for s in range(1, wa_size)
    ]
    half_rows = down_ref.shape[0] // 2
    spread = Spread(
        p,
        down_ref,
        lambda d: downs_ref.at[d],
        lambda d, h: downs_ref.at[d, pl.ds(h * half_rows, half_rows)],
        sems[:4],
    )
    spread.start()
    loads = [
        pltpu.make_async_copy(source, target, local.at[3 + i])
        for i, (source, target) in enumerate(
            (
                (prob_any, prob_ref),
                (unpick_any, unpick_ref),
                (act_t_any, act_t_ref),
                (w_all_any, w_all_ref),
            )
        )
    ]
    for copy in loads:
        copy.start()
    rows = dy_ref.shape[0]
    step = ATTEND_ROWS
    head_cols = heads * HEAD
    back_scale = 1.0 / math.sqrt(HEAD)
    d_out_ref[...] = lax.dot_general(
        o_ref[...], dy_ref[...], (((0,), (0,)), ((), ())), preferred_element_type=F32
    ).astype(BF)

    def part_of(device):
        place = pl.ds(pl.multiple_of(device * head_cols, head_cols), head_cols)
        return d_out_ref.at[:, place]

    part_copies = exchange_plane(peers, part_of, lambda d: parts_ref.at[d], part_send, part_recv)
    kept = [
        pltpu.make_async_copy(gu_ref.at[:, p.wa], gu_in_ref.at[p.wa], local.at[0]),
        pltpu.make_async_copy(down_ref, downs_ref.at[p.ctx], local.at[1]),
        pltpu.make_async_copy(part_of(p.ctx), parts_ref.at[p.ctx], local.at[2]),
    ]
    for copy in kept:
        copy.start()

    def project(i, carried):
        place = pl.ds(pl.multiple_of(i * step, step), step)
        do_ref[place, :] = lax.dot_general(
            dy_ref[place, :],
            w_ref[...],
            (((1,), (1,)), ((), ())),
            preferred_element_type=F32,
        ).astype(BF)
        return carried

    lax.fori_loop(0, rows // step, project, 0)
    loads[0].wait()
    dk_ref[...] = jnp.zeros_like(dk_ref)
    dv_ref[...] = jnp.zeros_like(dv_ref)

    def unrotate(u, place):
        return u * cos_ref[place, :] - pltpu.roll(u, HEAD // 2, 1) * sin_ref[place, :]

    for i in range(rows // step):
        here = slice(i * step, (i + 1) * step)
        keys = (i + 1) * step
        for head in range(heads):
            columns = slice(head * HEAD, (head + 1) * HEAD)
            d_o = do_ref[here, columns]
            q = q_ref[here, columns]
            probs = prob_ref[head, here, :keys]
            d_probs = lax.dot_general(
                d_o,
                v_ref[:keys, columns],
                (((1,), (1,)), ((), ())),
                preferred_element_type=F32,
            )
            wide = probs.astype(F32)
            row_dot = jnp.sum(wide * d_probs, axis=-1, keepdims=True)
            d_scores = (wide * (d_probs - row_dot)).astype(BF)
            d_query = jnp.dot(d_scores, k_ref[:keys, columns], preferred_element_type=F32)
            given_ref[here, columns] = unrotate(d_query * back_scale, here).astype(BF)
            dk_ref[:keys, columns] += lax.dot_general(
                d_scores, q, (((0,), (0,)), ((), ())), preferred_element_type=F32
            )
            dv_ref[:keys, columns] += lax.dot_general(
                probs, d_o, (((0,), (0,)), ((), ())), preferred_element_type=F32
            )
    for head in range(heads):
        columns = slice(head * HEAD, (head + 1) * HEAD)
        whole = slice(0, rows)
        d_key = unrotate(dk_ref[:, columns] * back_scale, whole)
        given_ref[:, head_cols + head * HEAD : head_cols + (head + 1) * HEAD] = d_key.astype(BF)
    given_ref[:, 2 * head_cols :] = dv_ref[...].astype(BF)
    arrivals = spread.arrivals()
    next(arrivals)
    next(arrivals)
    for copy in loads[1:]:
        copy.wait()

    def put_back(i, carried):
        place = pl.ds(pl.multiple_of(i * step, step), step)
        grads_ref[place, :] = jnp.dot(
            unpick_ref[place, :], given_ref[...], preferred_element_type=F32
        ).astype(BF)
        return carried

    lax.fori_loop(0, rows // step, put_back, 0)
    own_rows = dh_ref.shape[0]
    own_place = pl.ds(pl.multiple_of(p.ctx * own_rows, own_rows), own_rows)
    dh_ref[...] = jnp.dot(
        unpick_ref[own_place, :], dy_ref[...], preferred_element_type=F32
    ).astype(BF)
    wa_rows = dw_ref.shape[1]

    def weights(i, carried):
        place = pl.ds(pl.multiple_of(i * wa_rows, wa_rows), wa_rows)
        made = jnp.dot(act_t_ref[place, :], grads_ref[...], preferred_element_type=F32)
        dw_ref[i] = made.astype(BF)
        gain_ref[place, :] = jnp.sum(
            made * w_all_ref[place, : 3 * head_cols].astype(F32), axis=-1, keepdims=True
        )
        return carried

    lax.fori_loop(0, wa_size, weights, 0)
    for _ in arrivals:
        pass
    for copy in kept:
        copy.wait()
    spread.finish()
    for copy in deal + part_copies:
        copy.wait()


def attend_back(
    dy, w_rows, o, q, k, v, cosine, sine, probs, act_t, w_all, unpick, gu, down, ctx_size, wa_size
):
    rows, width = dy.shape
    head_cols = o.shape[1]
    heads = head_cols // HEAD
    vmem = pl.BlockSpec(memory_space=pltpu.VMEM)
    anywhere = pl.BlockSpec(memory_space=pl.ANY)
    return pl.pallas_call(
        functools.partial(attend_back_kernel, ctx_size, wa_size, heads),
        out_shape=(
            jax.ShapeDtypeStruct((rows, 3 * head_cols), BF),
            jax.ShapeDtypeStruct((rows // ctx_size, width), BF),
            jax.ShapeDtypeStruct((wa_size, width // wa_size, 3 * head_cols), BF),
            jax.ShapeDtypeStruct((width, 1), F32),
            jax.ShapeDtypeStruct((ctx_size, head_cols, head_cols), BF),
            jax.ShapeDtypeStruct((wa_size, 2) + gu.shape[2:], BF),
            jax.ShapeDtypeStruct((ctx_size,) + down.shape, BF),
        ),
        in_specs=[vmem] * 8 + [anywhere] * 6,
        out_specs=[vmem] * 4 + [anywhere] * 3,
        scratch_shapes=[
            pltpu.VMEM((rows, head_cols), BF),
            pltpu.VMEM((rows, head_cols), F32),
            pltpu.VMEM((rows, head_cols), F32),
            pltpu.VMEM((head_cols, width), BF),
            pltpu.VMEM((rows, 3 * head_cols), BF),
            pltpu.VMEM(probs.shape, BF),
            pltpu.VMEM(act_t.shape, BF),
            pltpu.VMEM(w_all.shape, BF),
            pltpu.VMEM(unpick.shape, BF),
        ]
        + plane_sems(ctx_size)
        + [pltpu.SemaphoreType.DMA((wa_size,))] * 2
        + [pltpu.SemaphoreType.DMA((ctx_size,))] * 2
        + [pltpu.SemaphoreType.DMA((7,))],
        compiler_params=pltpu.CompilerParams(
            collective_id=5, has_side_effects=True, vmem_limit_bytes=VMEM_LIMIT
        ),
        cost_estimate=pl.CostEstimate(
            flops=10 * rows * width * head_cols, bytes_accessed=100_000_000, transcendentals=0
        ),
        name="attend_back",
    )(dy, w_rows, o, q, k, v, cosine, sine, probs, act_t, w_all, unpick, gu, down)


def out_kernel(
    ctx_size,
    wa_size,
    mixed_ref,
    w_ref,
    x_ref,
    gain_ref,
    dz_ref,
    gu_ref,
    hidden_ref,
    acts_ref,
    dzs_ref,
    gw_ref,
    *scratch,
):
    p = place_of(ctx_size, wa_size)
    act_send, act_recv, dz_send, dz_recv, local = scratch[12:]
    greet([p.beside] + p.ahead[1:], [p.up[1], p.down[1]])
    own = pltpu.make_async_copy(gu_ref, gw_ref.at[:, :, p.ctx], local.at[0])
    own.start()
    spread = Spread(
        p,
        gu_ref,
        lambda d: gw_ref.at[:, :, d],
        lambda d, h: gw_ref.at[h, :, d],
        scratch[8:12],
    )
    rows = x_ref.shape[0]

    def part_of(device):
        block = mixed_ref[pl.ds(pl.multiple_of(device * rows, rows), rows), :]
        return jnp.dot(block, w_ref[...], preferred_element_type=F32)

    half_rows = rows // 2

    def pass_on(slots, sems, s, i):
        place = pl.ds(i * half_rows, half_rows)
        return send(
            slots.at[s, place],
            slots.at[s + 1, place],
            sems[0].at[s, i],
            sems[1].at[s, i],
            wa=p.up[1],
        )

    def ring_step(ring, slots, sems, s):
        for i in range(2):
            ring[2 * (s - 1) + i].wait_recv()
            if s < wa_size - 1:
                ring.append(pass_on(slots, sems, s, i))

    dz_sems, act_sems = (dz_send, dz_recv), (act_send, act_recv)
    dzs_ref[0] = dz_ref[...]
    dz_ring = [pass_on(dzs_ref, dz_sems, 0, i) for i in range(2)]
    scatter = Scatter(p, part_of, scratch[:8])
    scatter.start()
    ring_step(dz_ring, dzs_ref, dz_sems, 1)
    hidden = x_ref[...].astype(F32) + scatter.total()
    spread.start()
    hidden_ref[...] = hidden
    scale = lax.rsqrt(jnp.mean(hidden * hidden, axis=-1, keepdims=True) + EPSILON)
    acts_ref[0] = (hidden * scale * gain_ref[...]).astype(BF)
    ring = [pass_on(acts_ref, act_sems, 0, i) for i in range(2)]
    for s in range(2, wa_size):
        ring_step(dz_ring, dzs_ref, dz_sems, s)
    arrivals = spread.arrivals()
    for s in range(1, wa_size):
        ring_step(ring, acts_ref, act_sems, s)
        if s == 2:
            next(arrivals)
            next(arrivals)
    for _ in arrivals:
        pass
    scatter.finish()
    spread.finish()
    own.wait()
    for copy in ring + dz_ring:
        copy.wait_send()


def out_project(mixed, w_rows, x_own, gain, dz, gu, ctx_size, wa_size):
    rows, width = x_own.shape
    vmem = pl.BlockSpec(memory_space=pltpu.VMEM)
    anywhere = pl.BlockSpec(memory_space=pl.ANY)
    return pl.pallas_call(
        functools.partial(out_kernel, ctx_size, wa_size),
        out_shape=(
            jax.ShapeDtypeStruct((rows, width), F32),
            jax.ShapeDtypeStruct((wa_size, rows, width), BF),
            jax.ShapeDtypeStruct((wa_size, rows, width), BF),
            jax.ShapeDtypeStruct((2, wa_size, ctx_size) + gu.shape[2:], BF),
        ),
        in_specs=[vmem] * 5 + [anywhere],
        out_specs=[vmem] * 3 + [anywhere],
        scratch_shapes=scatter_scratch(ctx_size, rows, width)
        + plane_sems(ctx_size)
        + [pltpu.SemaphoreType.DMA((wa_size, 2))] * 4
        + [pltpu.SemaphoreType.DMA((1,))],
        compiler_params=pltpu.CompilerParams(
            collective_id=1, has_side_effects=True, vmem_limit_bytes=VMEM_LIMIT
        ),
        cost_estimate=pl.CostEstimate(
            flops=2 * mixed.size * width, bytes_accessed=200_000_000, transcendentals=0
        ),
        name="out_project",
    )(mixed, w_rows, x_own, gain, dz, gu)


def mlp_kernel(
    act_ref,
    dz_ref,
    gw_any,
    wd_any,
    d_act_ref,
    mlp_ref,
    act_t_ref,
    d_gu_ref,
    inner_t_ref,
    gw_ref,
    wd_ref,
    inner_ref,
    sems,
):
    hidden_rows = wd_any.shape[0]
    hidden = inner_ref.shape[1]
    width = act_ref.shape[1]
    loads = [
        pltpu.make_async_copy(gw_any.at[0], gw_ref.at[0], sems.at[0]),
        pltpu.make_async_copy(gw_any.at[1], gw_ref.at[1], sems.at[1]),
        pltpu.make_async_copy(wd_any, wd_ref.at[pl.ds(0, hidden_rows)], sems.at[2]),
    ]
    for copy in loads:
        copy.start()
    if hidden > hidden_rows:
        wd_ref[hidden_rows:, :] = jnp.zeros((hidden - hidden_rows, width), BF)
    act_t_ref[...] = act_ref[...].T
    for copy in loads:
        copy.wait()
    act = act_ref[...]
    dz = dz_ref[...]

    def part(first, size):
        columns = pl.ds(first, size)
        gate = jnp.dot(act, gw_ref[0, :, columns], preferred_element_type=F32)
        up = jnp.dot(act, gw_ref[1, :, columns], preferred_element_type=F32)
        d_inner = lax.dot_general(
            dz, wd_ref[columns, :], (((1,), (1,)), ((), ())), preferred_element_type=F32
        )
        sigmoid = 1.0 / (1.0 + jnp.exp(-gate))
        silu = gate * sigmoid
        inner = (silu * up).astype(BF)
        inner_ref[:, columns] = inner
        d_gate = (d_inner * up * sigmoid * (1.0 + gate * (1.0 - sigmoid))).astype(BF)
        d_up = (d_inner * silu).astype(BF)
        d_gu_ref[0, :, columns] = d_gate
        d_gu_ref[1, :, columns] = d_up
        inner_t_ref[columns, :] = inner.T

    whole = hidden // CHUNK

    def one(i, carried):
        part(pl.multiple_of(i * CHUNK, CHUNK), CHUNK)
        return carried

    lax.fori_loop(0, whole, one, 0)
    if hidden > whole * CHUNK:
        part(whole * CHUNK, hidden - whole * CHUNK)

    def two(i, carried):
        place = pl.ds(pl.multiple_of(i * CHUNK, CHUNK), CHUNK)
        back = lax.dot_general(
            d_gu_ref[0], gw_ref[0, place, :], (((1,), (1,)), ((), ())), preferred_element_type=F32
        )
        back = back + lax.dot_general(
            d_gu_ref[1], gw_ref[1, place, :], (((1,), (1,)), ((), ())), preferred_element_type=F32
        )
        d_act_ref[:, place] = back.astype(BF)
        mlp_ref[:, place] = jnp.dot(
            inner_ref[...], wd_ref[:, place], preferred_element_type=F32
        ).astype(BF)
        return carried

    lax.fori_loop(0, width // CHUNK, two, 0)


def mlp(act, dz, gw, wd):
    tokens, width = act.shape
    hidden = gw.shape[2]
    vmem = pl.BlockSpec(memory_space=pltpu.VMEM)
    anywhere = pl.BlockSpec(memory_space=pl.ANY)
    return pl.pallas_call(
        mlp_kernel,
        out_shape=(
            jax.ShapeDtypeStruct((tokens, width), BF),
            jax.ShapeDtypeStruct((tokens, width), BF),
            jax.ShapeDtypeStruct((width, tokens), BF),
            jax.ShapeDtypeStruct((2, tokens, hidden), BF),
            jax.ShapeDtypeStruct((hidden, tokens), BF),
        ),
        in_specs=[vmem, vmem, anywhere, anywhere],
        out_specs=[vmem] * 5,
        scratch_shapes=[
            pltpu.VMEM(gw.shape, BF),
            pltpu.VMEM((hidden, width), BF),
            pltpu.VMEM((tokens, hidden), BF),
            pltpu.SemaphoreType.DMA((3,)),
        ],
        compiler_params=pltpu.CompilerParams(vmem_limit_bytes=60 * 1024 * 1024),
        cost_estimate=pl.CostEstimate(
            flops=12 * tokens * width * hidden, bytes_accessed=50_000_000, transcendentals=0
        ),
        name="mlp",
    )(act, dz, gw, wd)


def turn_kernel(
    ctx_size,
    wa_size,
    parts_ref,
    mlp_ref,
    hidden_ref,
    gain_ref,
    dz_ref,
    act_t_ref,
    d_gu_ref,
    inner_t_ref,
    dz_all_ref,
    all_ref,
    gain_out_ref,
    out_ref,
    gu_out_ref,
    down_out_ref,
    *scratch,
):
    p = place_of(ctx_size, wa_size)
    got_ref, more_ref, wa_send, wa_recv, more_send, more_recv = scratch[:6]
    gu_both, gu_got, gu_near, gu_sent, down_both, down_got, down_near, down_sent = scratch[6:14]
    gu_sems, down_sems, spread_sems = scratch[14:18], scratch[18:22], scratch[22:26]
    own_parts, own_mlp, local = scratch[26:29]
    greet([p.beside] + p.ahead[1:], p.down[1:])
    copies = [
        send(parts_ref.at[s], got_ref.at[s], wa_send.at[s], wa_recv.at[s], wa=p.down[s])
        for s in range(1, wa_size)
    ]
    loads = [
        pltpu.make_async_copy(parts_ref.at[0], own_parts, local.at[0]),
        pltpu.make_async_copy(mlp_ref.at[0], own_mlp, local.at[1]),
    ]
    for copy in loads:
        copy.start()
    down_total = down_both.shape[1]
    down_rows = down_total // 2
    columns = dz_all_ref.shape[1] // ctx_size
    half = gu_both.shape[1] // 2
    piece_rows = gu_both.shape[3]
    wa_rows = act_t_ref.shape[0] // wa_size

    def down_piece(ref, chip):
        return ref.at[:, pl.ds(pl.multiple_of(chip * columns, columns), columns)]

    def down_half(ref, chip, h):
        place = pl.ds(h * down_rows, down_rows)
        if chip is None:
            return ref.at[place]
        return ref.at[place, pl.ds(pl.multiple_of(chip * columns, columns), columns)]

    down = Fold(
        p,
        down_both,
        down_got,
        down_near,
        down_sent,
        down_piece,
        down_half,
        lambda into, other: add_rows(into, other, 16),
        down_sems,
    )

    def gu_half(ref, chip, h):
        place = pl.ds(h * half, half)
        return ref.at[place] if chip is None else ref.at[place, chip]

    gu = Fold(
        p,
        gu_both,
        gu_got,
        gu_near,
        gu_sent,
        lambda ref, chip: ref.at[:, chip],
        gu_half,
        add_blocks,
        gu_sems,
    )

    def make(chip):
        first = chip * (2 * piece_rows)
        left = jnp.concatenate(
            [
                act_t_ref[pl.ds(pl.multiple_of(i * wa_rows + first, 2 * piece_rows), 2 * piece_rows), :]
                for i in range(wa_size)
            ],
            axis=0,
        )

        def gu_part(part, carried):
            made = jnp.dot(left, d_gu_ref[part], preferred_element_type=F32).astype(BF)
            for i in range(wa_size):
                for core in range(2):
                    at = (2 * i + core) * piece_rows
                    gu_both[core, part * wa_size + i, chip] = made[at : at + piece_rows]
            return carried

        lax.fori_loop(0, 2, gu_part, 0)

        def down_part(core, carried):
            place = pl.multiple_of((core * p.chips + chip) * columns, columns)
            made = jnp.dot(
                inner_t_ref[...], dz_all_ref[:, pl.ds(place, columns)], preferred_element_type=F32
            ).astype(BF)
            target = pl.ds(pl.multiple_of(chip * columns, columns), columns)
            down_both[core, :, target] = made[:down_total]
            return carried

        lax.fori_loop(0, 2, down_part, 0)

    for i in range(p.chips):
        make(gu.order[i])
        gu.start(i)
        down.start(i)
        if i > 0:
            gu.between(i - 1)
            down.between(i - 1)
    gu.between(p.chips - 1)
    down.between(p.chips - 1)
    hidden = hidden_ref[...]
    scale = lax.rsqrt(jnp.mean(hidden * hidden, axis=-1, keepdims=True) + EPSILON)
    down.onward()
    for copy in loads:
        copy.wait()
    d_normed = own_parts[...].astype(F32)
    for s in range(1, wa_size):
        copies[s - 1].wait_recv()
        d_normed = d_normed + got_ref[s].astype(F32)
    more = [
        send(mlp_ref.at[s], more_ref.at[s], more_send.at[s], more_recv.at[s], wa=p.down[s])
        for s in range(1, wa_size)
    ]
    gain_out_ref[...] = jnp.sum(d_normed * (hidden * scale), axis=0, keepdims=True)
    d_hidden = norm_back(hidden, scale, gain_ref[...], d_normed, dz_ref[...].astype(F32))
    all_ref[p.ctx] = d_hidden.astype(BF)
    half_rows = all_ref.shape[1] // 2
    spread = Spread(
        p,
        all_ref.at[p.ctx],
        lambda d: all_ref.at[d],
        lambda d, h: all_ref.at[d, pl.ds(h * half_rows, half_rows)],
        spread_sems,
    )
    spread.start()
    gu.onward()
    down_out_ref[...] = down.total()[...]
    for _ in spread.arrivals():
        pass
    gu_out_ref[...] = gu.total()[...]
    result = hidden + own_mlp[...].astype(F32)
    for s in range(1, wa_size):
        more[s - 1].wait_recv()
        result = result + more_ref[s].astype(F32)
    out_ref[...] = result.astype(BF)
    for copy in copies + more:
        copy.wait_send()
    down.finish()
    gu.finish()
    spread.finish()


def turn(
    parts, mlp, hidden, gain, dz, act_t, d_gu, inner_t, dz_all, hidden_rows, ctx_size, wa_size
):
    rows, width = hidden.shape
    chips = ctx_size // 2
    columns = width // ctx_size
    lead = 2 * wa_size
    gu_rows, gu_columns = width // (ctx_size * wa_size), d_gu.shape[2]
    vmem = pl.BlockSpec(memory_space=pltpu.VMEM)
    anywhere = pl.BlockSpec(memory_space=pl.ANY)
    many = 2 if chips == 4 else chips - 1
    return pl.pallas_call(
        functools.partial(turn_kernel, ctx_size, wa_size),
        out_shape=(
            jax.ShapeDtypeStruct((ctx_size, rows, width), BF),
            jax.ShapeDtypeStruct((1, width), F32),
            jax.ShapeDtypeStruct((rows, width), BF),
            jax.ShapeDtypeStruct((lead, gu_rows, gu_columns), BF),
            jax.ShapeDtypeStruct((hidden_rows, columns), BF),
        ),
        in_specs=[anywhere] * 2 + [vmem] * 7,
        out_specs=[vmem] * 5,
        scratch_shapes=[pltpu.VMEM((wa_size, rows, width), BF)] * 2
        + [pltpu.SemaphoreType.DMA((wa_size,))] * 4
        + [
            pltpu.VMEM((2, lead, chips, gu_rows, gu_columns), BF),
            pltpu.VMEM((lead, chips, gu_rows, gu_columns), BF),
            pltpu.VMEM((2, lead // 2, gu_rows, gu_columns), BF),
            pltpu.VMEM((many, lead, gu_rows, gu_columns), BF),
            pltpu.VMEM((2, hidden_rows, columns * chips), BF),
            pltpu.VMEM((hidden_rows, columns * chips), BF),
            pltpu.VMEM((2, hidden_rows // 2, columns), BF),
            pltpu.VMEM((many, hidden_rows, columns), BF),
        ]
        + [pltpu.SemaphoreType.DMA((max(chips, 6),))] * 8
        + plane_sems(ctx_size)
        + [pltpu.VMEM((rows, width), BF)] * 2
        + [pltpu.SemaphoreType.DMA((2,))],
        compiler_params=pltpu.CompilerParams(
            collective_id=2, has_side_effects=True, vmem_limit_bytes=VMEM_LIMIT
        ),
        cost_estimate=pl.CostEstimate(flops=0, bytes_accessed=200_000_000, transcendentals=0),
        name="turn",
    )(parts, mlp, hidden, gain, dz, act_t, d_gu, inner_t, dz_all)


def close_kernel(
    ctx_size,
    wa_size,
    grads_ref,
    w_ref,
    x_ref,
    gain_ref,
    dh_ref,
    gu_in,
    dw_ref,
    do_parts,
    gains_ref,
    out_ref,
    gus_ref,
    qkvs_ref,
    outs_ref,
    sums_ref,
    *scratch,
):
    p = place_of(ctx_size, wa_size)
    rows_ref, dw_in, share_ref, do_in, out_share_ref = scratch[8:13]
    wa_gains, ctx_gains, local = scratch[13:16]
    dw_sems, do_sems = scratch[16:18], scratch[18:20]
    wa_sems, ctx_sems = scratch[20:22], scratch[22:24]
    gu_plane, qkv_plane, out_plane = (scratch[i : i + 4] for i in (24, 28, 32))
    peers = [lax.rem(p.ctx + i, ctx_size) for i in range(1, ctx_size)]
    greet(peers, p.up[1:])
    locals_ = []

    def keep(source, target):
        copy = pltpu.make_async_copy(source, target, local.at[len(locals_)])
        copy.start()
        locals_.append(copy)

    def spread_of(own, slots, sems):
        half = slots.shape[1] // 2
        keep(own, slots.at[p.ctx])
        spread = Spread(
            p,
            own,
            lambda d: slots.at[d],
            lambda d, h: slots.at[d, pl.ds(h * half, half)],
            sems,
        )
        spread.start()
        return spread

    def over_wa(source, target, sems):
        return [
            send(
                source(p.up[s]),
                target.at[s],
                sems[0].at[s],
                sems[1].at[s],
                wa=p.up[s],
            )
            for s in range(1, wa_size)
        ]

    def add_up(found, into, step):
        def one(i, carried):
            place = pl.ds(pl.multiple_of(i * step, step), step)
            total = found[0, place, :].astype(F32)
            for s in range(1, wa_size):
                total = total + found[s, place, :].astype(F32)
            into[place, :] = total.astype(BF)
            return carried

        lax.fori_loop(0, into.shape[0] // step, one, 0)

    per_wa = ctx_size // wa_size

    def do_block(device):
        return do_parts.at[pl.ds(device * per_wa, per_wa)]

    do_copies = over_wa(do_block, do_in, do_sems)
    own_loads = [
        pltpu.make_async_copy(do_block(p.wa), do_in.at[0], local.at[3]),
        pltpu.make_async_copy(dw_ref.at[p.wa], dw_in.at[0], local.at[4]),
    ]
    for copy in own_loads:
        copy.start()
    rows = x_ref.shape[0]
    qkv_columns = grads_ref.shape[1]

    def part_of(device):
        place = pl.ds(pl.multiple_of(device * rows, rows), rows)
        return lax.dot_general(
            grads_ref[place, :],
            w_ref[:, :qkv_columns],
            (((1,), (1,)), ((), ())),
            preferred_element_type=F32,
        )

    scatter = Scatter(p, part_of, scratch[:8])
    scatter.start()
    wa_gains[p.wa] = gains_ref[...]
    small = [
        send(gains_ref, wa_gains.at[p.wa], wa_sems[0].at[s], wa_sems[1].at[s], wa=p.up[s])
        for s in range(1, wa_size)
    ]
    total_columns = rows_ref.shape[1] // 2
    own_columns = total_columns // wa_size
    for i in range(wa_size):
        for part in range(2):
            first = part * total_columns + i * own_columns
            rows_ref[:, first : first + own_columns] = gu_in[i, part, :, :own_columns]
    gu_spread = spread_of(rows_ref, gus_ref, gu_plane)
    for copy in small:
        copy.wait()
    plane_gain = wa_gains[0]
    for i in range(1, wa_size):
        plane_gain = plane_gain + wa_gains[i]
    ctx_gains[p.ctx] = plane_gain
    own_gain = ctx_gains.at[p.ctx]
    small = [
        send(own_gain, own_gain, ctx_sems[0].at[i], ctx_sems[1].at[i], ctx=peer)
        for i, peer in enumerate(peers)
    ]
    for copy in do_copies:
        copy.wait_recv()
    dw_copies = over_wa(lambda d: dw_ref.at[d], dw_in, dw_sems)
    own_loads[0].wait()
    for i in range(per_wa):
        place = pl.ds(i * do_parts.shape[1], do_parts.shape[1])
        total = do_in[0, i].astype(F32)
        for s in range(1, wa_size):
            total = total + do_in[s, i].astype(F32)
        out_share_ref[place, :] = total.astype(BF)
    out_spread = spread_of(out_share_ref, outs_ref, out_plane)
    x = x_ref[...].astype(F32)
    scale = lax.rsqrt(jnp.mean(x * x, axis=-1, keepdims=True) + EPSILON)
    d_normed = scatter.total()
    out_ref[...] = norm_back(
        x, scale, gain_ref[...], d_normed, dh_ref[...].astype(F32)
    ).astype(BF)
    for _ in out_spread.arrivals():
        pass
    for _ in gu_spread.arrivals():
        pass
    for copy in small:
        copy.wait()
    total_gain = ctx_gains[0]
    for i in range(1, ctx_size):
        total_gain = total_gain + ctx_gains[i]
    sums_ref[...] = total_gain
    for copy in dw_copies:
        copy.wait_recv()
    own_loads[1].wait()
    add_up(dw_in, share_ref, 16)
    qkv_spread = spread_of(share_ref, qkvs_ref, qkv_plane)
    for _ in qkv_spread.arrivals():
        pass
    scatter.finish()
    for spread in (gu_spread, qkv_spread, out_spread):
        spread.finish()
    for copy in dw_copies + do_copies:
        copy.wait_send()
    for copy in locals_:
        copy.wait()


def close(grads, w, x_own, gain, dh, gu, dw, do, gains_own, columns, ctx_size, wa_size):
    rows, width = x_own.shape
    vmem = pl.BlockSpec(memory_space=pltpu.VMEM)
    anywhere = pl.BlockSpec(memory_space=pl.ANY)
    gu_shape = (gu.shape[2], columns)
    out_shape = (width // wa_size, do.shape[1])
    shapes = [gu_shape, dw.shape[1:], out_shape]
    gains = (2, width)
    return pl.pallas_call(
        functools.partial(close_kernel, ctx_size, wa_size),
        out_shape=(jax.ShapeDtypeStruct((rows, width), BF),)
        + tuple(jax.ShapeDtypeStruct((ctx_size,) + shape, BF) for shape in shapes)
        + (jax.ShapeDtypeStruct(gains, F32),),
        in_specs=[vmem] * 6 + [anywhere] * 2 + [vmem],
        out_specs=[vmem] + [anywhere] * 3 + [vmem],
        scratch_shapes=scatter_scratch(ctx_size, rows, width)
        + [
            pltpu.VMEM(gu_shape, BF),
            pltpu.VMEM(dw.shape, BF),
            pltpu.VMEM(dw.shape[1:], BF),
            pltpu.VMEM((wa_size, ctx_size // wa_size) + do.shape[1:], BF),
            pltpu.VMEM(out_shape, BF),
            pltpu.VMEM((wa_size,) + gains, F32),
            pltpu.VMEM((ctx_size,) + gains, F32),
            pltpu.SemaphoreType.DMA((5,)),
        ]
        + [pltpu.SemaphoreType.DMA((wa_size,))] * 6
        + [pltpu.SemaphoreType.DMA((ctx_size,))] * 2
        + plane_sems(ctx_size) * 3,
        compiler_params=pltpu.CompilerParams(
            collective_id=3, has_side_effects=True, vmem_limit_bytes=VMEM_LIMIT
        ),
        cost_estimate=pl.CostEstimate(
            flops=2 * grads.size * width, bytes_accessed=400_000_000, transcendentals=0
        ),
        name="close",
    )(grads, w, x_own, gain, dh, gu, dw, do, gains_own)


def widen(blocks, columns, order, step):
    count, rows, own = blocks.shape
    parts = own // columns

    def body(block_ref, out_ref):
        for i in range(parts):
            for at, device in enumerate(order):
                first = (i * count + at) * columns
                out_ref[:, first : first + columns] = block_ref[
                    device, :, i * columns : (i + 1) * columns
                ].astype(F32)

    return pl.pallas_call(
        body,
        out_shape=jax.ShapeDtypeStruct((rows, count * own), F32),
        grid=(rows // step,),
        in_specs=[pl.BlockSpec((count, step, own), lambda r: (0, r, 0))],
        out_specs=pl.BlockSpec((step, count * own), lambda r: (r, 0)),
        compiler_params=pltpu.CompilerParams(vmem_limit_bytes=VMEM_LIMIT),
        name="widen",
    )(blocks)


def per_device(
    tokens, lengths, dealing, norm1_gain, w_qkv, w_out, norm2_gain, w_gate_up, w_down, grad_out
):
    tok_rows, width = tokens.shape[1], tokens.shape[2]
    ctx_size = lax.axis_size("ctx")
    wa_size = lax.axis_size("wa")
    ctx_index = lax.axis_index("ctx")
    wa_index = lax.axis_index("wa")
    block_order = dealing[0]
    block_total = block_order.shape[0]
    group_rows = block_total * BLOCK
    own_blocks = tok_rows // BLOCK
    first_length = lengths[0, 0]
    heads_own = HEADS // ctx_size
    head_cols = heads_own * HEAD
    wa_rows = width // wa_size
    ff_total = w_gate_up.shape[1] // 2
    ff_own = w_down.shape[0]
    piece_rows = wa_rows // ctx_size

    own_cols = jnp.concatenate(
        [
            lax.dynamic_slice_in_dim(w_qkv, part * width + ctx_index * head_cols, head_cols, 1)
            for part in range(3)
        ]
        + [lax.dynamic_slice_in_dim(w_out, ctx_index * head_cols, head_cols, 1)],
        axis=1,
    )
    dealt, all_cols, gu_send = gather_both(
        tokens[0], own_cols, w_gate_up, ff_own, ctx_size, wa_size
    )
    dealt = dealt.reshape(group_rows, width)
    all_cols = all_cols.reshape(width, 4 * head_cols)

    rows_given = jnp.arange(group_rows, dtype=jnp.int32)
    segments = (rows_given >= first_length).astype(jnp.int32)
    in_block = jnp.arange(BLOCK, dtype=jnp.int32)
    rows_dealt = (block_order[:, None] * BLOCK + in_block[None, :]).reshape(group_rows)
    unpick = (rows_dealt[:, None] == rows_given[None, :]).astype(BF)
    pick = (rows_given[:, None] == rows_dealt[None, :]).astype(BF)
    given_tables = rotary_tables(rows_given - segments * first_length)
    dealt_tables = rotary_tables(
        rows_dealt - (rows_dealt >= first_length).astype(jnp.int32) * first_length
    )
    act_one_t, own_given, query_b, key_b, value_b, mixed_b, probs_b, gu_mine, out_rows = attend(
        segments,
        dealt,
        all_cols,
        norm1_gain[None, :],
        pick,
        *dealt_tables,
        gu_send,
        ctx_size,
        wa_size,
    )
    gain_two = norm2_gain[None, :]
    hidden, acts, grads_all, gu_weight = out_project(
        mixed_b, out_rows, own_given, gain_two, grad_out[0], gu_mine, ctx_size, wa_size
    )
    gu_weight = gu_weight.reshape(2, width, gu_weight.shape[4])
    act_two = acts.reshape(wa_size * tok_rows, width)
    cotangent = grads_all.reshape(wa_size * tok_rows, width)

    d_act, mlp_parts, act_t, d_gu, inner_t = mlp(act_two, cotangent, gu_weight, w_down)
    d_branches, gain_two_part, out_given, gu_piece_grad, down_piece_grad = turn(
        d_act.reshape(wa_size, tok_rows, width),
        mlp_parts.reshape(wa_size, tok_rows, width),
        hidden,
        gain_two,
        grad_out[0],
        act_t,
        d_gu,
        inner_t,
        cotangent,
        ff_own,
        ctx_size,
        wa_size,
    )
    d_branch_b = d_branches.reshape(group_rows, width)
    dealt_qkv, d_hidden_dealt, qkv_parts, gain_column, out_parts, gu_pieces, downs = attend_back(
        d_branch_b,
        out_rows,
        mixed_b,
        query_b,
        key_b,
        value_b,
        *given_tables,
        probs_b,
        act_one_t,
        all_cols,
        unpick,
        gu_piece_grad.reshape((2, wa_size) + gu_piece_grad.shape[1:]),
        down_piece_grad,
        ctx_size,
        wa_size,
    )
    gain_one_part = gain_column.reshape(1, width) / norm1_gain[None, :]
    d_tokens, gus, qkvs, outs, gain_sums = close(
        dealt_qkv,
        all_cols,
        tokens[0],
        norm1_gain[None, :],
        d_hidden_dealt,
        gu_pieces,
        qkv_parts,
        out_parts,
        jnp.concatenate([gain_one_part, gain_two_part], axis=0),
        2 * ff_total,
        ctx_size,
        wa_size,
    )
    d_gate_up = gus.reshape(wa_rows, 2 * ff_total).astype(F32)
    in_order = list(range(ctx_size))
    by_core = in_order[0::2] + in_order[1::2]
    d_down = widen(downs, downs.shape[2], by_core, ff_own // 2 if ff_own % 32 == 0 else ff_own)
    d_qkv = widen(qkvs, head_cols, in_order, 64)
    d_out = widen(outs, head_cols, in_order, 128)
    return (
        out_given[None],
        d_tokens[None],
        gain_sums[0],
        d_qkv,
        d_out,
        gain_sums[1],
        d_gate_up,
        d_down,
    )


def solution(mesh):
    in_specs = (
        P("wa", "ctx", None),
        P("wa", None),
        P("wa", None),
        P(),
        P("wa", None),
        P("wa", None),
        P(),
        P("wa", None),
        P("wa", None),
        P("wa", "ctx", None),
    )
    out_specs = (
        P("wa", "ctx", None),
        P("wa", "ctx", None),
        P(),
        P("wa", None),
        P("wa", None),
        P(),
        P("wa", None),
        P("wa", None),
    )
    return jax.shard_map(
        per_device, mesh=mesh, in_specs=in_specs, out_specs=out_specs, check_vma=False
    )
```

```python
import functools
import math
import types

import jax
import jax.numpy as jnp
import numpy as np
from jax import lax
from jax.experimental import pallas as pl
from jax.experimental.pallas import tpu as pltpu
from jax.sharding import PartitionSpec as P

HEADS = 16
HEAD = 128
WINDOW = 2048
BLOCK = 128

EPSILON = 1e-06
BF = jnp.bfloat16
F32 = jnp.float32
VMEM_LIMIT = 60 * 1024 * 1024
ATTEND_ROWS = 256
CHUNK = 256


MESH = pl.DeviceIdType.MESH


def greet(ctx_peers, wa_peers):
    barrier = pltpu.get_barrier_semaphore()
    for peer in ctx_peers:
        pl.semaphore_signal(barrier, inc=1, device_id={"ctx": peer}, device_id_type=MESH)
    for peer in wa_peers:
        pl.semaphore_signal(barrier, inc=1, device_id={"wa": peer}, device_id_type=MESH)
    pl.semaphore_wait(barrier, len(ctx_peers) + len(wa_peers))


def send(source, target, send_sem, recv_sem, **peer):
    copy = pltpu.make_async_remote_copy(
        src_ref=source,
        dst_ref=target,
        send_sem=send_sem,
        recv_sem=recv_sem,
        device_id=peer,
        device_id_type=MESH,
    )
    copy.start()
    return copy


def place_of(ctx_size, wa_size):
    chips = ctx_size // 2
    p = types.SimpleNamespace(ctx_size=ctx_size, wa_size=wa_size, chips=chips)
    p.ctx, p.wa = lax.axis_index("ctx"), lax.axis_index("wa")
    p.core, p.chip = lax.rem(p.ctx, 2), lax.div(p.ctx, 2)
    p.beside = p.chip * 2 + 1 - p.core
    p.ahead = [lax.rem(p.chip + m, chips) * 2 + p.core for m in range(chips)]
    p.behind = [lax.rem(p.chip + chips - m, chips) * 2 + p.core for m in range(chips)]
    p.up = [lax.rem(p.wa + s, wa_size) for s in range(wa_size)]
    p.down = [lax.rem(p.wa + wa_size - s, wa_size) for s in range(wa_size)]
    p.square = chips == 4
    if p.square:
        p.near = [p.chip + 1 - 2 * lax.rem(p.chip, 2), lax.rem(p.chip + 2, 4)]
        p.far = 3 - p.chip
    return p


def on_core(p, chip):
    return chip * 2 + p.core


def off_core(p, chip):
    return chip * 2 + 1 - p.core


def plane_sems(ctx_size):
    count = max(ctx_size // 2, 5)
    return [pltpu.SemaphoreType.DMA((count,))] * 4


class Spread:
    def __init__(self, p, own, slot, half, sems):
        self.p, self.own, self.slot, self.half = p, own, slot, half
        self.chip_send, self.chip_recv, self.side_send, self.side_recv = sems
        self.chip, self.side = [], []

    def across(self, source, target, chip):
        i = len(self.chip)
        self.chip.append(
            send(source, target, self.chip_send.at[i], self.chip_recv.at[i], ctx=on_core(self.p, chip))
        )

    def aside(self, source, target):
        i = len(self.side)
        self.side.append(
            send(source, target, self.side_send.at[i], self.side_recv.at[i], ctx=self.p.beside)
        )

    def start(self):
        p = self.p
        target = self.slot(p.ctx)
        if p.square:
            for chip in p.near:
                self.across(self.own, target, chip)
        else:
            for m in range(1, p.chips):
                self.across(self.own, target, lax.rem(p.chip + m, p.chips))
        self.aside(self.own, target)

    def arrivals(self):
        p = self.p
        if not p.square:
            for m in range(1, p.chips):
                self.chip[m - 1].wait_recv()
                block = self.slot(p.behind[m])
                self.aside(block, block)
                yield p.behind[m]
            self.side[0].wait_recv()
            yield p.beside
            for m in range(1, p.chips):
                self.side[m].wait_recv()
                yield off_core(p, lax.rem(p.chip + p.chips - m, p.chips))
            return
        for i in range(2):
            self.chip[i].wait_recv()
            device = on_core(p, p.near[i])
            part = self.half(device, i)
            self.across(part, part, p.near[1 - i])
            self.aside(self.slot(device), self.slot(device))
            yield device
        self.side[0].wait_recv()
        yield p.beside
        for i in range(2):
            self.side[1 + i].wait_recv()
            yield off_core(p, p.near[i])
        device = on_core(p, p.far)
        for i in range(2):
            self.chip[2 + i].wait_recv()
            part = self.half(device, i)
            self.aside(part, part)
        yield device
        for i in range(2):
            self.side[3 + i].wait_recv()
        yield off_core(p, p.far)

    def finish(self):
        for copy in self.chip + self.side:
            copy.wait_send()


class Fold:
    def __init__(self, p, both, got, near, sent, piece, half, add, sems):
        self.p, self.both, self.got, self.near, self.sent = p, both, got, near, sent
        self.kept = both.at[p.core]
        self.piece, self.half, self.add = piece, half, add
        self.chip_send, self.chip_recv, self.side_send, self.side_recv = sems
        self.chip, self.side = [], []
        if p.square:
            self.order = [p.far] + p.near + [p.chip]
        else:
            self.order = [lax.rem(p.chip + m, p.chips) for m in range(1, p.chips)] + [p.chip]

    def across(self, source, target, chip):
        i = len(self.chip)
        self.chip.append(
            send(source, target, self.chip_send.at[i], self.chip_recv.at[i], ctx=on_core(self.p, chip))
        )

    def start(self, i):
        p = self.p
        chip = self.order[i]
        self.side.append(
            send(
                self.piece(self.both.at[1 - p.core], chip),
                self.piece(self.got, chip),
                self.side_send.at[i],
                self.side_recv.at[i],
                ctx=p.beside,
            )
        )

    def between(self, i):
        p = self.p
        chip = self.order[i]
        self.side[i].wait_recv()
        self.add(self.piece(self.kept, chip), self.piece(self.got, chip))
        if i == p.chips - 1:
            return
        if not p.square:
            self.across(self.piece(self.kept, chip), self.sent.at[i], chip)
        elif i == 0:
            for j in range(2):
                self.across(self.half(self.kept, chip, j), self.near.at[j], p.near[j])
        else:
            j = i - 1
            self.across(self.half(self.kept, chip, j), self.half(self.sent.at[j], None, j), chip)

    def onward(self):
        p = self.p
        if not p.square:
            return
        for i in range(2):
            self.chip[i].wait_recv()
            part = self.half(self.kept, p.near[1 - i], i)
            self.add(part, self.near.at[i])
            self.across(part, self.half(self.sent.at[1 - i], None, i), p.near[1 - i])

    def total(self):
        p = self.p
        for copy in self.chip[2:] if p.square else self.chip:
            copy.wait_recv()
        mine = self.piece(self.kept, p.chip)
        for i in range(2 if p.square else p.chips - 1):
            self.add(mine, self.sent.at[i])
        return mine

    def finish(self):
        for copy in self.side + self.chip:
            copy.wait_send()


def add_rows(into, other, step):
    def one(i, carried):
        place = pl.ds(pl.multiple_of(i * step, step), step)
        into[place, :] = (into[place, :].astype(F32) + other[place, :].astype(F32)).astype(BF)
        return carried

    lax.fori_loop(0, into.shape[0] // step, one, 0)


def add_blocks(into, other):
    lead = into.shape[:-2]

    def one(i, carried):
        at = (i,) if len(lead) == 1 else (i // lead[1], i % lead[1])
        into[at] = (into[at].astype(F32) + other[at].astype(F32)).astype(BF)
        return carried

    lax.fori_loop(0, math.prod(lead), one, 0)


class Scatter:
    def __init__(self, p, part_of, refs):
        self.p, self.part_of, self.refs = p, part_of, refs

    def start(self):
        p = self.p
        side_out, side_in, chip_out, chip_in, side_send, side_recv, chip_send, chip_recv = self.refs
        self.side, self.out = [], []
        order = list(range(1, p.chips)) + [0]
        for m in order:
            side_out[m] = self.part_of(lax.div(p.ahead[m], 2) * 2 + 1 - p.core).astype(BF)
            self.side.append(
                send(side_out.at[m], side_in.at[m], side_send.at[m], side_recv.at[m], ctx=p.beside)
            )
        for i, m in enumerate(order):
            mine = self.part_of(p.ahead[m])
            self.side[i].wait_recv()
            self.kept = mine + side_in[m].astype(F32)
            if m > 0:
                chip_out[m - 1] = self.kept.astype(BF)
                self.out.append(
                    send(
                        chip_out.at[m - 1],
                        chip_in.at[m - 1],
                        chip_send.at[m - 1],
                        chip_recv.at[m - 1],
                        ctx=p.ahead[m],
                    )
                )

    def total(self):
        chip_in = self.refs[3]
        total = self.kept
        for m in range(1, self.p.chips):
            self.out[m - 1].wait_recv()
            total = total + chip_in[m - 1].astype(F32)
        return total

    def finish(self):
        for copy in self.side + self.out:
            copy.wait_send()


def scatter_scratch(ctx_size, rows, width):
    chips = ctx_size // 2
    return [
        pltpu.VMEM((chips, rows, width), BF),
        pltpu.VMEM((chips, rows, width), BF),
        pltpu.VMEM((chips - 1, rows, width), BF),
        pltpu.VMEM((chips - 1, rows, width), BF),
    ] + [pltpu.SemaphoreType.DMA((chips,))] * 4


def norm_back(x, scale, gain, d_scaled, d_other):
    normed = x * scale
    scaled = d_scaled * gain
    return d_other + scale * (
        scaled - normed * jnp.mean(scaled * normed, axis=-1, keepdims=True)
    )


def gather_kernel(
    ctx_size,
    wa_size,
    cuts,
    own_columns,
    x_ref,
    w_ref,
    gu_ref,
    dealt_column_ref,
    length_ref,
    freq_ref,
    xs_ref,
    ws_ref,
    cut_ref,
    tables_ref,
    *scratch,
):
    p = place_of(ctx_size, wa_size)
    ring_send, ring_recv, local, piece_ref = scratch[4:]
    greet([p.beside] + p.ahead[1:], [p.up[1], p.down[1]])
    rows = w_ref.shape[0] // cuts
    half_rows = x_ref.shape[0] // 2
    ring = []
    for i in range(cuts):
        part = pl.ds(i * rows, rows)
        ring.append(
            send(
                w_ref.at[part],
                ws_ref.at[p.wa, part],
                ring_send.at[0, i],
                ring_recv.at[0, i],
                wa=p.up[1],
            )
        )
    spread = Spread(
        p,
        x_ref,
        lambda d: xs_ref.at[d],
        lambda d, h: xs_ref.at[d, pl.ds(h * half_rows, half_rows)],
        scratch[:4],
    )
    spread.start()
    piece_rows = piece_ref.shape[0]
    place = pl.ds(pl.multiple_of(p.ctx * piece_rows, piece_rows), piece_rows)
    loads = [
        pltpu.make_async_copy(x_ref, xs_ref.at[p.ctx], local.at[0]),
        pltpu.make_async_copy(w_ref, ws_ref.at[p.wa], local.at[1]),
        pltpu.make_async_copy(gu_ref.at[place], piece_ref, local.at[2]),
    ]
    for copy in loads:
        copy.start()
    loads[2].wait()
    total = piece_ref.shape[1] // 2
    hidden = cut_ref.shape[3]
    for to in range(wa_size):
        for part in range(2):
            first = part * total + to * own_columns
            cut_ref[to, part, :, :own_columns] = piece_ref[:, first : first + own_columns]
            if hidden > own_columns:
                cut_ref[to, part, :, own_columns:] = jnp.zeros(
                    (piece_rows, hidden - own_columns), BF
                )
    group_rows = tables_ref.shape[2]
    table_rows = min(group_rows, 256)
    first_length = length_ref[:, 0:1]
    lane = lax.broadcasted_iota(jnp.int32, (table_rows, HEAD), 1)
    sign = jnp.where(lane < HEAD // 2, -1.0, 1.0)

    def tables(i, carried):
        place = pl.ds(pl.multiple_of(i * table_rows, table_rows), table_rows)
        given = lax.broadcasted_iota(jnp.int32, (table_rows, 1), 0) + i * table_rows
        for kind, row in enumerate((dealt_column_ref[place, :], given)):
            position = row - jnp.where(row >= first_length, first_length, 0)
            angle = position.astype(F32) * freq_ref[...]
            tables_ref[kind, 0, place, :] = jnp.cos(angle)
            tables_ref[kind, 1, place, :] = jnp.sin(angle) * sign
        return carried

    late = []
    for step in range(1, wa_size):
        for i in range(cuts):
            ring[i].wait_recv()
            late.append(ring[i])
            if step < wa_size - 1:
                block = ws_ref.at[p.down[step], pl.ds(i * rows, rows)]
                ring[i] = send(
                    block, block, ring_send.at[step, i], ring_recv.at[step, i], wa=p.up[1]
                )
        if step == 1:
            for _ in spread.arrivals():
                pass
        if step == 2 or wa_size == 2:
            lax.fori_loop(0, group_rows // table_rows, tables, 0)
    for copy in late:
        copy.wait_send()
    spread.finish()
    for copy in loads[:2]:
        copy.wait()


def gather_both(x, w, gu, dealt_column, length, own_columns, ctx_size, wa_size, cuts=4):
    anywhere = pl.BlockSpec(memory_space=pl.ANY)
    piece_rows = w.shape[0] // ctx_size
    hidden = -(-own_columns // 128) * 128
    half = np.arange(HEAD) % (HEAD // 2)
    freq = (10000.0 ** (-2.0 * half / HEAD)).astype(np.float32)[None, :]
    vmem = pl.BlockSpec(memory_space=pltpu.VMEM)
    return pl.pallas_call(
        functools.partial(gather_kernel, ctx_size, wa_size, cuts, own_columns),
        out_shape=(
            jax.ShapeDtypeStruct((ctx_size,) + x.shape, x.dtype),
            jax.ShapeDtypeStruct((wa_size,) + w.shape, w.dtype),
            jax.ShapeDtypeStruct((wa_size, 2, piece_rows, hidden), BF),
            jax.ShapeDtypeStruct((2, 2, dealt_column.shape[0], HEAD), F32),
        ),
        in_specs=[anywhere] * 3 + [vmem] * 3,
        out_specs=[anywhere] * 2 + [vmem] * 2,
        scratch_shapes=plane_sems(ctx_size)
        + [pltpu.SemaphoreType.DMA((wa_size - 1, cuts))] * 2
        + [pltpu.SemaphoreType.DMA((3,)), pltpu.VMEM((piece_rows, gu.shape[1]), BF)],
        compiler_params=pltpu.CompilerParams(
            collective_id=0, has_side_effects=True, vmem_limit_bytes=VMEM_LIMIT
        ),
        cost_estimate=pl.CostEstimate(flops=0, bytes_accessed=200_000_000, transcendentals=0),
        name="gather_both",
    )(x, w, gu, dealt_column, length, jnp.asarray(freq))


def exchange_plane(peers, source, target, send_sem, recv_sem):
    here = target(peers[0])
    return [
        send(source(peer), here, send_sem.at[i], recv_sem.at[i], ctx=peer)
        for i, peer in enumerate(peers)
        if i > 0
    ]


def attend_kernel(
    ctx_size,
    wa_size,
    heads,
    length_ref,
    x_ref,
    w_ref,
    gain_ref,
    dealt_row_ref,
    tables_ref,
    gu_ref,
    act_t_ref,
    own_ref,
    q_ref,
    k_ref,
    v_ref,
    o_ref,
    prob_ref,
    gw_ref,
    rows_ref,
    gu_send,
    gu_recv,
    local,
    out_send,
    out_recv,
    dealt_ref,
):
    wa, ctx = lax.axis_index("wa"), lax.axis_index("ctx")
    up = [lax.rem(wa + s, wa_size) for s in range(wa_size)]
    peers = [lax.rem(ctx + i, ctx_size) for i in range(ctx_size)]
    greet(peers[1:], up[1:])
    head_cols = heads * HEAD

    def columns_of(d):
        rows = pl.ds(pl.multiple_of(d * head_cols, head_cols), head_cols)
        return w_ref.at[rows, pl.ds(3 * head_cols, head_cols)]

    def rows_of(d):
        return rows_ref.at[:, pl.ds(pl.multiple_of(d * head_cols, head_cols), head_cols)]

    deal_out = exchange_plane(peers, columns_of, rows_of, out_send, out_recv)
    own_out = pltpu.make_async_copy(columns_of(ctx), rows_of(ctx), local.at[1])
    own_out.start()
    deal = [
        send(gu_ref.at[up[s]], gw_ref.at[:, wa], gu_send.at[s], gu_recv.at[s], wa=up[s])
        for s in range(1, wa_size)
    ]
    own = pltpu.make_async_copy(gu_ref.at[wa], gw_ref.at[:, wa], local.at[0])
    own.start()
    rows = x_ref.shape[0]
    step = ATTEND_ROWS

    def project(i, carried):
        place = pl.ds(pl.multiple_of(i * step, step), step)
        x = x_ref[place, :].astype(F32)
        scale = lax.rsqrt(jnp.mean(x * x, axis=-1, keepdims=True) + EPSILON)
        act = (x * scale * gain_ref[...]).astype(BF)
        act_t_ref[:, place] = act.T
        made = jnp.dot(act, w_ref[:, : 3 * head_cols], preferred_element_type=F32)
        cosine, sine = tables_ref[0, place, :], tables_ref[1, place, :]
        for head in range(2 * heads):
            columns = slice(head * HEAD, (head + 1) * HEAD)
            u = made[:, columns]
            dealt_ref[place, columns] = (
                u * cosine + pltpu.roll(u, HEAD // 2, 1) * sine
            ).astype(BF)
        dealt_ref[place, 2 * head_cols :] = made[:, 2 * head_cols :].astype(BF)
        return carried

    lax.fori_loop(0, rows // step, project, 0)

    def pick(first, count):
        given_row = lax.broadcasted_iota(jnp.int32, (count, rows), 0) + first
        return jnp.where(given_row == dealt_row_ref[...], 1.0, 0.0).astype(BF)

    def put_in_order(i, carried):
        place = pl.ds(pl.multiple_of(i * step, step), step)
        given = jnp.dot(pick(i * step, step), dealt_ref[...], preferred_element_type=F32).astype(BF)
        q_ref[place, :] = given[:, :head_cols]
        k_ref[place, :] = given[:, head_cols : 2 * head_cols]
        v_ref[place, :] = given[:, 2 * head_cols :]
        return carried

    lax.fori_loop(0, rows // step, put_in_order, 0)
    own_rows = own_ref.shape[0]
    own_ref[...] = jnp.dot(
        pick(ctx * own_rows, own_rows), x_ref[...], preferred_element_type=F32
    ).astype(BF)
    first_length = length_ref[:, 0:1]
    for i in range(rows // step):
        here = slice(i * step, (i + 1) * step)
        keys = (i + 1) * step
        row = lax.broadcasted_iota(jnp.int32, (step, keys), 0) + i * step
        column = lax.broadcasted_iota(jnp.int32, (step, keys), 1)
        late_row = jnp.where(row >= first_length, 1, 0)
        late_column = jnp.where(column >= first_length, 1, 0)
        allowed = (column <= row) & (late_row == late_column)
        if rows > WINDOW:
            allowed = allowed & (row - column < WINDOW)

        def one_head(head, carried):
            columns = pl.ds(pl.multiple_of(head * HEAD, HEAD), HEAD)
            scores = lax.dot_general(
                q_ref[here, columns],
                k_ref[:keys, columns],
                (((1,), (1,)), ((), ())),
                preferred_element_type=F32,
            )
            scores = jnp.where(allowed, scores * (1.0 / math.sqrt(HEAD)), -1e30)
            largest = jnp.max(scores, axis=-1, keepdims=True)
            weights = jnp.exp(scores - largest)
            total = jnp.sum(weights, axis=-1, keepdims=True)
            probs = (weights * (1.0 / total)).astype(BF)
            prob_rows = pl.ds(pl.multiple_of(head * rows + i * step, step), step)
            prob_ref[prob_rows, :keys] = probs
            o_ref[here, columns] = jnp.dot(
                probs, v_ref[:keys, columns], preferred_element_type=F32
            ).astype(BF)
            return carried

        lax.fori_loop(0, heads, one_head, 0)
    own.wait()
    own_out.wait()
    for copy in deal + deal_out:
        copy.wait()


def attend(length, x, w, gain, dealt_rows, tables, gu, ctx_size, wa_size):
    rows, width = x.shape
    head_cols = w.shape[1] // 4
    heads = head_cols // HEAD
    vmem = pl.BlockSpec(memory_space=pltpu.VMEM)
    anywhere = pl.BlockSpec(memory_space=pl.ANY)
    heads_shape = jax.ShapeDtypeStruct((rows, head_cols), BF)
    return pl.pallas_call(
        functools.partial(attend_kernel, ctx_size, wa_size, heads),
        out_shape=(
            jax.ShapeDtypeStruct((width, rows), BF),
            jax.ShapeDtypeStruct((rows // ctx_size, width), BF),
            heads_shape,
            heads_shape,
            heads_shape,
            heads_shape,
            jax.ShapeDtypeStruct((heads * rows, rows), BF),
            jax.ShapeDtypeStruct((2, wa_size) + gu.shape[2:], BF),
            jax.ShapeDtypeStruct((head_cols, width), BF),
        ),
        in_specs=[vmem] * 6 + [anywhere],
        out_specs=[vmem] * 7 + [anywhere] * 2,
        scratch_shapes=[pltpu.SemaphoreType.DMA((wa_size,))] * 3
        + [pltpu.SemaphoreType.DMA((ctx_size,))] * 2
        + [pltpu.VMEM((rows, 3 * head_cols), BF)],
        compiler_params=pltpu.CompilerParams(
            collective_id=4, has_side_effects=True, vmem_limit_bytes=VMEM_LIMIT
        ),
        cost_estimate=pl.CostEstimate(
            flops=2 * rows * width * 3 * head_cols, bytes_accessed=100_000_000, transcendentals=0
        ),
        name="attend",
    )(length, x, w, gain, dealt_rows[None, :], tables, gu)


def out_kernel(
    ctx_size,
    wa_size,
    mixed_ref,
    w_ref,
    x_ref,
    gain_ref,
    dz_ref,
    gu_ref,
    hidden_ref,
    acts_ref,
    dzs_ref,
    gw_ref,
    *scratch,
):
    p = place_of(ctx_size, wa_size)
    act_send, act_recv, dz_send, dz_recv, local = scratch[12:]
    greet([p.beside] + p.ahead[1:], [p.up[1], p.down[1]])
    own = pltpu.make_async_copy(gu_ref, gw_ref.at[:, :, p.ctx], local.at[0])
    own.start()
    spread = Spread(
        p,
        gu_ref,
        lambda d: gw_ref.at[:, :, d],
        lambda d, h: gw_ref.at[h, :, d],
        scratch[8:12],
    )
    rows = x_ref.shape[0]

    def part_of(device):
        block = mixed_ref[pl.ds(pl.multiple_of(device * rows, rows), rows), :]
        return jnp.dot(block, w_ref[...], preferred_element_type=F32)

    half_rows = rows // 2

    def pass_on(slots, sems, s, i):
        place = pl.ds(i * half_rows, half_rows)
        return send(
            slots.at[s, place],
            slots.at[s + 1, place],
            sems[0].at[s, i],
            sems[1].at[s, i],
            wa=p.up[1],
        )

    def ring_step(ring, slots, sems, s):
        for i in range(2):
            ring[2 * (s - 1) + i].wait_recv()
            if s < wa_size - 1:
                ring.append(pass_on(slots, sems, s, i))

    dz_sems, act_sems = (dz_send, dz_recv), (act_send, act_recv)
    dzs_ref[0] = dz_ref[...]
    dz_ring = [pass_on(dzs_ref, dz_sems, 0, i) for i in range(2)]
    scatter = Scatter(p, part_of, scratch[:8])
    scatter.start()
    ring_step(dz_ring, dzs_ref, dz_sems, 1)
    hidden = x_ref[...].astype(F32) + scatter.total()
    spread.start()
    hidden_ref[...] = hidden
    scale = lax.rsqrt(jnp.mean(hidden * hidden, axis=-1, keepdims=True) + EPSILON)
    acts_ref[0] = (hidden * scale * gain_ref[...]).astype(BF)
    ring = [pass_on(acts_ref, act_sems, 0, i) for i in range(2)]
    for s in range(2, wa_size):
        ring_step(dz_ring, dzs_ref, dz_sems, s)
    arrivals = spread.arrivals()
    for s in range(1, wa_size):
        ring_step(ring, acts_ref, act_sems, s)
        if s == 2:
            next(arrivals)
            next(arrivals)
    for _ in arrivals:
        pass
    scatter.finish()
    spread.finish()
    own.wait()
    for copy in ring + dz_ring:
        copy.wait_send()


def out_project(mixed, w_rows, x_own, gain, dz, gu, ctx_size, wa_size):
    rows, width = x_own.shape
    vmem = pl.BlockSpec(memory_space=pltpu.VMEM)
    anywhere = pl.BlockSpec(memory_space=pl.ANY)
    return pl.pallas_call(
        functools.partial(out_kernel, ctx_size, wa_size),
        out_shape=(
            jax.ShapeDtypeStruct((rows, width), F32),
            jax.ShapeDtypeStruct((wa_size, rows, width), BF),
            jax.ShapeDtypeStruct((wa_size, rows, width), BF),
            jax.ShapeDtypeStruct((2, wa_size, ctx_size) + gu.shape[2:], BF),
        ),
        in_specs=[vmem] * 5 + [anywhere],
        out_specs=[vmem] * 3 + [anywhere],
        scratch_shapes=scatter_scratch(ctx_size, rows, width)
        + plane_sems(ctx_size)
        + [pltpu.SemaphoreType.DMA((wa_size, 2))] * 4
        + [pltpu.SemaphoreType.DMA((1,))],
        compiler_params=pltpu.CompilerParams(
            collective_id=1, has_side_effects=True, vmem_limit_bytes=VMEM_LIMIT
        ),
        cost_estimate=pl.CostEstimate(
            flops=2 * mixed.size * width, bytes_accessed=200_000_000, transcendentals=0
        ),
        name="out_project",
    )(mixed, w_rows, x_own, gain, dz, gu)


def mlp_kernel(
    act_ref,
    dz_ref,
    gw_any,
    wd_any,
    d_act_ref,
    mlp_ref,
    act_t_any,
    d_gu_any,
    inner_t_any,
    gw_ref,
    wd_ref,
    inner_ref,
    act_t_ref,
    d_gu_ref,
    inner_t_ref,
    gw_sems,
    sems,
):
    hidden_rows = wd_any.shape[0]
    hidden = inner_ref.shape[1]
    width = act_ref.shape[1]
    tiles = hidden // 128

    def gw_load(i):
        columns = pl.ds(pl.multiple_of(i * 128, 128), 128)
        return pltpu.make_async_copy(
            gw_any.at[:, :, columns], gw_ref.at[:, :, columns], gw_sems.at[i]
        )

    wd_load = pltpu.make_async_copy(wd_any, wd_ref.at[pl.ds(0, hidden_rows)], sems.at[0])
    for i in range(tiles):
        gw_load(i).start()
        if i == 1:
            wd_load.start()
    if hidden > hidden_rows:
        wd_ref[hidden_rows:, :] = jnp.zeros((hidden - hidden_rows, width), BF)
    act_t_ref[...] = act_ref[...].T
    act_t_store = pltpu.make_async_copy(act_t_ref, act_t_any, sems.at[1])
    act_t_store.start()
    act = act_ref[...]
    dz = dz_ref[...]

    def part(first, size):
        columns = pl.ds(first, size)
        gate = jnp.dot(act, gw_ref[0, :, columns], preferred_element_type=F32)
        up = jnp.dot(act, gw_ref[1, :, columns], preferred_element_type=F32)

        @pl.when(first == 0)
        def _():
            wd_load.wait()

        d_inner = lax.dot_general(
            dz, wd_ref[columns, :], (((1,), (1,)), ((), ())), preferred_element_type=F32
        )
        sigmoid = 1.0 / (1.0 + jnp.exp(-gate))
        silu = gate * sigmoid
        inner = (silu * up).astype(BF)
        inner_ref[:, columns] = inner
        d_gate = (d_inner * up * sigmoid * (1.0 + gate * (1.0 - sigmoid))).astype(BF)
        d_up = (d_inner * silu).astype(BF)
        d_gu_ref[0, :, columns] = d_gate
        d_gu_ref[1, :, columns] = d_up
        inner_t_ref[columns, :] = inner.T

    per_chunk = CHUNK // 128

    def one(i, carried):
        for j in range(per_chunk):

            @pl.when(i * per_chunk + j < tiles)
            def _():
                gw_load(i * per_chunk + j).wait()

        first = jnp.minimum(i * per_chunk, tiles - per_chunk) * 128
        part(pl.multiple_of(first, 128), CHUNK)
        return carried

    lax.fori_loop(0, -(-tiles // per_chunk), one, 0)
    stores = [
        pltpu.make_async_copy(d_gu_ref, d_gu_any, sems.at[2]),
        pltpu.make_async_copy(inner_t_ref, inner_t_any, sems.at[3]),
    ]
    for copy in stores:
        copy.start()

    def two(i, carried):
        place = pl.ds(pl.multiple_of(i * CHUNK, CHUNK), CHUNK)
        back = lax.dot_general(
            d_gu_ref[0], gw_ref[0, place, :], (((1,), (1,)), ((), ())), preferred_element_type=F32
        )
        back = back + lax.dot_general(
            d_gu_ref[1], gw_ref[1, place, :], (((1,), (1,)), ((), ())), preferred_element_type=F32
        )
        d_act_ref[:, place] = back.astype(BF)
        mlp_ref[:, place] = jnp.dot(
            inner_ref[...], wd_ref[:, place], preferred_element_type=F32
        ).astype(BF)
        return carried

    lax.fori_loop(0, width // CHUNK, two, 0)
    for copy in stores + [act_t_store]:
        copy.wait()


def mlp(act, dz, gw, wd):
    tokens, width = act.shape
    hidden = gw.shape[2]
    vmem = pl.BlockSpec(memory_space=pltpu.VMEM)
    anywhere = pl.BlockSpec(memory_space=pl.ANY)
    return pl.pallas_call(
        mlp_kernel,
        out_shape=(
            jax.ShapeDtypeStruct((tokens, width), BF),
            jax.ShapeDtypeStruct((tokens, width), BF),
            jax.ShapeDtypeStruct((width, tokens), BF),
            jax.ShapeDtypeStruct((2, tokens, hidden), BF),
            jax.ShapeDtypeStruct((hidden, tokens), BF),
        ),
        in_specs=[vmem, vmem, anywhere, anywhere],
        out_specs=[vmem] * 2 + [anywhere] * 3,
        scratch_shapes=[
            pltpu.VMEM(gw.shape, BF),
            pltpu.VMEM((hidden, width), BF),
            pltpu.VMEM((tokens, hidden), BF),
            pltpu.VMEM((width, tokens), BF),
            pltpu.VMEM((2, tokens, hidden), BF),
            pltpu.VMEM((hidden, tokens), BF),
            pltpu.SemaphoreType.DMA((hidden // 128,)),
            pltpu.SemaphoreType.DMA((4,)),
        ],
        compiler_params=pltpu.CompilerParams(vmem_limit_bytes=60 * 1024 * 1024),
        cost_estimate=pl.CostEstimate(
            flops=12 * tokens * width * hidden, bytes_accessed=50_000_000, transcendentals=0
        ),
        name="mlp",
    )(act, dz, gw, wd)


def turn_kernel(
    ctx_size,
    wa_size,
    parts_ref,
    mlp_ref,
    hidden_ref,
    gain_ref,
    dz_ref,
    act_t_ref,
    d_gu_ref,
    inner_t_ref,
    dz_all_ref,
    all_ref,
    gain_out_ref,
    out_ref,
    gu_out_ref,
    down_out_ref,
    *scratch,
):
    p = place_of(ctx_size, wa_size)
    got_ref, more_ref, wa_send, wa_recv, more_send, more_recv = scratch[:6]
    gu_both, gu_got, gu_near, gu_sent, down_both, down_got, down_near, down_sent = scratch[6:14]
    gu_sems, down_sems, spread_sems = scratch[14:18], scratch[18:22], scratch[22:26]
    own_parts, own_mlp, local = scratch[26:29]
    greet([p.beside] + p.ahead[1:], p.down[1:])
    copies = [
        send(parts_ref.at[s], got_ref.at[s], wa_send.at[s], wa_recv.at[s], wa=p.down[s])
        for s in range(1, wa_size)
    ]
    loads = [
        pltpu.make_async_copy(parts_ref.at[0], own_parts, local.at[0]),
        pltpu.make_async_copy(mlp_ref.at[0], own_mlp, local.at[1]),
    ]
    for copy in loads:
        copy.start()
    down_total = down_both.shape[1]
    down_rows = down_total // 2
    columns = dz_all_ref.shape[1] // ctx_size
    half = gu_both.shape[1] // 2
    piece_rows = gu_both.shape[3]
    wa_rows = act_t_ref.shape[0] // wa_size

    def down_piece(ref, chip):
        return ref.at[:, pl.ds(pl.multiple_of(chip * columns, columns), columns)]

    def down_half(ref, chip, h):
        place = pl.ds(h * down_rows, down_rows)
        if chip is None:
            return ref.at[place]
        return ref.at[place, pl.ds(pl.multiple_of(chip * columns, columns), columns)]

    down = Fold(
        p,
        down_both,
        down_got,
        down_near,
        down_sent,
        down_piece,
        down_half,
        lambda into, other: add_rows(into, other, 16),
        down_sems,
    )

    def gu_half(ref, chip, h):
        place = pl.ds(h * half, half)
        return ref.at[place] if chip is None else ref.at[place, chip]

    gu = Fold(
        p,
        gu_both,
        gu_got,
        gu_near,
        gu_sent,
        lambda ref, chip: ref.at[:, chip],
        gu_half,
        add_blocks,
        gu_sems,
    )

    def make(chip):
        first = chip * (2 * piece_rows)
        left = jnp.concatenate(
            [
                act_t_ref[pl.ds(pl.multiple_of(i * wa_rows + first, 2 * piece_rows), 2 * piece_rows), :]
                for i in range(wa_size)
            ],
            axis=0,
        )

        def gu_part(part, carried):
            made = jnp.dot(left, d_gu_ref[part], preferred_element_type=F32).astype(BF)
            for i in range(wa_size):
                for core in range(2):
                    at = (2 * i + core) * piece_rows
                    gu_both[core, part * wa_size + i, chip] = made[at : at + piece_rows]
            return carried

        lax.fori_loop(0, 2, gu_part, 0)

        def down_part(core, carried):
            place = pl.multiple_of((core * p.chips + chip) * columns, columns)
            made = jnp.dot(
                inner_t_ref[...], dz_all_ref[:, pl.ds(place, columns)], preferred_element_type=F32
            ).astype(BF)
            target = pl.ds(pl.multiple_of(chip * columns, columns), columns)
            down_both[core, :, target] = made[:down_total]
            return carried

        lax.fori_loop(0, 2, down_part, 0)

    for i in range(p.chips):
        make(gu.order[i])
        gu.start(i)
        down.start(i)
        if i > 0:
            gu.between(i - 1)
            down.between(i - 1)
    gu.between(p.chips - 1)
    down.between(p.chips - 1)
    hidden = hidden_ref[...]
    scale = lax.rsqrt(jnp.mean(hidden * hidden, axis=-1, keepdims=True) + EPSILON)
    down.onward()
    for copy in loads:
        copy.wait()
    d_normed = own_parts[...].astype(F32)
    for s in range(1, wa_size):
        copies[s - 1].wait_recv()
        d_normed = d_normed + got_ref[s].astype(F32)
    more = [
        send(mlp_ref.at[s], more_ref.at[s], more_send.at[s], more_recv.at[s], wa=p.down[s])
        for s in range(1, wa_size)
    ]
    gain_out_ref[...] = jnp.sum(d_normed * (hidden * scale), axis=0, keepdims=True)
    d_hidden = norm_back(hidden, scale, gain_ref[...], d_normed, dz_ref[...].astype(F32))
    all_ref[p.ctx] = d_hidden.astype(BF)
    half_rows = all_ref.shape[1] // 2
    spread = Spread(
        p,
        all_ref.at[p.ctx],
        lambda d: all_ref.at[d],
        lambda d, h: all_ref.at[d, pl.ds(h * half_rows, half_rows)],
        spread_sems,
    )
    spread.start()
    gu.onward()
    down_out_ref[...] = down.total()[...]
    for _ in spread.arrivals():
        pass
    gu_out_ref[...] = gu.total()[...]
    result = hidden + own_mlp[...].astype(F32)
    for s in range(1, wa_size):
        more[s - 1].wait_recv()
        result = result + more_ref[s].astype(F32)
    out_ref[...] = result.astype(BF)
    for copy in copies + more:
        copy.wait_send()
    down.finish()
    gu.finish()
    spread.finish()


def turn(
    parts, mlp, hidden, gain, dz, act_t, d_gu, inner_t, dz_all, hidden_rows, ctx_size, wa_size
):
    rows, width = hidden.shape
    chips = ctx_size // 2
    columns = width // ctx_size
    lead = 2 * wa_size
    gu_rows, gu_columns = width // (ctx_size * wa_size), d_gu.shape[2]
    vmem = pl.BlockSpec(memory_space=pltpu.VMEM)
    anywhere = pl.BlockSpec(memory_space=pl.ANY)
    many = 2 if chips == 4 else chips - 1
    return pl.pallas_call(
        functools.partial(turn_kernel, ctx_size, wa_size),
        out_shape=(
            jax.ShapeDtypeStruct((ctx_size, rows, width), BF),
            jax.ShapeDtypeStruct((1, width), F32),
            jax.ShapeDtypeStruct((rows, width), BF),
            jax.ShapeDtypeStruct((lead, gu_rows, gu_columns), BF),
            jax.ShapeDtypeStruct((hidden_rows, columns), BF),
        ),
        in_specs=[anywhere] * 2 + [vmem] * 7,
        out_specs=[vmem] * 5,
        scratch_shapes=[pltpu.VMEM((wa_size, rows, width), BF)] * 2
        + [pltpu.SemaphoreType.DMA((wa_size,))] * 4
        + [
            pltpu.VMEM((2, lead, chips, gu_rows, gu_columns), BF),
            pltpu.VMEM((lead, chips, gu_rows, gu_columns), BF),
            pltpu.VMEM((2, lead // 2, gu_rows, gu_columns), BF),
            pltpu.VMEM((many, lead, gu_rows, gu_columns), BF),
            pltpu.VMEM((2, hidden_rows, columns * chips), BF),
            pltpu.VMEM((hidden_rows, columns * chips), BF),
            pltpu.VMEM((2, hidden_rows // 2, columns), BF),
            pltpu.VMEM((many, hidden_rows, columns), BF),
        ]
        + [pltpu.SemaphoreType.DMA((max(chips, 6),))] * 8
        + plane_sems(ctx_size)
        + [pltpu.VMEM((rows, width), BF)] * 2
        + [pltpu.SemaphoreType.DMA((2,))],
        compiler_params=pltpu.CompilerParams(
            collective_id=2, has_side_effects=True, vmem_limit_bytes=VMEM_LIMIT
        ),
        cost_estimate=pl.CostEstimate(flops=0, bytes_accessed=200_000_000, transcendentals=0),
        name="turn",
    )(parts, mlp, hidden, gain, dz, act_t, d_gu, inner_t, dz_all)


def finish_kernel(
    ctx_size,
    wa_size,
    heads,
    dy_ref,
    w_ref,
    o_ref,
    q_ref,
    k_ref,
    v_ref,
    tables_ref,
    x_ref,
    gain_ref,
    gain_two_ref,
    dealt_column_ref,
    prob_any,
    act_t_any,
    w_all_any,
    gu_ref,
    down_ref,
    out_ref,
    gus_ref,
    downs_ref,
    qkvs_ref,
    outs_ref,
    sums_ref,
    *scratch,
):
    p = place_of(ctx_size, wa_size)
    do_ref, dk_ref, dv_ref, d_out_ref, given_ref = scratch[8:13]
    late_ref, w_all_ref = scratch[13:15]
    grads_ref, dw_ref, parts_ref, gu_in_ref, gains_ref = scratch[15:20]
    rows_ref, dw_in, share_ref, do_in, out_share_ref = scratch[20:25]
    wa_gains, ctx_gains, local, load_sems = scratch[25:29]
    gu_sems, dw_sems, do_sems, wa_sems = (scratch[i : i + 2] for i in (29, 31, 33, 35))
    part_sems, ctx_sems = scratch[37:39], scratch[39:41]
    down_plane, gu_plane, qkv_plane, out_plane = (scratch[i : i + 4] for i in (41, 45, 49, 53))
    peers = [lax.rem(p.ctx + i, ctx_size) for i in range(ctx_size)]
    greet(peers[1:], p.up[1:])
    locals_ = []

    def keep(source, target):
        copy = pltpu.make_async_copy(source, target, local.at[len(locals_)])
        copy.start()
        locals_.append(copy)
        return copy

    def spread_of(own, slots, sems):
        half = slots.shape[1] // 2
        keep(own, slots.at[p.ctx])
        spread = Spread(
            p,
            own,
            lambda d: slots.at[d],
            lambda d, h: slots.at[d, pl.ds(h * half, half)],
            sems,
        )
        spread.start()
        return spread

    deal = [
        send(
            gu_ref.at[:, p.up[s]], gu_in_ref.at[p.wa], gu_sems[0].at[s], gu_sems[1].at[s], wa=p.up[s]
        )
        for s in range(1, wa_size)
    ]
    own_deal = keep(gu_ref.at[:, p.wa], gu_in_ref.at[p.wa])
    down_spread = spread_of(down_ref, downs_ref, down_plane)
    loads = [
        pltpu.make_async_copy(source, target, load_sems.at[i])
        for i, (source, target) in enumerate(
            (
                (prob_any, late_ref),
                (w_all_any, w_all_ref),
                (act_t_any, late_ref),
            )
        )
    ]
    for copy in loads[:2]:
        copy.start()
    rows = dy_ref.shape[0]
    width = dy_ref.shape[1]
    step = ATTEND_ROWS
    head_cols = heads * HEAD
    qkv_cols = 3 * head_cols
    back_scale = 1.0 / math.sqrt(HEAD)
    d_out_ref[...] = lax.dot_general(
        o_ref[...], dy_ref[...], (((0,), (0,)), ((), ())), preferred_element_type=F32
    ).astype(BF)

    def d_out_part(device):
        place = pl.ds(pl.multiple_of(device * head_cols, head_cols), head_cols)
        return d_out_ref.at[:, place]

    part_copies = exchange_plane(
        peers, d_out_part, lambda d: parts_ref.at[d], part_sems[0], part_sems[1]
    )
    own_part = keep(d_out_part(p.ctx), parts_ref.at[p.ctx])

    def project(i, carried):
        place = pl.ds(pl.multiple_of(i * step, step), step)
        do_ref[place, :] = lax.dot_general(
            dy_ref[place, :],
            w_ref[...],
            (((1,), (1,)), ((), ())),
            preferred_element_type=F32,
        ).astype(BF)
        return carried

    lax.fori_loop(0, rows // step, project, 0)
    loads[0].wait()
    dk_ref[...] = jnp.zeros_like(dk_ref)
    dv_ref[...] = jnp.zeros_like(dv_ref)

    def unrotate(u, place):
        cosine, sine = tables_ref[0, place, :], tables_ref[1, place, :]
        return u * cosine - pltpu.roll(u, HEAD // 2, 1) * sine

    for i in range(rows // step):
        here = slice(i * step, (i + 1) * step)
        keys = (i + 1) * step

        def back(head, carried):
            columns = pl.ds(pl.multiple_of(head * HEAD, HEAD), HEAD)
            d_o = do_ref[here, columns]
            q = q_ref[here, columns]
            prob_rows = pl.ds(pl.multiple_of(head * rows + i * step, step), step)
            probs = late_ref[prob_rows, :keys]
            d_probs = lax.dot_general(
                d_o,
                v_ref[:keys, columns],
                (((1,), (1,)), ((), ())),
                preferred_element_type=F32,
            )
            wide = probs.astype(F32)
            row_dot = jnp.sum(wide * d_probs, axis=-1, keepdims=True)
            d_scores = (wide * (d_probs - row_dot)).astype(BF)
            d_query = jnp.dot(d_scores, k_ref[:keys, columns], preferred_element_type=F32)
            given_ref[here, columns] = unrotate(d_query * back_scale, here).astype(BF)
            dk_ref[:keys, columns] += lax.dot_general(
                d_scores, q, (((0,), (0,)), ((), ())), preferred_element_type=F32
            )
            dv_ref[:keys, columns] += lax.dot_general(
                probs, d_o, (((0,), (0,)), ((), ())), preferred_element_type=F32
            )
            return carried

        lax.fori_loop(0, heads, back, 0)
    loads[2].start()
    for head in range(heads):
        columns = slice(head * HEAD, (head + 1) * HEAD)
        d_key = unrotate(dk_ref[:, columns] * back_scale, slice(0, rows))
        given_ref[:, head_cols + head * HEAD : head_cols + (head + 1) * HEAD] = d_key.astype(BF)
    given_ref[:, 2 * head_cols :] = dv_ref[...].astype(BF)
    down_arrivals = down_spread.arrivals()
    next(down_arrivals)
    next(down_arrivals)
    loads[1].wait()

    def unpick(place, count):
        given_row = lax.broadcasted_iota(jnp.int32, (count, rows), 1)
        return jnp.where(given_row == dealt_column_ref[place, :], 1.0, 0.0).astype(BF)

    def put_back(i, carried):
        place = pl.ds(pl.multiple_of(i * step, step), step)
        grads_ref[place, :] = jnp.dot(
            unpick(place, step), given_ref[...], preferred_element_type=F32
        ).astype(BF)
        return carried

    lax.fori_loop(0, rows // step, put_back, 0)
    own_rows = x_ref.shape[0]

    def part_of(device):
        place = pl.ds(pl.multiple_of(device * own_rows, own_rows), own_rows)
        return lax.dot_general(
            grads_ref[place, :],
            w_all_ref[:, :qkv_cols],
            (((1,), (1,)), ((), ())),
            preferred_element_type=F32,
        )

    loads[2].wait()
    wa_rows = dw_ref.shape[1]

    def weights(i, carried):
        place = pl.ds(pl.multiple_of(i * wa_rows, wa_rows), wa_rows)
        made = jnp.dot(late_ref[place, :], grads_ref[...], preferred_element_type=F32)
        dw_ref[i] = made.astype(BF)
        return carried

    lax.fori_loop(0, wa_size, weights, 0)
    dw_copies = [
        send(
            dw_ref.at[p.up[s]], dw_in.at[s - 1], dw_sems[0].at[s], dw_sems[1].at[s], wa=p.up[s]
        )
        for s in range(1, wa_size)
    ]
    scatter = Scatter(p, part_of, scratch[:8])
    scatter.start()
    ones = jnp.ones((8, qkv_cols), BF)

    def gains(i, carried):
        place = pl.ds(pl.multiple_of(i * wa_rows, wa_rows), wa_rows)
        products = dw_ref[i].astype(F32) * w_all_ref[place, :qkv_cols].astype(F32)
        high = products.astype(BF)
        low = (products - high.astype(F32)).astype(BF)
        sums = [
            lax.dot_general(
                ones, part, (((1,), (1,)), ((), ())), preferred_element_type=F32
            )
            for part in (high, low)
        ]
        gains_ref[0:1, place] = (sums[0] + sums[1])[0:1] / gain_ref[:, place]
        return carried

    lax.fori_loop(0, wa_size, gains, 0)
    gains_ref[1:2] = gain_two_ref[...]
    wa_gains[p.wa] = gains_ref[...]
    small = [
        send(gains_ref, wa_gains.at[p.wa], wa_sems[0].at[s], wa_sems[1].at[s], wa=p.up[s])
        for s in range(1, wa_size)
    ]
    for _ in down_arrivals:
        pass
    own_deal.wait()
    for copy in deal:
        copy.wait_recv()
    total_columns = rows_ref.shape[1] // 2
    own_columns = total_columns // wa_size
    for i in range(wa_size):
        for part in range(2):
            first = part * total_columns + i * own_columns
            rows_ref[:, first : first + own_columns] = gu_in_ref[i, part, :, :own_columns]
    gu_spread = spread_of(rows_ref, gus_ref, gu_plane)
    for copy in small:
        copy.wait()
    plane_gain = wa_gains[0]
    for i in range(1, wa_size):
        plane_gain = plane_gain + wa_gains[i]
    ctx_gains[p.ctx] = plane_gain
    own_gain = ctx_gains.at[p.ctx]
    small = [
        send(own_gain, own_gain, ctx_sems[0].at[i], ctx_sems[1].at[i], ctx=peer)
        for i, peer in enumerate(peers)
        if i > 0
    ]
    dh_place = pl.ds(pl.multiple_of(p.ctx * own_rows, own_rows), own_rows)
    d_hidden = jnp.dot(unpick(dh_place, own_rows), dy_ref[...], preferred_element_type=F32)
    x = x_ref[...].astype(F32)
    scale = lax.rsqrt(jnp.mean(x * x, axis=-1, keepdims=True) + EPSILON)
    out_ref[...] = norm_back(x, scale, gain_ref[...], scatter.total(), d_hidden).astype(BF)
    gu_arrivals = gu_spread.arrivals()
    next(gu_arrivals)
    next(gu_arrivals)
    for _ in gu_arrivals:
        pass
    for copy in small:
        copy.wait()
    total_gain = ctx_gains[0]
    for i in range(1, ctx_size):
        total_gain = total_gain + ctx_gains[i]
    sums_ref[...] = total_gain
    for copy in dw_copies:
        copy.wait_recv()
    own_part.wait()
    for copy in part_copies:
        copy.wait_recv()
    per_wa = ctx_size // wa_size

    def d_out_block(device):
        return parts_ref.at[pl.ds(device * per_wa, per_wa)]

    do_copies = [
        send(
            d_out_block(p.up[s]), do_in.at[s], do_sems[0].at[s], do_sems[1].at[s], wa=p.up[s]
        )
        for s in range(1, wa_size)
    ]

    def add_up(i, carried):
        place = pl.ds(pl.multiple_of(i * 16, 16), 16)
        total = dw_ref[p.wa, place, :].astype(F32)
        for s in range(1, wa_size):
            total = total + dw_in[s - 1, place, :].astype(F32)
        share_ref[place, :] = total.astype(BF)
        return carried

    lax.fori_loop(0, wa_rows // 16, add_up, 0)
    qkv_spread = spread_of(share_ref, qkvs_ref, qkv_plane)
    for copy in do_copies:
        copy.wait_recv()
    for i in range(per_wa):
        total = parts_ref[p.wa * per_wa + i].astype(F32)
        for s in range(1, wa_size):
            total = total + do_in[s, i].astype(F32)
        out_share_ref[pl.ds(i * head_cols, head_cols), :] = total.astype(BF)
    out_spread = spread_of(out_share_ref, outs_ref, out_plane)
    for _ in qkv_spread.arrivals():
        pass
    for _ in out_spread.arrivals():
        pass
    scatter.finish()
    for spread in (down_spread, gu_spread, qkv_spread, out_spread):
        spread.finish()
    for copy in deal + dw_copies + do_copies + part_copies:
        copy.wait_send()
    for copy in locals_:
        if copy is not own_deal and copy is not own_part:
            copy.wait()


def finish(
    dy,
    w_rows,
    o,
    q,
    k,
    v,
    tables,
    x_own,
    gain,
    gain_two,
    dealt_column,
    probs,
    act_t,
    w_all,
    gu,
    down,
    columns,
    ctx_size,
    wa_size,
):
    rows, width = dy.shape
    head_cols = o.shape[1]
    heads = head_cols // HEAD
    own_rows = x_own.shape[0]
    vmem = pl.BlockSpec(memory_space=pltpu.VMEM)
    anywhere = pl.BlockSpec(memory_space=pl.ANY)
    wa_rows = width // wa_size
    gu_shape = (gu.shape[2], columns)
    share_shape = (wa_rows, 3 * head_cols)
    out_shape = (wa_rows, head_cols)
    gains = (2, width)
    return pl.pallas_call(
        functools.partial(finish_kernel, ctx_size, wa_size, heads),
        out_shape=(jax.ShapeDtypeStruct((own_rows, width), BF),)
        + tuple(
            jax.ShapeDtypeStruct((ctx_size,) + shape, BF)
            for shape in (gu_shape, down.shape, share_shape, out_shape)
        )
        + (jax.ShapeDtypeStruct(gains, F32),),
        in_specs=[vmem] * 11 + [anywhere] * 5,
        out_specs=[vmem] + [anywhere] * 4 + [vmem],
        scratch_shapes=scatter_scratch(ctx_size, own_rows, width)
        + [
            pltpu.VMEM((rows, head_cols), BF),
            pltpu.VMEM((rows, head_cols), F32),
            pltpu.VMEM((rows, head_cols), F32),
            pltpu.VMEM((head_cols, width), BF),
            pltpu.VMEM((rows, 3 * head_cols), BF),
            pltpu.VMEM(act_t.shape, BF),
            pltpu.VMEM(w_all.shape, BF),
            pltpu.VMEM((rows, 3 * head_cols), BF),
            pltpu.VMEM((wa_size,) + share_shape, BF),
            pltpu.VMEM((ctx_size, head_cols, head_cols), BF),
            pltpu.VMEM((wa_size, 2) + gu.shape[2:], BF),
            pltpu.VMEM(gains, F32),
            pltpu.VMEM(gu_shape, BF),
            pltpu.VMEM((wa_size - 1,) + share_shape, BF),
            pltpu.VMEM(share_shape, BF),
            pltpu.VMEM((wa_size, ctx_size // wa_size, head_cols, head_cols), BF),
            pltpu.VMEM(out_shape, BF),
            pltpu.VMEM((wa_size,) + gains, F32),
            pltpu.VMEM((ctx_size,) + gains, F32),
            pltpu.SemaphoreType.DMA((6,)),
            pltpu.SemaphoreType.DMA((4,)),
        ]
        + [pltpu.SemaphoreType.DMA((wa_size,))] * 8
        + [pltpu.SemaphoreType.DMA((ctx_size,))] * 4
        + plane_sems(ctx_size) * 4,
        compiler_params=pltpu.CompilerParams(
            collective_id=3, has_side_effects=True, vmem_limit_bytes=VMEM_LIMIT + 2 * 1024 * 1024
        ),
        cost_estimate=pl.CostEstimate(
            flops=12 * rows * width * head_cols, bytes_accessed=400_000_000, transcendentals=0
        ),
        name="finish",
    )(
        dy,
        w_rows,
        o,
        q,
        k,
        v,
        tables,
        x_own,
        gain,
        gain_two,
        dealt_column,
        probs,
        act_t,
        w_all,
        gu,
        down,
    )


def widen(blocks, columns, groups, step):
    count, rows, own = blocks.shape
    parts, per_group = own // columns, count // groups

    def body(block_ref, out_ref):
        for i in range(parts):
            for at in range(per_group):
                first = (i * per_group + at) * columns
                out_ref[:, first : first + columns] = block_ref[
                    at, 0, :, i * columns : (i + 1) * columns
                ].astype(F32)

    return pl.pallas_call(
        body,
        out_shape=jax.ShapeDtypeStruct((rows, count * own), F32),
        grid=(rows // step, groups),
        in_specs=[pl.BlockSpec((per_group, 1, step, own), lambda r, g: (0, g, r, 0))],
        out_specs=pl.BlockSpec((step, per_group * own), lambda r, g: (r, g)),
        compiler_params=pltpu.CompilerParams(vmem_limit_bytes=VMEM_LIMIT),
        name="widen",
    )(blocks.reshape(per_group, groups, rows, own))


def per_device(
    tokens, lengths, dealing, norm1_gain, w_qkv, w_out, norm2_gain, w_gate_up, w_down, grad_out
):
    tok_rows, width = tokens.shape[1], tokens.shape[2]
    ctx_size = lax.axis_size("ctx")
    wa_size = lax.axis_size("wa")
    ctx_index = lax.axis_index("ctx")
    wa_index = lax.axis_index("wa")
    block_order = dealing[0]
    block_total = block_order.shape[0]
    group_rows = block_total * BLOCK
    own_blocks = tok_rows // BLOCK
    heads_own = HEADS // ctx_size
    head_cols = heads_own * HEAD
    wa_rows = width // wa_size
    ff_total = w_gate_up.shape[1] // 2
    ff_own = w_down.shape[0]
    piece_rows = wa_rows // ctx_size

    own_cols = jnp.concatenate(
        [
            lax.dynamic_slice_in_dim(w_qkv, part * width + ctx_index * head_cols, head_cols, 1)
            for part in range(3)
        ]
        + [lax.dynamic_slice_in_dim(w_out, ctx_index * head_cols, head_cols, 1)],
        axis=1,
    )
    in_block = jnp.arange(BLOCK, dtype=jnp.int32)
    rows_dealt = (block_order[:, None] * BLOCK + in_block[None, :]).reshape(group_rows)
    dealt_column = rows_dealt[:, None]
    dealt, all_cols, gu_send, tables = gather_both(
        tokens[0], own_cols, w_gate_up, dealt_column, lengths, ff_own, ctx_size, wa_size
    )
    dealt = dealt.reshape(group_rows, width)
    all_cols = all_cols.reshape(width, 4 * head_cols)
    act_one_t, own_given, query_b, key_b, value_b, mixed_b, probs_b, gu_mine, out_rows = attend(
        lengths,
        dealt,
        all_cols,
        norm1_gain[None, :],
        rows_dealt,
        tables[0],
        gu_send,
        ctx_size,
        wa_size,
    )
    gain_two = norm2_gain[None, :]
    hidden, acts, grads_all, gu_weight = out_project(
        mixed_b, out_rows, own_given, gain_two, grad_out[0], gu_mine, ctx_size, wa_size
    )
    gu_weight = gu_weight.reshape(2, width, gu_weight.shape[4])
    act_two = acts.reshape(wa_size * tok_rows, width)
    cotangent = grads_all.reshape(wa_size * tok_rows, width)

    d_act, mlp_parts, act_t, d_gu, inner_t = mlp(act_two, cotangent, gu_weight, w_down)
    d_branches, gain_two_part, out_given, gu_piece_grad, down_piece_grad = turn(
        d_act.reshape(wa_size, tok_rows, width),
        mlp_parts.reshape(wa_size, tok_rows, width),
        hidden,
        gain_two,
        grad_out[0],
        act_t,
        d_gu,
        inner_t,
        cotangent,
        ff_own,
        ctx_size,
        wa_size,
    )
    d_branch_b = d_branches.reshape(group_rows, width)
    d_tokens, gus, downs, qkvs, outs, gain_sums = finish(
        d_branch_b,
        out_rows,
        mixed_b,
        query_b,
        key_b,
        value_b,
        tables[1],
        tokens[0],
        norm1_gain[None, :],
        gain_two_part,
        dealt_column,
        probs_b,
        act_one_t,
        all_cols,
        gu_piece_grad.reshape((2, wa_size) + gu_piece_grad.shape[1:]),
        down_piece_grad,
        2 * ff_total,
        ctx_size,
        wa_size,
    )
    d_gate_up = gus.reshape(wa_rows, 2 * ff_total).astype(F32)
    d_down = widen(downs, downs.shape[2], 2, ff_own // 2 if ff_own % 32 == 0 else ff_own)
    d_qkv = widen(qkvs, head_cols, 1, 64)
    d_out = widen(outs, head_cols, 1, 64)
    return (
        out_given[None],
        d_tokens[None],
        gain_sums[0],
        d_qkv,
        d_out,
        gain_sums[1],
        d_gate_up,
        d_down,
    )


def solution(mesh):
    in_specs = (
        P("wa", "ctx", None),
        P("wa", None),
        P("wa", None),
        P(),
        P("wa", None),
        P("wa", None),
        P(),
        P("wa", None),
        P("wa", None),
        P("wa", "ctx", None),
    )
    out_specs = (
        P("wa", "ctx", None),
        P("wa", "ctx", None),
        P(),
        P("wa", None),
        P("wa", None),
        P(),
        P("wa", None),
        P("wa", None),
    )
    return jax.shard_map(
        per_device, mesh=mesh, in_specs=in_specs, out_specs=out_specs, check_vma=False
    )
```

```python
import functools
import math
import types

import jax
import jax.numpy as jnp
import numpy as np
from jax import lax
from jax.experimental import pallas as pl
from jax.experimental.pallas import tpu as pltpu
from jax.sharding import PartitionSpec as P

HEADS = 16
HEAD = 128
WINDOW = 2048
BLOCK = 128

EPSILON = 1e-06
BF = jnp.bfloat16
F32 = jnp.float32
VMEM_LIMIT = 60 * 1024 * 1024
ATTEND_ROWS = 256
CHUNK = 256


MESH = pl.DeviceIdType.MESH


def greet(ctx_peers, wa_peers):
    barrier = pltpu.get_barrier_semaphore()
    for peer in ctx_peers:
        pl.semaphore_signal(barrier, inc=1, device_id={"ctx": peer}, device_id_type=MESH)
    for peer in wa_peers:
        pl.semaphore_signal(barrier, inc=1, device_id={"wa": peer}, device_id_type=MESH)
    pl.semaphore_wait(barrier, len(ctx_peers) + len(wa_peers))


def send(source, target, send_sem, recv_sem, **peer):
    copy = pltpu.make_async_remote_copy(
        src_ref=source,
        dst_ref=target,
        send_sem=send_sem,
        recv_sem=recv_sem,
        device_id=peer,
        device_id_type=MESH,
    )
    copy.start()
    return copy


def place_of(ctx_size, wa_size):
    chips = ctx_size // 2
    p = types.SimpleNamespace(ctx_size=ctx_size, wa_size=wa_size, chips=chips)
    p.ctx, p.wa = lax.axis_index("ctx"), lax.axis_index("wa")
    p.core, p.chip = lax.rem(p.ctx, 2), lax.div(p.ctx, 2)
    p.beside = p.chip * 2 + 1 - p.core
    p.ahead = [lax.rem(p.chip + m, chips) * 2 + p.core for m in range(chips)]
    p.behind = [lax.rem(p.chip + chips - m, chips) * 2 + p.core for m in range(chips)]
    p.up = [lax.rem(p.wa + s, wa_size) for s in range(wa_size)]
    p.down = [lax.rem(p.wa + wa_size - s, wa_size) for s in range(wa_size)]
    p.square = chips == 4
    if p.square:
        p.near = [p.chip + 1 - 2 * lax.rem(p.chip, 2), lax.rem(p.chip + 2, 4)]
        p.far = 3 - p.chip
    return p


def on_core(p, chip):
    return chip * 2 + p.core


def off_core(p, chip):
    return chip * 2 + 1 - p.core


def plane_sems(ctx_size):
    count = max(ctx_size // 2, 5)
    return [pltpu.SemaphoreType.DMA((count,))] * 4


class Spread:
    def __init__(self, p, own, slot, half, sems):
        self.p, self.own, self.slot, self.half = p, own, slot, half
        self.chip_send, self.chip_recv, self.side_send, self.side_recv = sems
        self.chip, self.side = [], []

    def across(self, source, target, chip):
        i = len(self.chip)
        self.chip.append(
            send(source, target, self.chip_send.at[i], self.chip_recv.at[i], ctx=on_core(self.p, chip))
        )

    def aside(self, source, target):
        i = len(self.side)
        self.side.append(
            send(source, target, self.side_send.at[i], self.side_recv.at[i], ctx=self.p.beside)
        )

    def start(self):
        p = self.p
        target = self.slot(p.ctx)
        if p.square:
            for chip in p.near:
                self.across(self.own, target, chip)
        else:
            for m in range(1, p.chips):
                self.across(self.own, target, lax.rem(p.chip + m, p.chips))
        self.aside(self.own, target)

    def arrivals(self):
        p = self.p
        if not p.square:
            for m in range(1, p.chips):
                self.chip[m - 1].wait_recv()
                block = self.slot(p.behind[m])
                self.aside(block, block)
                yield p.behind[m]
            self.side[0].wait_recv()
            yield p.beside
            for m in range(1, p.chips):
                self.side[m].wait_recv()
                yield off_core(p, lax.rem(p.chip + p.chips - m, p.chips))
            return
        for i in range(2):
            self.chip[i].wait_recv()
            device = on_core(p, p.near[i])
            part = self.half(device, i)
            self.across(part, part, p.near[1 - i])
            self.aside(self.slot(device), self.slot(device))
            yield device
        self.side[0].wait_recv()
        yield p.beside
        for i in range(2):
            self.side[1 + i].wait_recv()
            yield off_core(p, p.near[i])
        device = on_core(p, p.far)
        for i in range(2):
            self.chip[2 + i].wait_recv()
            part = self.half(device, i)
            self.aside(part, part)
        yield device
        for i in range(2):
            self.side[3 + i].wait_recv()
        yield off_core(p, p.far)

    def finish(self):
        for copy in self.chip + self.side:
            copy.wait_send()


class Fold:
    def __init__(self, p, both, got, near, sent, piece, half, add, sems):
        self.p, self.both, self.got, self.near, self.sent = p, both, got, near, sent
        self.kept = both.at[p.core]
        self.piece, self.half, self.add = piece, half, add
        self.chip_send, self.chip_recv, self.side_send, self.side_recv = sems
        self.chip, self.side = [], []
        if p.square:
            self.order = [p.far] + p.near + [p.chip]
        else:
            self.order = [lax.rem(p.chip + m, p.chips) for m in range(1, p.chips)] + [p.chip]

    def across(self, source, target, chip):
        i = len(self.chip)
        self.chip.append(
            send(source, target, self.chip_send.at[i], self.chip_recv.at[i], ctx=on_core(self.p, chip))
        )

    def start(self, i):
        p = self.p
        chip = self.order[i]
        self.side.append(
            send(
                self.piece(self.both.at[1 - p.core], chip),
                self.piece(self.got, chip),
                self.side_send.at[i],
                self.side_recv.at[i],
                ctx=p.beside,
            )
        )

    def between(self, i):
        p = self.p
        chip = self.order[i]
        self.side[i].wait_recv()
        self.add(self.piece(self.kept, chip), self.piece(self.got, chip))
        if i == p.chips - 1:
            return
        if not p.square:
            self.across(self.piece(self.kept, chip), self.sent.at[i], chip)
        elif i == 0:
            for j in range(2):
                self.across(self.half(self.kept, chip, j), self.near.at[j], p.near[j])
        else:
            j = i - 1
            self.across(self.half(self.kept, chip, j), self.half(self.sent.at[j], None, j), chip)

    def onward(self):
        p = self.p
        if not p.square:
            return
        for i in range(2):
            self.chip[i].wait_recv()
            part = self.half(self.kept, p.near[1 - i], i)
            self.add(part, self.near.at[i])
            self.across(part, self.half(self.sent.at[1 - i], None, i), p.near[1 - i])

    def total(self):
        p = self.p
        for copy in self.chip[2:] if p.square else self.chip:
            copy.wait_recv()
        mine = self.piece(self.kept, p.chip)
        for i in range(2 if p.square else p.chips - 1):
            self.add(mine, self.sent.at[i])
        return mine

    def finish(self):
        for copy in self.side + self.chip:
            copy.wait_send()


def add_rows(into, other, step):
    def one(i, carried):
        place = pl.ds(pl.multiple_of(i * step, step), step)
        into[place, :] = (into[place, :].astype(F32) + other[place, :].astype(F32)).astype(BF)
        return carried

    lax.fori_loop(0, into.shape[0] // step, one, 0)


def add_blocks(into, other):
    lead = into.shape[:-2]

    def one(i, carried):
        at = (i,) if len(lead) == 1 else (i // lead[1], i % lead[1])
        into[at] = (into[at].astype(F32) + other[at].astype(F32)).astype(BF)
        return carried

    lax.fori_loop(0, math.prod(lead), one, 0)


class Scatter:
    def __init__(self, p, part_of, refs):
        self.p, self.part_of, self.refs = p, part_of, refs

    def start(self):
        p = self.p
        side_out, side_in, chip_out, chip_in, side_send, side_recv, chip_send, chip_recv = self.refs
        self.side, self.out = [], []
        order = list(range(1, p.chips)) + [0]
        for m in order:
            side_out[m] = self.part_of(lax.div(p.ahead[m], 2) * 2 + 1 - p.core).astype(BF)
            self.side.append(
                send(side_out.at[m], side_in.at[m], side_send.at[m], side_recv.at[m], ctx=p.beside)
            )
        for i, m in enumerate(order):
            mine = self.part_of(p.ahead[m])
            self.side[i].wait_recv()
            self.kept = mine + side_in[m].astype(F32)
            if m > 0:
                chip_out[m - 1] = self.kept.astype(BF)
                self.out.append(
                    send(
                        chip_out.at[m - 1],
                        chip_in.at[m - 1],
                        chip_send.at[m - 1],
                        chip_recv.at[m - 1],
                        ctx=p.ahead[m],
                    )
                )

    def total(self):
        chip_in = self.refs[3]
        total = self.kept
        for m in range(1, self.p.chips):
            self.out[m - 1].wait_recv()
            total = total + chip_in[m - 1].astype(F32)
        return total

    def finish(self):
        for copy in self.side + self.out:
            copy.wait_send()


def scatter_scratch(ctx_size, rows, width):
    chips = ctx_size // 2
    return [
        pltpu.VMEM((chips, rows, width), BF),
        pltpu.VMEM((chips, rows, width), BF),
        pltpu.VMEM((chips - 1, rows, width), BF),
        pltpu.VMEM((chips - 1, rows, width), BF),
    ] + [pltpu.SemaphoreType.DMA((chips,))] * 4


def norm_back(x, scale, gain, d_scaled, d_other):
    normed = x * scale
    scaled = d_scaled * gain
    return d_other + scale * (
        scaled - normed * jnp.mean(scaled * normed, axis=-1, keepdims=True)
    )


def gather_kernel(
    ctx_size,
    wa_size,
    cuts,
    own_columns,
    x_ref,
    w_ref,
    gu_ref,
    dealt_column_ref,
    length_ref,
    freq_ref,
    xs_ref,
    ws_ref,
    cut_ref,
    dealt_tables_ref,
    given_tables_ref,
    *scratch,
):
    p = place_of(ctx_size, wa_size)
    ring_send, ring_recv, local, piece_ref = scratch[4:]
    greet([p.beside] + p.ahead[1:], [p.up[1], p.down[1]])
    rows = w_ref.shape[0] // cuts
    half_rows = x_ref.shape[0] // 2
    ring = []
    for i in range(cuts):
        part = pl.ds(i * rows, rows)
        ring.append(
            send(
                w_ref.at[part],
                ws_ref.at[p.wa, part],
                ring_send.at[0, i],
                ring_recv.at[0, i],
                wa=p.up[1],
            )
        )
    spread = Spread(
        p,
        x_ref,
        lambda d: xs_ref.at[d],
        lambda d, h: xs_ref.at[d, pl.ds(h * half_rows, half_rows)],
        scratch[:4],
    )
    spread.start()
    piece_rows = piece_ref.shape[0]
    place = pl.ds(pl.multiple_of(p.ctx * piece_rows, piece_rows), piece_rows)
    loads = [
        pltpu.make_async_copy(x_ref, xs_ref.at[p.ctx], local.at[0]),
        pltpu.make_async_copy(w_ref, ws_ref.at[p.wa], local.at[1]),
        pltpu.make_async_copy(gu_ref.at[place], piece_ref, local.at[2]),
    ]
    for copy in loads:
        copy.start()
    loads[2].wait()
    total = piece_ref.shape[1] // 2
    hidden = cut_ref.shape[3]
    for to in range(wa_size):
        for part in range(2):
            first = part * total + to * own_columns
            cut_ref[to, part, :, :own_columns] = piece_ref[:, first : first + own_columns]
            if hidden > own_columns:
                cut_ref[to, part, :, own_columns:] = jnp.zeros(
                    (piece_rows, hidden - own_columns), BF
                )
    group_rows = given_tables_ref.shape[1]
    table_rows = min(group_rows, 256)
    first_length = length_ref[:, 0:1]
    lane = lax.broadcasted_iota(jnp.int32, (table_rows, HEAD), 1)
    sign = jnp.where(lane < HEAD // 2, -1.0, 1.0)

    def tables(i, carried):
        place = pl.ds(pl.multiple_of(i * table_rows, table_rows), table_rows)
        given = lax.broadcasted_iota(jnp.int32, (table_rows, 1), 0) + i * table_rows
        for target, row in (
            (dealt_tables_ref, dealt_column_ref[place, :]),
            (given_tables_ref, given),
        ):
            position = row - jnp.where(row >= first_length, first_length, 0)
            angle = position.astype(F32) * freq_ref[...]
            target[0, place, :] = jnp.cos(angle)
            target[1, place, :] = jnp.sin(angle) * sign
        return carried

    late = []
    for step in range(1, wa_size):
        for i in range(cuts):
            ring[i].wait_recv()
            late.append(ring[i])
            if step < wa_size - 1:
                block = ws_ref.at[p.down[step], pl.ds(i * rows, rows)]
                ring[i] = send(
                    block, block, ring_send.at[step, i], ring_recv.at[step, i], wa=p.up[1]
                )
        if step == 1:
            for _ in spread.arrivals():
                pass
        if step == 2 or wa_size == 2:
            lax.fori_loop(0, group_rows // table_rows, tables, 0)
    for copy in late:
        copy.wait_send()
    spread.finish()
    for copy in loads[:2]:
        copy.wait()


def gather_both(x, w, gu, dealt_column, length, own_columns, ctx_size, wa_size, cuts=4):
    anywhere = pl.BlockSpec(memory_space=pl.ANY)
    piece_rows = w.shape[0] // ctx_size
    hidden = -(-own_columns // 128) * 128
    half = np.arange(HEAD) % (HEAD // 2)
    freq = (10000.0 ** (-2.0 * half / HEAD)).astype(np.float32)[None, :]
    vmem = pl.BlockSpec(memory_space=pltpu.VMEM)
    return pl.pallas_call(
        functools.partial(gather_kernel, ctx_size, wa_size, cuts, own_columns),
        out_shape=(
            jax.ShapeDtypeStruct((ctx_size,) + x.shape, x.dtype),
            jax.ShapeDtypeStruct((wa_size,) + w.shape, w.dtype),
            jax.ShapeDtypeStruct((wa_size, 2, piece_rows, hidden), BF),
            jax.ShapeDtypeStruct((2, dealt_column.shape[0], HEAD), F32),
            jax.ShapeDtypeStruct((2, dealt_column.shape[0], HEAD), F32),
        ),
        in_specs=[anywhere] * 3 + [vmem] * 3,
        out_specs=[anywhere] * 2 + [vmem] * 3,
        scratch_shapes=plane_sems(ctx_size)
        + [pltpu.SemaphoreType.DMA((wa_size - 1, cuts))] * 2
        + [pltpu.SemaphoreType.DMA((3,)), pltpu.VMEM((piece_rows, gu.shape[1]), BF)],
        compiler_params=pltpu.CompilerParams(
            collective_id=0, has_side_effects=True, vmem_limit_bytes=VMEM_LIMIT
        ),
        cost_estimate=pl.CostEstimate(flops=0, bytes_accessed=200_000_000, transcendentals=0),
        name="gather_both",
    )(x, w, gu, dealt_column, length, jnp.asarray(freq))


def exchange_plane(peers, source, target, send_sem, recv_sem):
    here = target(peers[0])
    return [
        send(source(peer), here, send_sem.at[i], recv_sem.at[i], ctx=peer)
        for i, peer in enumerate(peers)
        if i > 0
    ]


def attend_kernel(
    ctx_size,
    wa_size,
    heads,
    length_ref,
    x_ref,
    w_ref,
    gain_ref,
    dealt_row_ref,
    tables_ref,
    gu_ref,
    act_t_ref,
    own_ref,
    q_ref,
    k_ref,
    v_ref,
    o_ref,
    prob_ref,
    gw_ref,
    rows_ref,
    gu_send,
    gu_recv,
    local,
    out_send,
    out_recv,
    dealt_ref,
):
    wa, ctx = lax.axis_index("wa"), lax.axis_index("ctx")
    up = [lax.rem(wa + s, wa_size) for s in range(wa_size)]
    peers = [lax.rem(ctx + i, ctx_size) for i in range(ctx_size)]
    greet(peers[1:], up[1:])
    head_cols = heads * HEAD

    def columns_of(d):
        rows = pl.ds(pl.multiple_of(d * head_cols, head_cols), head_cols)
        return w_ref.at[rows, pl.ds(3 * head_cols, head_cols)]

    def rows_of(d):
        return rows_ref.at[:, pl.ds(pl.multiple_of(d * head_cols, head_cols), head_cols)]

    deal_out = exchange_plane(peers, columns_of, rows_of, out_send, out_recv)
    own_out = pltpu.make_async_copy(columns_of(ctx), rows_of(ctx), local.at[1])
    own_out.start()
    deal = [
        send(gu_ref.at[up[s]], gw_ref.at[:, wa], gu_send.at[s], gu_recv.at[s], wa=up[s])
        for s in range(1, wa_size)
    ]
    own = pltpu.make_async_copy(gu_ref.at[wa], gw_ref.at[:, wa], local.at[0])
    own.start()
    rows = x_ref.shape[0]
    step = ATTEND_ROWS

    def project(i, carried):
        place = pl.ds(pl.multiple_of(i * step, step), step)
        x = x_ref[place, :].astype(F32)
        scale = lax.rsqrt(jnp.mean(x * x, axis=-1, keepdims=True) + EPSILON)
        act = (x * scale * gain_ref[...]).astype(BF)
        act_t_ref[:, place] = act.T
        made = jnp.dot(act, w_ref[:, : 3 * head_cols], preferred_element_type=F32)
        cosine, sine = tables_ref[0, place, :], tables_ref[1, place, :]
        for head in range(2 * heads):
            columns = slice(head * HEAD, (head + 1) * HEAD)
            u = made[:, columns]
            dealt_ref[place, columns] = (
                u * cosine + pltpu.roll(u, HEAD // 2, 1) * sine
            ).astype(BF)
        dealt_ref[place, 2 * head_cols :] = made[:, 2 * head_cols :].astype(BF)
        return carried

    lax.fori_loop(0, rows // step, project, 0)

    def pick(first, count):
        given_row = lax.broadcasted_iota(jnp.int32, (count, rows), 0) + first
        return jnp.where(given_row == dealt_row_ref[...], 1.0, 0.0).astype(BF)

    def put_in_order(i, carried):
        place = pl.ds(pl.multiple_of(i * step, step), step)
        given = jnp.dot(pick(i * step, step), dealt_ref[...], preferred_element_type=F32).astype(BF)
        q_ref[place, :] = given[:, :head_cols]
        k_ref[place, :] = given[:, head_cols : 2 * head_cols]
        v_ref[place, :] = given[:, 2 * head_cols :]
        return carried

    lax.fori_loop(0, rows // step, put_in_order, 0)
    own_rows = own_ref.shape[0]
    own_ref[...] = jnp.dot(
        pick(ctx * own_rows, own_rows), x_ref[...], preferred_element_type=F32
    ).astype(BF)
    first_length = length_ref[:, 0:1]
    for i in range(rows // step):
        here = slice(i * step, (i + 1) * step)
        keys = (i + 1) * step
        row = lax.broadcasted_iota(jnp.int32, (step, keys), 0) + i * step
        column = lax.broadcasted_iota(jnp.int32, (step, keys), 1)
        late_row = jnp.where(row >= first_length, 1, 0)
        late_column = jnp.where(column >= first_length, 1, 0)
        allowed = (column <= row) & (late_row == late_column)
        if rows > WINDOW:
            allowed = allowed & (row - column < WINDOW)

        def one_head(head, carried):
            columns = pl.ds(pl.multiple_of(head * HEAD, HEAD), HEAD)
            scores = lax.dot_general(
                q_ref[here, columns],
                k_ref[:keys, columns],
                (((1,), (1,)), ((), ())),
                preferred_element_type=F32,
            )
            scores = jnp.where(allowed, scores * (1.0 / math.sqrt(HEAD)), -1e30)
            largest = jnp.max(scores, axis=-1, keepdims=True)
            weights = jnp.exp(scores - largest)
            total = jnp.sum(weights, axis=-1, keepdims=True)
            probs = (weights * (1.0 / total)).astype(BF)
            prob_rows = pl.ds(pl.multiple_of(head * rows + i * step, step), step)
            prob_ref[prob_rows, :keys] = probs
            o_ref[here, columns] = jnp.dot(
                probs, v_ref[:keys, columns], preferred_element_type=F32
            ).astype(BF)
            return carried

        lax.fori_loop(0, heads, one_head, 0)
    own.wait()
    own_out.wait()
    for copy in deal + deal_out:
        copy.wait()


def attend(length, x, w, gain, dealt_rows, tables, gu, ctx_size, wa_size):
    rows, width = x.shape
    head_cols = w.shape[1] // 4
    heads = head_cols // HEAD
    vmem = pl.BlockSpec(memory_space=pltpu.VMEM)
    anywhere = pl.BlockSpec(memory_space=pl.ANY)
    heads_shape = jax.ShapeDtypeStruct((rows, head_cols), BF)
    return pl.pallas_call(
        functools.partial(attend_kernel, ctx_size, wa_size, heads),
        out_shape=(
            jax.ShapeDtypeStruct((width, rows), BF),
            jax.ShapeDtypeStruct((rows // ctx_size, width), BF),
            heads_shape,
            heads_shape,
            heads_shape,
            heads_shape,
            jax.ShapeDtypeStruct((heads * rows, rows), BF),
            jax.ShapeDtypeStruct((2, wa_size) + gu.shape[2:], BF),
            jax.ShapeDtypeStruct((head_cols, width), BF),
        ),
        in_specs=[vmem] * 6 + [anywhere],
        out_specs=[vmem] * 7 + [anywhere] * 2,
        scratch_shapes=[pltpu.SemaphoreType.DMA((wa_size,))] * 3
        + [pltpu.SemaphoreType.DMA((ctx_size,))] * 2
        + [pltpu.VMEM((rows, 3 * head_cols), BF)],
        compiler_params=pltpu.CompilerParams(
            collective_id=4, has_side_effects=True, vmem_limit_bytes=VMEM_LIMIT
        ),
        cost_estimate=pl.CostEstimate(
            flops=2 * rows * width * 3 * head_cols, bytes_accessed=100_000_000, transcendentals=0
        ),
        name="attend",
    )(length, x, w, gain, dealt_rows[None, :], tables, gu)


def out_kernel(
    ctx_size,
    wa_size,
    mixed_ref,
    w_ref,
    x_ref,
    gain_ref,
    dz_ref,
    gu_ref,
    hidden_ref,
    acts_ref,
    dzs_ref,
    gw_ref,
    *scratch,
):
    p = place_of(ctx_size, wa_size)
    act_send, act_recv, dz_send, dz_recv, local = scratch[12:]
    greet([p.beside] + p.ahead[1:], [p.up[1], p.down[1]])
    own = pltpu.make_async_copy(gu_ref, gw_ref.at[:, :, p.ctx], local.at[0])
    own.start()
    spread = Spread(
        p,
        gu_ref,
        lambda d: gw_ref.at[:, :, d],
        lambda d, h: gw_ref.at[h, :, d],
        scratch[8:12],
    )
    rows = x_ref.shape[0]

    def part_of(device):
        block = mixed_ref[pl.ds(pl.multiple_of(device * rows, rows), rows), :]
        return jnp.dot(block, w_ref[...], preferred_element_type=F32)

    half_rows = rows // 2

    def pass_on(slots, sems, s, i):
        place = pl.ds(i * half_rows, half_rows)
        return send(
            slots.at[s, place],
            slots.at[s + 1, place],
            sems[0].at[s, i],
            sems[1].at[s, i],
            wa=p.up[1],
        )

    def ring_step(ring, slots, sems, s):
        for i in range(2):
            ring[2 * (s - 1) + i].wait_recv()
            if s < wa_size - 1:
                ring.append(pass_on(slots, sems, s, i))

    dz_sems, act_sems = (dz_send, dz_recv), (act_send, act_recv)
    dzs_ref[0] = dz_ref[...]
    dz_ring = [pass_on(dzs_ref, dz_sems, 0, i) for i in range(2)]
    scatter = Scatter(p, part_of, scratch[:8])
    scatter.start()
    ring_step(dz_ring, dzs_ref, dz_sems, 1)
    hidden = x_ref[...].astype(F32) + scatter.total()
    spread.start()
    hidden_ref[...] = hidden
    scale = lax.rsqrt(jnp.mean(hidden * hidden, axis=-1, keepdims=True) + EPSILON)
    acts_ref[0] = (hidden * scale * gain_ref[...]).astype(BF)
    ring = [pass_on(acts_ref, act_sems, 0, i) for i in range(2)]
    for s in range(2, wa_size):
        ring_step(dz_ring, dzs_ref, dz_sems, s)
    arrivals = spread.arrivals()
    for s in range(1, wa_size):
        ring_step(ring, acts_ref, act_sems, s)
        if s == 2:
            next(arrivals)
            next(arrivals)
    for _ in arrivals:
        pass
    scatter.finish()
    spread.finish()
    own.wait()
    for copy in ring + dz_ring:
        copy.wait_send()


def out_project(mixed, w_rows, x_own, gain, dz, gu, ctx_size, wa_size):
    rows, width = x_own.shape
    vmem = pl.BlockSpec(memory_space=pltpu.VMEM)
    anywhere = pl.BlockSpec(memory_space=pl.ANY)
    return pl.pallas_call(
        functools.partial(out_kernel, ctx_size, wa_size),
        out_shape=(
            jax.ShapeDtypeStruct((rows, width), F32),
            jax.ShapeDtypeStruct((wa_size, rows, width), BF),
            jax.ShapeDtypeStruct((wa_size, rows, width), BF),
            jax.ShapeDtypeStruct((2, wa_size, ctx_size) + gu.shape[2:], BF),
        ),
        in_specs=[vmem] * 5 + [anywhere],
        out_specs=[vmem] * 3 + [anywhere],
        scratch_shapes=scatter_scratch(ctx_size, rows, width)
        + plane_sems(ctx_size)
        + [pltpu.SemaphoreType.DMA((wa_size, 2))] * 4
        + [pltpu.SemaphoreType.DMA((1,))],
        compiler_params=pltpu.CompilerParams(
            collective_id=1, has_side_effects=True, vmem_limit_bytes=VMEM_LIMIT
        ),
        cost_estimate=pl.CostEstimate(
            flops=2 * mixed.size * width, bytes_accessed=200_000_000, transcendentals=0
        ),
        name="out_project",
    )(mixed, w_rows, x_own, gain, dz, gu)


def mlp_kernel(
    act_ref,
    dz_ref,
    gw_any,
    wd_any,
    d_act_ref,
    mlp_ref,
    act_t_any,
    d_gu_any,
    inner_t_any,
    gw_ref,
    wd_ref,
    inner_ref,
    act_t_ref,
    d_gu_ref,
    inner_t_ref,
    sems,
):
    hidden_rows = wd_any.shape[0]
    hidden = inner_ref.shape[1]
    width = act_ref.shape[1]
    whole = hidden // CHUNK
    ahead = min(2, whole) * CHUNK
    loads = [
        pltpu.make_async_copy(gw_any.at[:, :, :ahead], gw_ref.at[:, :, :ahead], sems.at[4]),
        pltpu.make_async_copy(wd_any, wd_ref.at[pl.ds(0, hidden_rows)], sems.at[0]),
    ]
    if hidden > ahead:
        loads.append(
            pltpu.make_async_copy(gw_any.at[:, :, ahead:], gw_ref.at[:, :, ahead:], sems.at[5])
        )
    for copy in loads:
        copy.start()
    if hidden > hidden_rows:
        wd_ref[hidden_rows:, :] = jnp.zeros((hidden - hidden_rows, width), BF)
    act_t_ref[...] = act_ref[...].T
    act_t_store = pltpu.make_async_copy(act_t_ref, act_t_any, sems.at[1])
    act_t_store.start()
    for copy in loads[:2]:
        copy.wait()
    act = act_ref[...]
    dz = dz_ref[...]

    def part(first, size):
        columns = pl.ds(first, size)
        gate = jnp.dot(act, gw_ref[0, :, columns], preferred_element_type=F32)
        up = jnp.dot(act, gw_ref[1, :, columns], preferred_element_type=F32)
        d_inner = lax.dot_general(
            dz, wd_ref[columns, :], (((1,), (1,)), ((), ())), preferred_element_type=F32
        )
        sigmoid = 1.0 / (1.0 + jnp.exp(-gate))
        silu = gate * sigmoid
        inner = (silu * up).astype(BF)
        inner_ref[:, columns] = inner
        d_gate = (d_inner * up * sigmoid * (1.0 + gate * (1.0 - sigmoid))).astype(BF)
        d_up = (d_inner * silu).astype(BF)
        d_gu_ref[0, :, columns] = d_gate
        d_gu_ref[1, :, columns] = d_up
        inner_t_ref[columns, :] = inner.T

    def one(i, carried):
        part(pl.multiple_of(i * CHUNK, CHUNK), CHUNK)
        return carried

    lax.fori_loop(0, ahead // CHUNK, one, 0)
    for copy in loads[2:]:
        copy.wait()
    lax.fori_loop(ahead // CHUNK, whole, one, 0)
    if hidden > whole * CHUNK:
        part(whole * CHUNK, hidden - whole * CHUNK)
    stores = [
        pltpu.make_async_copy(d_gu_ref, d_gu_any, sems.at[2]),
        pltpu.make_async_copy(inner_t_ref, inner_t_any, sems.at[3]),
    ]
    for copy in stores:
        copy.start()

    def two(i, carried):
        place = pl.ds(pl.multiple_of(i * CHUNK, CHUNK), CHUNK)
        back = lax.dot_general(
            d_gu_ref[0], gw_ref[0, place, :], (((1,), (1,)), ((), ())), preferred_element_type=F32
        )
        back = back + lax.dot_general(
            d_gu_ref[1], gw_ref[1, place, :], (((1,), (1,)), ((), ())), preferred_element_type=F32
        )
        d_act_ref[:, place] = back.astype(BF)
        mlp_ref[:, place] = jnp.dot(
            inner_ref[...], wd_ref[:, place], preferred_element_type=F32
        ).astype(BF)
        return carried

    lax.fori_loop(0, width // CHUNK, two, 0)
    for copy in stores + [act_t_store]:
        copy.wait()


def mlp(act, dz, gw, wd):
    tokens, width = act.shape
    hidden = gw.shape[2]
    vmem = pl.BlockSpec(memory_space=pltpu.VMEM)
    anywhere = pl.BlockSpec(memory_space=pl.ANY)
    return pl.pallas_call(
        mlp_kernel,
        out_shape=(
            jax.ShapeDtypeStruct((tokens, width), BF),
            jax.ShapeDtypeStruct((tokens, width), BF),
            jax.ShapeDtypeStruct((width, tokens), BF),
            jax.ShapeDtypeStruct((2, tokens, hidden), BF),
            jax.ShapeDtypeStruct((hidden, tokens), BF),
        ),
        in_specs=[vmem, vmem, anywhere, anywhere],
        out_specs=[vmem] * 2 + [anywhere] * 3,
        scratch_shapes=[
            pltpu.VMEM(gw.shape, BF),
            pltpu.VMEM((hidden, width), BF),
            pltpu.VMEM((tokens, hidden), BF),
            pltpu.VMEM((width, tokens), BF),
            pltpu.VMEM((2, tokens, hidden), BF),
            pltpu.VMEM((hidden, tokens), BF),
            pltpu.SemaphoreType.DMA((6,)),
        ],
        compiler_params=pltpu.CompilerParams(vmem_limit_bytes=60 * 1024 * 1024),
        cost_estimate=pl.CostEstimate(
            flops=12 * tokens * width * hidden, bytes_accessed=50_000_000, transcendentals=0
        ),
        name="mlp",
    )(act, dz, gw, wd)


def turn_kernel(
    ctx_size,
    wa_size,
    parts_ref,
    mlp_ref,
    hidden_ref,
    gain_ref,
    dz_ref,
    act_t_ref,
    d_gu_ref,
    inner_t_ref,
    dz_all_ref,
    all_ref,
    gain_out_ref,
    out_ref,
    gu_out_ref,
    down_out_ref,
    *scratch,
):
    p = place_of(ctx_size, wa_size)
    got_ref, more_ref, wa_send, wa_recv, more_send, more_recv = scratch[:6]
    gu_both, gu_got, gu_near, gu_sent, down_both, down_got, down_near, down_sent = scratch[6:14]
    gu_sems, down_sems, spread_sems = scratch[14:18], scratch[18:22], scratch[22:26]
    own_parts, own_mlp, local = scratch[26:29]
    greet([p.beside] + p.ahead[1:], p.down[1:])
    copies = [
        send(parts_ref.at[s], got_ref.at[s], wa_send.at[s], wa_recv.at[s], wa=p.down[s])
        for s in range(1, wa_size)
    ]
    loads = [
        pltpu.make_async_copy(parts_ref.at[0], own_parts, local.at[0]),
        pltpu.make_async_copy(mlp_ref.at[0], own_mlp, local.at[1]),
    ]
    for copy in loads:
        copy.start()
    down_total = down_both.shape[1]
    down_rows = down_total // 2
    columns = dz_all_ref.shape[1] // ctx_size
    half = gu_both.shape[1] // 2
    piece_rows = gu_both.shape[3]
    wa_rows = act_t_ref.shape[0] // wa_size

    def down_piece(ref, chip):
        return ref.at[:, pl.ds(pl.multiple_of(chip * columns, columns), columns)]

    def down_half(ref, chip, h):
        place = pl.ds(h * down_rows, down_rows)
        if chip is None:
            return ref.at[place]
        return ref.at[place, pl.ds(pl.multiple_of(chip * columns, columns), columns)]

    down = Fold(
        p,
        down_both,
        down_got,
        down_near,
        down_sent,
        down_piece,
        down_half,
        lambda into, other: add_rows(into, other, 16),
        down_sems,
    )

    def gu_half(ref, chip, h):
        place = pl.ds(h * half, half)
        return ref.at[place] if chip is None else ref.at[place, chip]

    gu = Fold(
        p,
        gu_both,
        gu_got,
        gu_near,
        gu_sent,
        lambda ref, chip: ref.at[:, chip],
        gu_half,
        add_blocks,
        gu_sems,
    )

    def make(chip):
        first = chip * (2 * piece_rows)
        left = jnp.concatenate(
            [
                act_t_ref[pl.ds(pl.multiple_of(i * wa_rows + first, 2 * piece_rows), 2 * piece_rows), :]
                for i in range(wa_size)
            ],
            axis=0,
        )

        def gu_part(part, carried):
            made = jnp.dot(left, d_gu_ref[part], preferred_element_type=F32).astype(BF)
            for i in range(wa_size):
                for core in range(2):
                    at = (2 * i + core) * piece_rows
                    gu_both[core, part * wa_size + i, chip] = made[at : at + piece_rows]
            return carried

        lax.fori_loop(0, 2, gu_part, 0)

        def down_part(core, carried):
            place = pl.multiple_of((core * p.chips + chip) * columns, columns)
            made = jnp.dot(
                inner_t_ref[...], dz_all_ref[:, pl.ds(place, columns)], preferred_element_type=F32
            ).astype(BF)
            target = pl.ds(pl.multiple_of(chip * columns, columns), columns)
            down_both[core, :, target] = made[:down_total]
            return carried

        lax.fori_loop(0, 2, down_part, 0)

    for i in range(p.chips):
        make(gu.order[i])
        gu.start(i)
        down.start(i)
        if i > 0:
            gu.between(i - 1)
            down.between(i - 1)
    gu.between(p.chips - 1)
    down.between(p.chips - 1)
    hidden = hidden_ref[...]
    scale = lax.rsqrt(jnp.mean(hidden * hidden, axis=-1, keepdims=True) + EPSILON)
    down.onward()
    for copy in loads:
        copy.wait()
    d_normed = own_parts[...].astype(F32)
    for s in range(1, wa_size):
        copies[s - 1].wait_recv()
        d_normed = d_normed + got_ref[s].astype(F32)
    more = [
        send(mlp_ref.at[s], more_ref.at[s], more_send.at[s], more_recv.at[s], wa=p.down[s])
        for s in range(1, wa_size)
    ]
    gain_out_ref[...] = jnp.sum(d_normed * (hidden * scale), axis=0, keepdims=True)
    d_hidden = norm_back(hidden, scale, gain_ref[...], d_normed, dz_ref[...].astype(F32))
    all_ref[p.ctx] = d_hidden.astype(BF)
    half_rows = all_ref.shape[1] // 2
    spread = Spread(
        p,
        all_ref.at[p.ctx],
        lambda d: all_ref.at[d],
        lambda d, h: all_ref.at[d, pl.ds(h * half_rows, half_rows)],
        spread_sems,
    )
    spread.start()
    gu.onward()
    down_out_ref[...] = down.total()[...]
    for _ in spread.arrivals():
        pass
    gu_out_ref[...] = gu.total()[...]
    result = hidden + own_mlp[...].astype(F32)
    for s in range(1, wa_size):
        more[s - 1].wait_recv()
        result = result + more_ref[s].astype(F32)
    out_ref[...] = result.astype(BF)
    for copy in copies + more:
        copy.wait_send()
    down.finish()
    gu.finish()
    spread.finish()


def turn(
    parts, mlp, hidden, gain, dz, act_t, d_gu, inner_t, dz_all, hidden_rows, ctx_size, wa_size
):
    rows, width = hidden.shape
    chips = ctx_size // 2
    columns = width // ctx_size
    lead = 2 * wa_size
    gu_rows, gu_columns = width // (ctx_size * wa_size), d_gu.shape[2]
    vmem = pl.BlockSpec(memory_space=pltpu.VMEM)
    anywhere = pl.BlockSpec(memory_space=pl.ANY)
    many = 2 if chips == 4 else chips - 1
    return pl.pallas_call(
        functools.partial(turn_kernel, ctx_size, wa_size),
        out_shape=(
            jax.ShapeDtypeStruct((ctx_size, rows, width), BF),
            jax.ShapeDtypeStruct((1, width), F32),
            jax.ShapeDtypeStruct((rows, width), BF),
            jax.ShapeDtypeStruct((lead, gu_rows, gu_columns), BF),
            jax.ShapeDtypeStruct((hidden_rows, columns), BF),
        ),
        in_specs=[anywhere] * 2 + [vmem] * 7,
        out_specs=[vmem] * 5,
        scratch_shapes=[pltpu.VMEM((wa_size, rows, width), BF)] * 2
        + [pltpu.SemaphoreType.DMA((wa_size,))] * 4
        + [
            pltpu.VMEM((2, lead, chips, gu_rows, gu_columns), BF),
            pltpu.VMEM((lead, chips, gu_rows, gu_columns), BF),
            pltpu.VMEM((2, lead // 2, gu_rows, gu_columns), BF),
            pltpu.VMEM((many, lead, gu_rows, gu_columns), BF),
            pltpu.VMEM((2, hidden_rows, columns * chips), BF),
            pltpu.VMEM((hidden_rows, columns * chips), BF),
            pltpu.VMEM((2, hidden_rows // 2, columns), BF),
            pltpu.VMEM((many, hidden_rows, columns), BF),
        ]
        + [pltpu.SemaphoreType.DMA((max(chips, 6),))] * 8
        + plane_sems(ctx_size)
        + [pltpu.VMEM((rows, width), BF)] * 2
        + [pltpu.SemaphoreType.DMA((2,))],
        compiler_params=pltpu.CompilerParams(
            collective_id=2, has_side_effects=True, vmem_limit_bytes=VMEM_LIMIT
        ),
        cost_estimate=pl.CostEstimate(flops=0, bytes_accessed=200_000_000, transcendentals=0),
        name="turn",
    )(parts, mlp, hidden, gain, dz, act_t, d_gu, inner_t, dz_all)


def finish_kernel(
    ctx_size,
    wa_size,
    heads,
    dy_ref,
    w_ref,
    o_ref,
    q_ref,
    k_ref,
    v_ref,
    tables_ref,
    x_ref,
    gain_ref,
    gain_two_ref,
    dealt_column_ref,
    prob_any,
    act_t_any,
    w_all_any,
    gu_ref,
    down_ref,
    out_ref,
    gus_ref,
    downs_ref,
    qkvs_ref,
    outs_ref,
    sums_ref,
    *scratch,
):
    p = place_of(ctx_size, wa_size)
    do_ref, dk_ref, dv_ref, d_out_ref, given_ref = scratch[8:13]
    late_ref, w_all_ref = scratch[13:15]
    grads_ref, dw_ref, parts_ref, gu_in_ref, gains_ref = scratch[15:20]
    rows_ref, dw_in, share_ref, do_in, out_share_ref = scratch[20:25]
    wa_gains, ctx_gains, local, load_sems = scratch[25:29]
    gu_sems, dw_sems, do_sems, wa_sems = (scratch[i : i + 2] for i in (29, 31, 33, 35))
    part_sems, ctx_sems = scratch[37:39], scratch[39:41]
    down_plane, gu_plane, qkv_plane, out_plane = (scratch[i : i + 4] for i in (41, 45, 49, 53))
    peers = [lax.rem(p.ctx + i, ctx_size) for i in range(ctx_size)]
    greet(peers[1:], p.up[1:])
    locals_ = []

    def keep(source, target):
        copy = pltpu.make_async_copy(source, target, local.at[len(locals_)])
        copy.start()
        locals_.append(copy)
        return copy

    def spread_of(own, slots, sems):
        half = slots.shape[1] // 2
        keep(own, slots.at[p.ctx])
        spread = Spread(
            p,
            own,
            lambda d: slots.at[d],
            lambda d, h: slots.at[d, pl.ds(h * half, half)],
            sems,
        )
        spread.start()
        return spread

    deal = [
        send(
            gu_ref.at[:, p.up[s]], gu_in_ref.at[p.wa], gu_sems[0].at[s], gu_sems[1].at[s], wa=p.up[s]
        )
        for s in range(1, wa_size)
    ]
    own_deal = keep(gu_ref.at[:, p.wa], gu_in_ref.at[p.wa])
    down_spread = spread_of(down_ref, downs_ref, down_plane)
    loads = [
        pltpu.make_async_copy(source, target, load_sems.at[i])
        for i, (source, target) in enumerate(
            (
                (prob_any, late_ref),
                (w_all_any, w_all_ref),
                (act_t_any, late_ref),
            )
        )
    ]
    for copy in loads[:2]:
        copy.start()
    rows = dy_ref.shape[0]
    width = dy_ref.shape[1]
    step = ATTEND_ROWS
    head_cols = heads * HEAD
    qkv_cols = 3 * head_cols
    back_scale = 1.0 / math.sqrt(HEAD)
    d_out_ref[...] = lax.dot_general(
        o_ref[...], dy_ref[...], (((0,), (0,)), ((), ())), preferred_element_type=F32
    ).astype(BF)

    def d_out_part(device):
        place = pl.ds(pl.multiple_of(device * head_cols, head_cols), head_cols)
        return d_out_ref.at[:, place]

    part_copies = exchange_plane(
        peers, d_out_part, lambda d: parts_ref.at[d], part_sems[0], part_sems[1]
    )
    own_part = keep(d_out_part(p.ctx), parts_ref.at[p.ctx])

    def project(i, carried):
        place = pl.ds(pl.multiple_of(i * step, step), step)
        do_ref[place, :] = lax.dot_general(
            dy_ref[place, :],
            w_ref[...],
            (((1,), (1,)), ((), ())),
            preferred_element_type=F32,
        ).astype(BF)
        return carried

    lax.fori_loop(0, rows // step, project, 0)
    loads[0].wait()
    dk_ref[...] = jnp.zeros_like(dk_ref)
    dv_ref[...] = jnp.zeros_like(dv_ref)

    def unrotate(u, place):
        cosine, sine = tables_ref[0, place, :], tables_ref[1, place, :]
        return u * cosine - pltpu.roll(u, HEAD // 2, 1) * sine

    for i in range(rows // step):
        here = slice(i * step, (i + 1) * step)
        keys = (i + 1) * step

        def back(head, carried):
            columns = pl.ds(pl.multiple_of(head * HEAD, HEAD), HEAD)
            d_o = do_ref[here, columns]
            q = q_ref[here, columns]
            prob_rows = pl.ds(pl.multiple_of(head * rows + i * step, step), step)
            probs = late_ref[prob_rows, :keys]
            d_probs = lax.dot_general(
                d_o,
                v_ref[:keys, columns],
                (((1,), (1,)), ((), ())),
                preferred_element_type=F32,
            )
            wide = probs.astype(F32)
            row_dot = jnp.sum(wide * d_probs, axis=-1, keepdims=True)
            d_scores = (wide * (d_probs - row_dot)).astype(BF)
            d_query = jnp.dot(d_scores, k_ref[:keys, columns], preferred_element_type=F32)
            given_ref[here, columns] = unrotate(d_query * back_scale, here).astype(BF)
            dk_ref[:keys, columns] += lax.dot_general(
                d_scores, q, (((0,), (0,)), ((), ())), preferred_element_type=F32
            )
            dv_ref[:keys, columns] += lax.dot_general(
                probs, d_o, (((0,), (0,)), ((), ())), preferred_element_type=F32
            )
            return carried

        lax.fori_loop(0, heads, back, 0)
    loads[2].start()
    for head in range(heads):
        columns = slice(head * HEAD, (head + 1) * HEAD)
        d_key = unrotate(dk_ref[:, columns] * back_scale, slice(0, rows))
        given_ref[:, head_cols + head * HEAD : head_cols + (head + 1) * HEAD] = d_key.astype(BF)
    given_ref[:, 2 * head_cols :] = dv_ref[...].astype(BF)
    down_arrivals = down_spread.arrivals()
    next(down_arrivals)
    next(down_arrivals)
    loads[1].wait()

    def unpick(place, count):
        given_row = lax.broadcasted_iota(jnp.int32, (count, rows), 1)
        return jnp.where(given_row == dealt_column_ref[place, :], 1.0, 0.0).astype(BF)

    def put_back(i, carried):
        place = pl.ds(pl.multiple_of(i * step, step), step)
        grads_ref[place, :] = jnp.dot(
            unpick(place, step), given_ref[...], preferred_element_type=F32
        ).astype(BF)
        return carried

    lax.fori_loop(0, rows // step, put_back, 0)
    own_rows = x_ref.shape[0]

    def part_of(device):
        place = pl.ds(pl.multiple_of(device * own_rows, own_rows), own_rows)
        return lax.dot_general(
            grads_ref[place, :],
            w_all_ref[:, :qkv_cols],
            (((1,), (1,)), ((), ())),
            preferred_element_type=F32,
        )

    loads[2].wait()
    wa_rows = dw_ref.shape[1]

    def weights(i, carried):
        place = pl.ds(pl.multiple_of(i * wa_rows, wa_rows), wa_rows)
        made = jnp.dot(late_ref[place, :], grads_ref[...], preferred_element_type=F32)
        dw_ref[i] = made.astype(BF)
        return carried

    lax.fori_loop(0, wa_size, weights, 0)
    dw_copies = [
        send(
            dw_ref.at[p.up[s]], dw_in.at[s - 1], dw_sems[0].at[s], dw_sems[1].at[s], wa=p.up[s]
        )
        for s in range(1, wa_size)
    ]
    scatter = Scatter(p, part_of, scratch[:8])
    scatter.start()
    ones = jnp.ones((8, qkv_cols), BF)

    def gains(i, carried):
        place = pl.ds(pl.multiple_of(i * wa_rows, wa_rows), wa_rows)
        products = dw_ref[i].astype(F32) * w_all_ref[place, :qkv_cols].astype(F32)
        high = products.astype(BF)
        low = (products - high.astype(F32)).astype(BF)
        sums = [
            lax.dot_general(
                ones, part, (((1,), (1,)), ((), ())), preferred_element_type=F32
            )
            for part in (high, low)
        ]
        gains_ref[0:1, place] = (sums[0] + sums[1])[0:1] / gain_ref[:, place]
        return carried

    lax.fori_loop(0, wa_size, gains, 0)
    gains_ref[1:2] = gain_two_ref[...]
    wa_gains[p.wa] = gains_ref[...]
    small = [
        send(gains_ref, wa_gains.at[p.wa], wa_sems[0].at[s], wa_sems[1].at[s], wa=p.up[s])
        for s in range(1, wa_size)
    ]
    for _ in down_arrivals:
        pass
    own_deal.wait()
    for copy in deal:
        copy.wait_recv()
    total_columns = rows_ref.shape[1] // 2
    own_columns = total_columns // wa_size
    for i in range(wa_size):
        for part in range(2):
            first = part * total_columns + i * own_columns
            rows_ref[:, first : first + own_columns] = gu_in_ref[i, part, :, :own_columns]
    gu_spread = spread_of(rows_ref, gus_ref, gu_plane)
    for copy in small:
        copy.wait()
    plane_gain = wa_gains[0]
    for i in range(1, wa_size):
        plane_gain = plane_gain + wa_gains[i]
    ctx_gains[p.ctx] = plane_gain
    own_gain = ctx_gains.at[p.ctx]
    small = [
        send(own_gain, own_gain, ctx_sems[0].at[i], ctx_sems[1].at[i], ctx=peer)
        for i, peer in enumerate(peers)
        if i > 0
    ]
    dh_place = pl.ds(pl.multiple_of(p.ctx * own_rows, own_rows), own_rows)
    d_hidden = jnp.dot(unpick(dh_place, own_rows), dy_ref[...], preferred_element_type=F32)
    x = x_ref[...].astype(F32)
    scale = lax.rsqrt(jnp.mean(x * x, axis=-1, keepdims=True) + EPSILON)
    out_ref[...] = norm_back(x, scale, gain_ref[...], scatter.total(), d_hidden).astype(BF)
    gu_arrivals = gu_spread.arrivals()
    next(gu_arrivals)
    next(gu_arrivals)
    for _ in gu_arrivals:
        pass
    for copy in small:
        copy.wait()
    total_gain = ctx_gains[0]
    for i in range(1, ctx_size):
        total_gain = total_gain + ctx_gains[i]
    sums_ref[...] = total_gain
    for copy in dw_copies:
        copy.wait_recv()
    own_part.wait()
    for copy in part_copies:
        copy.wait_recv()
    per_wa = ctx_size // wa_size

    def d_out_block(device):
        return parts_ref.at[pl.ds(device * per_wa, per_wa)]

    do_copies = [
        send(
            d_out_block(p.up[s]), do_in.at[s], do_sems[0].at[s], do_sems[1].at[s], wa=p.up[s]
        )
        for s in range(1, wa_size)
    ]

    def add_up(i, carried):
        place = pl.ds(pl.multiple_of(i * 16, 16), 16)
        total = dw_ref[p.wa, place, :].astype(F32)
        for s in range(1, wa_size):
            total = total + dw_in[s - 1, place, :].astype(F32)
        share_ref[place, :] = total.astype(BF)
        return carried

    lax.fori_loop(0, wa_rows // 16, add_up, 0)
    qkv_spread = spread_of(share_ref, qkvs_ref, qkv_plane)
    for copy in do_copies:
        copy.wait_recv()
    for i in range(per_wa):
        total = parts_ref[p.wa * per_wa + i].astype(F32)
        for s in range(1, wa_size):
            total = total + do_in[s, i].astype(F32)
        out_share_ref[pl.ds(i * head_cols, head_cols), :] = total.astype(BF)
    out_spread = spread_of(out_share_ref, outs_ref, out_plane)
    for _ in qkv_spread.arrivals():
        pass
    for _ in out_spread.arrivals():
        pass
    scatter.finish()
    for spread in (down_spread, gu_spread, qkv_spread, out_spread):
        spread.finish()
    for copy in deal + dw_copies + do_copies + part_copies:
        copy.wait_send()
    for copy in locals_:
        if copy is not own_deal and copy is not own_part:
            copy.wait()


def finish(
    dy,
    w_rows,
    o,
    q,
    k,
    v,
    tables,
    x_own,
    gain,
    gain_two,
    dealt_column,
    probs,
    act_t,
    w_all,
    gu,
    down,
    columns,
    ctx_size,
    wa_size,
):
    rows, width = dy.shape
    head_cols = o.shape[1]
    heads = head_cols // HEAD
    own_rows = x_own.shape[0]
    vmem = pl.BlockSpec(memory_space=pltpu.VMEM)
    anywhere = pl.BlockSpec(memory_space=pl.ANY)
    wa_rows = width // wa_size
    gu_shape = (gu.shape[2], columns)
    share_shape = (wa_rows, 3 * head_cols)
    out_shape = (wa_rows, head_cols)
    gains = (2, width)
    return pl.pallas_call(
        functools.partial(finish_kernel, ctx_size, wa_size, heads),
        out_shape=(jax.ShapeDtypeStruct((own_rows, width), BF),)
        + tuple(
            jax.ShapeDtypeStruct((ctx_size,) + shape, BF)
            for shape in (gu_shape, down.shape, share_shape, out_shape)
        )
        + (jax.ShapeDtypeStruct(gains, F32),),
        in_specs=[vmem] * 11 + [anywhere] * 5,
        out_specs=[vmem] + [anywhere] * 4 + [vmem],
        scratch_shapes=scatter_scratch(ctx_size, own_rows, width)
        + [
            pltpu.VMEM((rows, head_cols), BF),
            pltpu.VMEM((rows, head_cols), F32),
            pltpu.VMEM((rows, head_cols), F32),
            pltpu.VMEM((head_cols, width), BF),
            pltpu.VMEM((rows, 3 * head_cols), BF),
            pltpu.VMEM(act_t.shape, BF),
            pltpu.VMEM(w_all.shape, BF),
            pltpu.VMEM((rows, 3 * head_cols), BF),
            pltpu.VMEM((wa_size,) + share_shape, BF),
            pltpu.VMEM((ctx_size, head_cols, head_cols), BF),
            pltpu.VMEM((wa_size, 2) + gu.shape[2:], BF),
            pltpu.VMEM(gains, F32),
            pltpu.VMEM(gu_shape, BF),
            pltpu.VMEM((wa_size - 1,) + share_shape, BF),
            pltpu.VMEM(share_shape, BF),
            pltpu.VMEM((wa_size, ctx_size // wa_size, head_cols, head_cols), BF),
            pltpu.VMEM(out_shape, BF),
            pltpu.VMEM((wa_size,) + gains, F32),
            pltpu.VMEM((ctx_size,) + gains, F32),
            pltpu.SemaphoreType.DMA((6,)),
            pltpu.SemaphoreType.DMA((4,)),
        ]
        + [pltpu.SemaphoreType.DMA((wa_size,))] * 8
        + [pltpu.SemaphoreType.DMA((ctx_size,))] * 4
        + plane_sems(ctx_size) * 4,
        compiler_params=pltpu.CompilerParams(
            collective_id=3, has_side_effects=True, vmem_limit_bytes=VMEM_LIMIT + 2 * 1024 * 1024
        ),
        cost_estimate=pl.CostEstimate(
            flops=12 * rows * width * head_cols, bytes_accessed=400_000_000, transcendentals=0
        ),
        name="finish",
    )(
        dy,
        w_rows,
        o,
        q,
        k,
        v,
        tables,
        x_own,
        gain,
        gain_two,
        dealt_column,
        probs,
        act_t,
        w_all,
        gu,
        down,
    )


def widen_kernel(count, head_cols, gu_ref, down_ref, qkv_ref, do_ref, *out_refs):
    gu_out, down_out, qkv_out, do_out = out_refs
    gu_out[...] = gu_ref[0].astype(F32)
    down_out[...] = down_ref[0].astype(F32)
    for device in range(count):
        for part in range(3):
            first = (part * count + device) * head_cols
            qkv_out[:, first : first + head_cols] = qkv_ref[
                device, :, part * head_cols : (part + 1) * head_cols
            ].astype(F32)
        first = device * head_cols
        do_out[:, first : first + head_cols] = do_ref[device].astype(F32)


def widen(gus, downs, qkvs, outs):
    count, gu_rows, gu_columns = gus.shape
    down_rows, down_columns = downs.shape[1:]
    rows, qkv_columns = qkvs.shape[1:]
    head_cols = outs.shape[2]
    step = rows // count
    return pl.pallas_call(
        functools.partial(widen_kernel, count, head_cols),
        out_shape=(
            jax.ShapeDtypeStruct((count * gu_rows, gu_columns), F32),
            jax.ShapeDtypeStruct((down_rows, count * down_columns), F32),
            jax.ShapeDtypeStruct((rows, count * qkv_columns), F32),
            jax.ShapeDtypeStruct((rows, count * head_cols), F32),
        ),
        grid=(count,),
        in_specs=[
            pl.BlockSpec((1, gu_rows, gu_columns), lambda i: (i, 0, 0)),
            pl.BlockSpec((1, down_rows, down_columns), lambda i: (i, 0, 0)),
            pl.BlockSpec((count, step, qkv_columns), lambda i: (0, i, 0)),
            pl.BlockSpec((count, step, head_cols), lambda i: (0, i, 0)),
        ],
        out_specs=[
            pl.BlockSpec((gu_rows, gu_columns), lambda i: (i, 0)),
            pl.BlockSpec(
                (down_rows, down_columns), lambda i: (0, (i % 2) * (count // 2) + i // 2)
            ),
            pl.BlockSpec((step, count * qkv_columns), lambda i: (i, 0)),
            pl.BlockSpec((step, count * head_cols), lambda i: (i, 0)),
        ],
        compiler_params=pltpu.CompilerParams(vmem_limit_bytes=VMEM_LIMIT),
        name="widen",
    )(gus, downs, qkvs, outs)


def per_device(
    tokens, lengths, dealing, norm1_gain, w_qkv, w_out, norm2_gain, w_gate_up, w_down, grad_out
):
    tok_rows, width = tokens.shape[1], tokens.shape[2]
    ctx_size = lax.axis_size("ctx")
    wa_size = lax.axis_size("wa")
    ctx_index = lax.axis_index("ctx")
    wa_index = lax.axis_index("wa")
    block_order = dealing[0]
    block_total = block_order.shape[0]
    group_rows = block_total * BLOCK
    own_blocks = tok_rows // BLOCK
    heads_own = HEADS // ctx_size
    head_cols = heads_own * HEAD
    wa_rows = width // wa_size
    ff_total = w_gate_up.shape[1] // 2
    ff_own = w_down.shape[0]
    piece_rows = wa_rows // ctx_size

    own_cols = jnp.concatenate(
        [
            lax.dynamic_slice_in_dim(w_qkv, part * width + ctx_index * head_cols, head_cols, 1)
            for part in range(3)
        ]
        + [lax.dynamic_slice_in_dim(w_out, ctx_index * head_cols, head_cols, 1)],
        axis=1,
    )
    in_block = jnp.arange(BLOCK, dtype=jnp.int32)
    rows_dealt = (block_order[:, None] * BLOCK + in_block[None, :]).reshape(group_rows)
    dealt_column = rows_dealt[:, None]
    dealt, all_cols, gu_send, dealt_tables, given_tables = gather_both(
        tokens[0], own_cols, w_gate_up, dealt_column, lengths, ff_own, ctx_size, wa_size
    )
    dealt = dealt.reshape(group_rows, width)
    all_cols = all_cols.reshape(width, 4 * head_cols)
    act_one_t, own_given, query_b, key_b, value_b, mixed_b, probs_b, gu_mine, out_rows = attend(
        lengths,
        dealt,
        all_cols,
        norm1_gain[None, :],
        rows_dealt,
        dealt_tables,
        gu_send,
        ctx_size,
        wa_size,
    )
    gain_two = norm2_gain[None, :]
    hidden, acts, grads_all, gu_weight = out_project(
        mixed_b, out_rows, own_given, gain_two, grad_out[0], gu_mine, ctx_size, wa_size
    )
    gu_weight = gu_weight.reshape(2, width, gu_weight.shape[4])
    act_two = acts.reshape(wa_size * tok_rows, width)
    cotangent = grads_all.reshape(wa_size * tok_rows, width)

    d_act, mlp_parts, act_t, d_gu, inner_t = mlp(act_two, cotangent, gu_weight, w_down)
    d_branches, gain_two_part, out_given, gu_piece_grad, down_piece_grad = turn(
        d_act.reshape(wa_size, tok_rows, width),
        mlp_parts.reshape(wa_size, tok_rows, width),
        hidden,
        gain_two,
        grad_out[0],
        act_t,
        d_gu,
        inner_t,
        cotangent,
        ff_own,
        ctx_size,
        wa_size,
    )
    d_branch_b = d_branches.reshape(group_rows, width)
    d_tokens, gus, downs, qkvs, outs, gain_sums = finish(
        d_branch_b,
        out_rows,
        mixed_b,
        query_b,
        key_b,
        value_b,
        given_tables,
        tokens[0],
        norm1_gain[None, :],
        gain_two_part,
        dealt_column,
        probs_b,
        act_one_t,
        all_cols,
        gu_piece_grad.reshape((2, wa_size) + gu_piece_grad.shape[1:]),
        down_piece_grad,
        2 * ff_total,
        ctx_size,
        wa_size,
    )
    d_gate_up, d_down, d_qkv, d_out = widen(gus, downs, qkvs, outs)
    return (
        out_given[None],
        d_tokens[None],
        gain_sums[0],
        d_qkv,
        d_out,
        gain_sums[1],
        d_gate_up,
        d_down,
    )


def solution(mesh):
    in_specs = (
        P("wa", "ctx", None),
        P("wa", None),
        P("wa", None),
        P(),
        P("wa", None),
        P("wa", None),
        P(),
        P("wa", None),
        P("wa", None),
        P("wa", "ctx", None),
    )
    out_specs = (
        P("wa", "ctx", None),
        P("wa", "ctx", None),
        P(),
        P("wa", None),
        P("wa", None),
        P(),
        P("wa", None),
        P("wa", None),
    )
    return jax.shard_map(
        per_device, mesh=mesh, in_specs=in_specs, out_specs=out_specs, check_vma=False
    )
```
